32 devices in a mesh: view: 4 (over x, core), patch: 8 (over z, y).
Axes of the slice: x: 2, y: 2, z: 4, core: 2. Of those that a mesh axis runs over, the one named last changes fastest.
Arguments:
- queries: bfloat16 [4096, 768], P(('view', 'patch')), may hold values from -6 to 6
- key_rows: bfloat16 [4096, 768], P(('view', 'patch')), may hold values from -6 to 6
- value_rows: bfloat16 [4096, 768], P(('view', 'patch')), may hold values from -6 to 6
- step_rates: float32 [4096, 4], P(('view', 'patch')), may hold values from 0.5 to 18, as said below
- fast_init: float32 [192, 4608], replicated, may hold values from -2.598076 to 2.598076
- out_grad: bfloat16 [4096, 768], P(('view', 'patch')), may hold values from -6 to 6
Outputs:
- query_grad: bfloat16 [4096, 768], P(('view', 'patch'))
- key_grad: bfloat16 [4096, 768], P(('view', 'patch'))
- value_grad: bfloat16 [4096, 768], P(('view', 'patch'))
- rate_grad: float32 [4096, 4], P(('view', 'patch'))
- fast_grad: float32 [192, 4608], P(None, ('view', 'patch'))
The draws below stay inside these ranges and needn't reach their ends.
Inputs may be any that keep to these rules, and one draw needn't show every extreme that they name: `step_rates`: positive learning rates.
All inputs are finite; a program needn't handle non-finite values.
Results may differ from the reference program's by a relative error of at most 0.0023.
Values sent between devices are 32-bit elements; how exact they have to be, the bound alone decides.
No kernel may reach another device: no remote copies, remote signals or barrier semaphores. Data moves between devices by JAX's collectives and lax.ppermute only.
A program may use at most 128 MiB of HBM per device.

```python
import math
import jax
import jax.numpy as jnp
from jax import lax

HEADS = 4
HEAD_DIM = 192
FF = 384
D = 768
PATCHES = 4096
N_VIEW = 4
N_PATCH = 8


def draw_step_rates(key, part):
    position_ramp = jnp.arange(PATCHES, dtype=jnp.float32)[:, None] / max(PATCHES - 1, 1)
    growth = 1.0 + 2.0 * position_ramp
    spread = jnp.exp(jax.random.uniform(key, (PATCHES, HEADS), jnp.float32, math.log(0.5), math.log(2.0)))
    return spread * growth


def draw_fast_init(key, part):
    key_one, key_two, key_three = jax.random.split(key, 3)
    columns = 3 * HEADS * FF
    row_scale = jnp.exp(jax.random.uniform(key_one, (HEAD_DIM, 1), jnp.float32, math.log(0.3), math.log(3.0)))
    col_scale = jnp.exp(jax.random.uniform(key_two, (1, columns), jnp.float32, math.log(0.3), math.log(3.0)))
    entries = jnp.clip(jax.random.normal(key_three, (HEAD_DIM, columns), jnp.float32), -4.0, 4.0)
    return entries * row_scale * col_scale / math.sqrt(HEAD_DIM)


def steps_of(key, shape, cuts, low, largest):
    def one(position, parts):
        steps = jax.random.uniform(jax.random.fold_in(jax.random.fold_in(key, 6), position), (parts,), jnp.float32, low / len(cuts), largest / len(cuts))
        return jnp.repeat(jnp.exp(steps), shape[position] // parts).reshape((-1,) + (1,) * (len(shape) - position - 1))

    level = one(*cuts[0])
    for cut in cuts[1:]:
        level = level * one(*cut)
    return level


def normal_values(own_key, shape, deviation, limit, cuts=(), kind=jnp.bfloat16):
    factor_of = steps_of(own_key, shape, cuts, -0.22, 0.18) if cuts else 1.0
    result = jax.random.normal(own_key, shape, jnp.float32) * deviation * factor_of
    return jnp.minimum(jnp.maximum(result, -limit), limit).astype(kind)


def setup_inputs(seed: int = 0) -> dict:
    splits = jax.random.split(jax.random.key(seed), 7)
    return {
        "queries": normal_values(splits[0], (PATCHES, D), 1.0, 6.0, ((0, 32),)),
        "key_rows": normal_values(splits[1], (PATCHES, D), 1.0, 6.0, ((0, 32),)),
        "value_rows": normal_values(splits[2], (PATCHES, D), 1.0, 6.0, ((0, 32),)),
        "step_rates": draw_step_rates(jax.random.fold_in(splits[6], 71), 0),
        "fast_init": draw_fast_init(jax.random.fold_in(splits[6], 71), 0),
        "out_grad": normal_values(splits[5], (PATCHES, D), 1.0, 6.0, ((0, 32),)),
    }


highest = lax.Precision.HIGHEST
product_precision = lax.Precision.HIGH
step_size = 0.2
epsilon = 1e-06

def fast_apply(inputs, weights):
    gate_act = jnp.einsum('rhd,dhc->rhc', inputs, weights[:, 0], precision=product_precision)
    up_act = jnp.einsum('rhd,dhc->rhc', inputs, weights[:, 1], precision=product_precision)
    hidden = jax.nn.silu(gate_act) * up_act
    return jnp.einsum('rhc,dhc->rhd', hidden, weights[:, 2], precision=product_precision)

def update_term(key_part, value_part, rate_part, weights):

    def objective(fast):
        return -jnp.sum(rate_part[:, :, None] * value_part * fast_apply(key_part, fast))
    return jax.grad(objective)(weights)

def forward(query_heads, key_heads, value_heads, step_rates, weights):
    blocks = N_VIEW * N_PATCH // 8
    block_rows = PATCHES // blocks
    totals = lax.optimization_barrier(jnp.sum(step_rates, 0))
    eta = step_rates * (step_size * math.sqrt(PATCHES) / totals)

    def shaped(tensor):
        return tensor.reshape((blocks, block_rows) + tensor.shape[1:])

    def accumulate(running, block_data):
        return (running + update_term(block_data[0], block_data[1], block_data[2], weights), None)
    grad_sum, _ = lax.scan(jax.checkpoint(accumulate), jnp.zeros_like(weights), (shaped(key_heads), shaped(value_heads), shaped(eta)))
    moved = weights - grad_sum
    init_norm = jnp.sqrt(lax.optimization_barrier(jnp.sum(weights * weights, 0)) + epsilon)
    renormed = moved * init_norm * lax.rsqrt(lax.optimization_barrier(jnp.sum(moved * moved, 0)) + epsilon)

    def apply_block(block_data):
        return fast_apply(block_data, renormed)
    applied = lax.map(jax.checkpoint(apply_block), shaped(query_heads))
    return applied.reshape(query_heads.shape)

def reference(queries, key_rows, value_rows, step_rates, fast_init, out_grad):

    def to_heads(tensor):
        return tensor.astype(jnp.float32).reshape(PATCHES, HEADS, HEAD_DIM)

    def from_heads(tensor):
        return tensor.reshape(PATCHES, HEADS * HEAD_DIM).astype(jnp.bfloat16)
    weights = fast_init.reshape(HEAD_DIM, 3, HEADS, FF)
    _, pull_back = jax.vjp(forward, to_heads(queries), to_heads(key_rows), to_heads(value_rows), step_rates, weights)
    query_part, key_part, value_part, rate_part, fast_part = pull_back(to_heads(out_grad))
    fast_grad = fast_part.reshape(HEAD_DIM, 3 * HEADS * FF) / math.sqrt(PATCHES)
    return (from_heads(query_part), from_heads(key_part), from_heads(value_part), rate_part, fast_grad)
```

```python
import functools
import math

import jax
import jax.numpy as jnp
from jax import lax
from jax.experimental import pallas as pl
from jax.experimental.pallas import tpu as pltpu
from jax.sharding import PartitionSpec as P

AXES = ("view", "patch")
step_size = 0.2
epsilon = 1e-06
F32, BF16 = jnp.float32, jnp.bfloat16
LANES, SUBLANES = 128, 8


class Layout:
    def __init__(self, views, patches, heads, hidden, head_dim):
        self.heads, self.head_dim, self.hidden = heads, head_dim, hidden
        self.cores = 2 if views % 2 == 0 else 1
        self.patches, self.devices = patches, views * patches
        self.sub = patches // heads
        self.plane = (views // self.cores) * self.sub
        self.half = hidden // self.cores
        self.slot = self.half // self.plane
        self.pow2 = self.plane & (self.plane - 1) == 0
        rows = 3 * self.slot
        self.packed = head_dim == LANES + LANES // 2 and rows % (4 * SUBLANES) in (0, 2 * SUBLANES)

    def place(self, device):
        view, patch = divmod(device, self.patches)
        outer, core = divmod(view, self.cores)
        head, sub = divmod(patch, self.sub)
        return outer * self.sub + sub, core, head

    def device(self, member, core, head):
        outer, sub = divmod(member, self.sub)
        return (outer * self.cores + core) * self.patches + head * self.sub + sub

    def target(self, member, step):
        return member ^ step if self.pow2 else (member + step) % self.plane

    def origin(self, member, step):
        return member ^ step if self.pow2 else (member - step) % self.plane

    def perm(self, move):
        return [(i, self.device(*move(*self.place(i)))) for i in range(self.devices)]

    def core_perm(self):
        return self.perm(lambda j, c, h: (j, (c + 1) % self.cores, h))

    def head_perm(self, shift):
        return self.perm(lambda j, c, h: (j, c, (h + shift) % self.heads))

    def scatter_perm(self, step):
        return self.perm(lambda j, c, h: (self.target(j, step), c, h))

    def gather_perm(self, step):
        return self.perm(lambda j, c, h: (self.origin(j, step), c, h))

    def owner_rounds(self):
        count = self.devices
        edges = []
        for i in range(count):
            j, c, h = self.place(i)
            for m in range(3):
                piece = (m * self.heads + h) * self.cores * self.plane + c * self.plane + j
                edges.append((i, piece // 3, m, piece % 3))
        left, rounds = list(edges), []
        for _ in range(3):
            out_edges = [[] for _ in range(count)]
            for edge in left:
                out_edges[edge[0]].append(edge)
            match = {}

            def place_one(i, seen):
                for edge in out_edges[i]:
                    if edge[1] in seen:
                        continue
                    seen.add(edge[1])
                    if edge[1] not in match or place_one(match[edge[1]][0], seen):
                        match[edge[1]] = edge
                        return True
                return False

            for i in range(count):
                place_one(i, set())
            chosen = sorted(match.values())
            rounds.append(chosen)
            left = [edge for edge in left if edge not in match.values()]
        return rounds


def split(lay, x):
    if not lay.packed:
        return (x,)
    high = x.astype(BF16)
    return high, (x - high.astype(F32)).astype(BF16)


def dot(a, b, dims, precision=None):
    return lax.dot_general(
        a, b, (dims, ((), ())), precision=precision, preferred_element_type=F32
    )


NN, NT = ((1,), (0,)), ((1,), (1,))


def dot_left(parts, exact, dims):
    if len(parts) == 1:
        return dot(parts[0], exact, dims, lax.Precision.HIGH)
    return dot(parts[0], exact, dims) + dot(parts[1], exact, dims)


def dot_both(a, b, dims):
    if len(a) == 1:
        return dot(a[0], b[0], dims, lax.Precision.HIGH)
    return dot(a[0], b[0], dims) + (dot(a[0], b[1], dims) + dot(a[1], b[0], dims))


def gates(act):
    sig = 1.0 / (1.0 + jnp.exp(-act))
    silu = act * sig
    rest = 1.0 - sig
    return sig, silu, rest, sig + silu * rest


def cat(parts, axis):
    return jnp.concatenate(parts, axis)


def pack(lay, body, extra):
    if not lay.packed:
        return cat([body, jnp.broadcast_to(extra, (SUBLANES, lay.head_dim))], 0)
    rows = body.shape[0]
    tail = body[:, LANES:]
    tail = cat([tail[: rows // 2], tail[rows // 2 :]], 1)
    return cat([body[:, :LANES], tail, jnp.broadcast_to(extra, (SUBLANES, LANES))], 0)


def unpack(lay, payload):
    rows = 3 * lay.slot
    if not lay.packed:
        return payload[:rows], payload[rows : rows + 1, :1]
    tail = payload[rows : rows + rows // 2]
    half = LANES // 2
    tail = cat([tail[:, :half], tail[:, half:]], 0)
    return cat([payload[:rows], tail], 1), payload[rows + rows // 2 : rows + rows // 2 + 1, :1]


def pack_all(lay, grads, extra):
    outs = []
    for step in range(lay.plane):
        take = slice(step * lay.slot, (step + 1) * lay.slot)
        outs.append(pack(lay, cat([g[take] for g in grads], 0), extra))
    return outs


def unpack_all(lay, payloads):
    bodies = [unpack(lay, p)[0] for p in payloads]
    slot = lay.slot
    return [cat([b[m * slot : (m + 1) * slot] for b in bodies], 0) for m in range(3)]


def select_heads(lay, pieces, head_ids, shift):
    wanted = lax.rem(head_ids[0:1, :] + shift, lay.heads)
    result = pieces[0]
    for h in range(1, lay.heads):
        result = jnp.where(wanted == h, pieces[h], result)
    return result


def spread_rows(lay, with_rates, first, second, *rest):
    dim = lay.head_dim
    head_ids = rest[-1]
    turned = [x.astype(F32).T for x in (first, second)]
    pieces = [[t[h * dim : (h + 1) * dim] for h in range(lay.heads)] for t in turned]
    if with_rates:
        rates = rest[0]
        rows = rates.shape[0]
        rates = cat([rates, jnp.zeros((rows, LANES - lay.heads), F32)], 1).T
        pieces.append(
            [jnp.broadcast_to(rates[h : h + 1], (SUBLANES, rows)) for h in range(lay.heads)]
        )
    return [
        cat([select_heads(lay, p, head_ids, shift) for p in pieces], 0)
        for shift in range(lay.heads)
    ]


def join_rows(lay, slabs):
    dim = lay.head_dim
    kind = BF16 if lay.packed else F32
    first = cat([s[:dim] for s in slabs], 1).astype(kind)
    second = cat([s[dim : 2 * dim] for s in slabs], 1).astype(kind)
    return first, second


def join_rates(lay, slabs):
    dim = lay.head_dim
    return cat([s[2 * dim : 2 * dim + 1] for s in slabs], 1)


def update_fn(lay, *args):
    slabs, weights = args[:-1], args[-1]
    keys, values = join_rows(lay, slabs)
    rates = join_rates(lay, slabs)
    gate, up, down = (split(lay, weights[m]) for m in range(3))
    a = dot_left(gate, keys, NN)
    b = dot_left(up, keys, NN)
    u = dot_left(down, values, NN)
    _, silu, _, slope = gates(a)
    mu = -rates * u
    d_gate = dot_left(split(lay, mu * b * slope), keys, NT)
    d_up = dot_left(split(lay, mu * silu), keys, NT)
    d_down = dot_left(split(lay, -rates * (silu * b)), values, NT)
    total = jnp.sum(rates, 1, keepdims=True)
    return pack_all(lay, (d_gate, d_up, d_down), total)


def norms(initial, moved):
    norm = jnp.sqrt(jnp.sum(initial * initial, 1, keepdims=True) + epsilon)
    inverse = lax.rsqrt(jnp.sum(moved * moved, 1, keepdims=True) + epsilon)
    return norm, inverse


def own_weights(lay, weights):
    return cat([weights[m][: lay.slot] for m in range(3)], 0)


def renorm_fn(lay, coefficient, *args):
    payloads, initial = args[:-1], args[-1]
    body, total = unpack(lay, functools.reduce(jnp.add, payloads))
    grad = body * (coefficient / total)
    moved = initial - grad
    norm, inverse = norms(initial, moved)
    return [pack(lay, moved * (norm * inverse), total), grad, moved]


def apply_fn(lay, *args):
    count = lay.plane
    payloads, slabs = args[:count], args[count:]
    queries, cotangents = join_rows(lay, slabs)
    weights = unpack_all(lay, payloads)
    gate, up, down = (split(lay, w) for w in weights)
    a = dot_left(gate, queries, NN)
    b = dot_left(up, queries, NN)
    u = dot_left(down, cotangents, NN)
    _, silu, _, slope = gates(a)
    da = split(lay, u * b * slope)
    db = split(lay, u * silu)
    h = split(lay, silu * b)
    d_gate = dot_left(da, queries, NT)
    d_up = dot_left(db, queries, NT)
    d_down = dot_left(h, cotangents, NT)
    outs = pack_all(lay, (d_gate, d_up, d_down), jnp.zeros((1, 1), F32))
    turned = split(lay, cat([weights[0], weights[1]], 0).T)
    both = tuple(cat([x, y], 0) for x, y in zip(da, db))
    d_query = dot_both(turned, both, NN)
    rows = slabs[0].shape[1]
    cut = [d_query[:, i * rows : (i + 1) * rows] for i in range(len(slabs))]
    heads = lay.heads
    return outs + [stack(cut[:heads])] + ([stack(cut[heads:])] if lay.cores > 1 else [])


def stack(parts):
    return cat([p[None] for p in parts], 0)


def renorm_back_fn(lay, coefficient, *args):
    payloads = args[: lay.plane]
    total_payload, initial, grad, moved = args[lay.plane :]
    d_new, _ = unpack(lay, functools.reduce(jnp.add, payloads))
    _, total = unpack(lay, total_payload)
    norm, inverse = norms(initial, moved)
    dots = jnp.sum(d_new * moved, 1, keepdims=True)
    d_moved = d_new * (norm * inverse) - moved * (dots * norm * inverse * inverse * inverse)
    direct = d_moved + initial * (dots * inverse / norm)
    d_update = -d_moved
    part = jnp.sum(jnp.sum(d_update * grad, 1, keepdims=True), 0, keepdims=True)
    return [pack(lay, d_update * (coefficient / total), -part / total), direct]


def pull_fn(lay, *args):
    count = lay.plane
    payloads, slabs, weights = args[:count], args[count:-1], args[-1]
    keys, values = join_rows(lay, slabs)
    rates = join_rates(lay, slabs)
    moves = unpack_all(lay, payloads)
    d_totals = functools.reduce(jnp.add, [unpack(lay, p)[1] for p in payloads])
    gate, up, down = (split(lay, weights[m]) for m in range(3))
    gate_move, up_move, down_move = (split(lay, w) for w in moves)
    a = dot_left(gate, keys, NN)
    b = dot_left(up, keys, NN)
    u = dot_left(down, values, NN)
    ta = dot_left(gate_move, keys, NN)
    tb = dot_left(up_move, keys, NN)
    w = dot_left(down_move, values, NN)
    sig, silu, rest, slope = gates(a)
    bend = sig * rest * (2.0 + a * (rest - sig))
    hidden = silu * b
    hidden_dot = slope * ta * b + silu * tb
    rate_part = -jnp.sum(w * hidden + u * hidden_dot, 0, keepdims=True)
    mu = -rates
    wm, um = mu * w, mu * u
    ga = split(lay, wm * b * slope + um * (bend * ta * b + slope * tb))
    gb = split(lay, wm * silu + um * slope * ta)
    gta = split(lay, um * slope * b)
    gtb = split(lay, um * silu)
    mh = split(lay, mu * hidden)
    md = split(lay, mu * hidden_dot)
    d_gate = dot_left(ga, keys, NT)
    d_up = dot_left(gb, keys, NT)
    d_down = dot_left(md, values, NT)
    outs = pack_all(lay, (d_gate, d_up, d_down), jnp.zeros((1, 1), F32))
    turned = split(lay, cat([weights[0], weights[1], moves[0], moves[1]], 0).T)
    stacked = tuple(cat(x, 0) for x in zip(ga, gb, gta, gtb))
    d_key = dot_both(turned, stacked, NN)
    turned = split(lay, cat([moves[2], weights[2]], 0).T)
    d_value = dot_both(turned, tuple(cat(x, 0) for x in zip(mh, md)), NN)
    rate_part = rate_part + d_totals
    rows = slabs[0].shape[1]
    cut = []
    for i in range(len(slabs)):
        take = slice(i * rows, (i + 1) * rows)
        rate_rows = jnp.broadcast_to(rate_part[:, take], (SUBLANES, rows))
        cut.append(cat([d_key[:, take], d_value[:, take], rate_rows], 0))
    heads = lay.heads
    return outs + [stack(cut[:heads])] + ([stack(cut[heads:])] if lay.cores > 1 else [])


def finish_fn(lay, count, *args):
    slabs, head_ids = args[:-1], args[-1]
    dim = lay.head_dim
    outs = []
    for n in range(count):
        pieces = [s[n * dim : (n + 1) * dim] for s in slabs]
        ordered = [
            select_heads(lay, pieces, lay.heads - head_ids, h) for h in range(lay.heads)
        ]
        outs.append(cat(ordered, 0).T.astype(BF16))
    if slabs[0].shape[0] > count * dim:
        pieces = [s[count * dim : count * dim + 1] for s in slabs]
        rows = [select_heads(lay, pieces, lay.heads - head_ids, h) for h in range(lay.heads)]
        rows.append(jnp.zeros((LANES - lay.heads, slabs[0].shape[1]), F32))
        outs.append(cat(rows, 0).T[:, : lay.heads])
    return outs


def run(lay, name, fn, args, always=False):
    if not (lay.packed or always):
        return fn(*args)
    shapes = jax.eval_shape(fn, *args)

    def kernel(*refs):
        ins, outs = refs[: len(args)], refs[len(args) :]
        for ref, value in zip(outs, fn(*[r[...] for r in ins])):
            ref[...] = value

    vmem = pl.BlockSpec(memory_space=pltpu.VMEM)
    return pl.pallas_call(
        kernel,
        out_shape=[jax.ShapeDtypeStruct(s.shape, s.dtype) for s in shapes],
        in_specs=[vmem] * len(args),
        out_specs=[vmem] * len(shapes),
        compiler_params=pltpu.CompilerParams(vmem_limit_bytes=40 * 1024 * 1024),
        name=name,
    )(*args)


def on_device(lay, queries, key_rows, value_rows, step_rates, fast_init, out_grad):
    head_dim, columns = fast_init.shape
    heads, slot, plane = lay.heads, lay.slot, lay.plane
    coefficient = step_size * math.sqrt(queries.shape[0] * lay.devices)
    view, patch = lax.axis_index("view"), lax.axis_index("patch")
    core = lax.rem(view, lay.cores)
    head = patch // lay.sub
    member = view // lay.cores * lay.sub + lax.rem(patch, lay.sub)
    me = view * lay.patches + patch
    head_ids = jnp.full((SUBLANES, LANES), head, jnp.int32)

    def send(x, perm):
        return lax.ppermute(x, AXES, perm)

    def to_heads(slabs):
        mine = [slabs[0]] + [send(slabs[s], lay.head_perm(s)) for s in range(1, heads)]
        others = [send(x, lay.core_perm()) for x in mine] if lay.cores > 1 else []
        return mine + others

    def from_heads(parts):
        mine = parts[0]
        if lay.cores > 1:
            mine = mine + send(parts[1], lay.core_perm())
        return [mine[0]] + [send(mine[s], lay.head_perm(heads - s)) for s in range(1, heads)]

    def scatter(payloads):
        moved = [send(payloads[r], lay.scatter_perm(r)) for r in range(1, plane)]
        return [payloads[0]] + moved

    def gather(payload):
        return [payload] + [send(payload, lay.gather_perm(r)) for r in range(1, plane)]

    fn = functools.partial
    kv = to_heads(
        run(lay, "spread_kv", fn(spread_rows, lay, True), (key_rows, value_rows, step_rates, head_ids), True)
    )
    qg = to_heads(run(lay, "spread_qg", fn(spread_rows, lay, False), (queries, out_grad, head_ids), True))

    first = head * lay.hidden + core * lay.half
    order = jnp.stack([lay.target(member, r) for r in range(plane)])
    turned = []
    for m in range(3):
        part = lax.dynamic_slice_in_dim(fast_init, m * heads * lay.hidden + first, lay.half, 1)
        turned.append(part.T.reshape(plane, slot, head_dim)[order].reshape(lay.half, head_dim))
    weights = jnp.stack(turned)
    own = jnp.concatenate([t[:slot] for t in turned], 0)

    sums = scatter(run(lay, "update", fn(update_fn, lay), (*kv, weights)))
    payload, grad, moved = run(lay, "renorm", fn(renorm_fn, lay, coefficient), (*sums, own))
    applied = run(lay, "apply", fn(apply_fn, lay), (*gather(payload), *qg))
    sums, query_parts = scatter(applied[:plane]), applied[plane:]
    d_payload, direct = run(
        lay, "renorm_back", fn(renorm_back_fn, lay, coefficient), (*sums, payload, own, grad, moved)
    )
    pulled = run(lay, "pull", fn(pull_fn, lay), (*gather(d_payload), *kv, weights))
    sums, key_parts = scatter(pulled[:plane]), pulled[plane:]
    (query_grad,) = run(
        lay, "finish_query", fn(finish_fn, lay, 1), (*from_heads(query_parts), head_ids), True
    )
    key_grad, value_grad, rate_grad = run(
        lay, "finish_key", fn(finish_fn, lay, 2), (*from_heads(key_parts), head_ids), True
    )

    def total_fn(*args):
        body, _ = unpack(lay, functools.reduce(jnp.add, args[:-1]))
        return [(body + args[-1]) / math.sqrt(queries.shape[0] * lay.devices)]

    (final,) = run(lay, "total", total_fn, (*sums, direct))
    pieces = final.reshape(3, slot, head_dim)
    arrived, places = [], []
    for chosen in lay.owner_rounds():
        which = jnp.array([m for _, _, m, _ in chosen], jnp.int32)[me]
        perm = [(i, o) for i, o, _, _ in chosen]
        spots = [0] * lay.devices
        for _, o, _, spot in chosen:
            spots[o] = spot
        arrived.append(send(lax.dynamic_index_in_dim(pieces, which, 0, False), perm))
        places.append(spots)
    rounds = [[places[t][i] for t in range(3)] for i in range(lay.devices)]
    inverse = jnp.array([[r.index(q) for q in range(3)] for r in rounds], jnp.int32)[me]
    fast_grad = jnp.stack(arrived)[inverse].reshape(3 * slot, head_dim).T
    return query_grad, key_grad, value_grad, rate_grad, fast_grad


def solution(mesh):
    rows = P(AXES, None)

    def whole(queries, key_rows, value_rows, step_rates, fast_init, out_grad):
        heads = step_rates.shape[1]
        head_dim, columns = fast_init.shape
        lay = Layout(
            mesh.shape["view"], mesh.shape["patch"], heads, columns // (3 * heads), head_dim
        )
        return jax.shard_map(
            functools.partial(on_device, lay),
            mesh=mesh,
            in_specs=(rows, rows, rows, rows, P(), rows),
            out_specs=(rows, rows, rows, rows, P(None, AXES)),
            check_vma=False,
        )(queries, key_rows, value_rows, step_rates, fast_init, out_grad)

    return whole
```

```python
import functools
import math

import jax
import jax.numpy as jnp
from jax import lax
from jax.experimental import pallas as pl
from jax.experimental.pallas import tpu as pltpu
from jax.sharding import PartitionSpec as P

AXES = ("view", "patch")
step_size = 0.2
epsilon = 1e-06
F32, BF16 = jnp.float32, jnp.bfloat16
LANES, SUBLANES = 128, 8


class Layout:
    def __init__(self, views, patches, heads, hidden, head_dim):
        self.heads, self.head_dim, self.hidden = heads, head_dim, hidden
        self.cores = 2 if views % 2 == 0 else 1
        self.patches, self.devices = patches, views * patches
        self.sub = patches // heads
        self.plane = (views // self.cores) * self.sub
        self.half = hidden // self.cores
        self.slot = self.half // self.plane
        self.pow2 = self.plane & (self.plane - 1) == 0
        rows = 3 * self.slot
        self.packed = head_dim == LANES + LANES // 2 and rows % (4 * SUBLANES) in (0, 2 * SUBLANES)

    def place(self, device):
        view, patch = divmod(device, self.patches)
        outer, core = divmod(view, self.cores)
        head, sub = divmod(patch, self.sub)
        return outer * self.sub + sub, core, head

    def device(self, member, core, head):
        outer, sub = divmod(member, self.sub)
        return (outer * self.cores + core) * self.patches + head * self.sub + sub

    def target(self, member, step):
        return member ^ step if self.pow2 else (member + step) % self.plane

    def origin(self, member, step):
        return member ^ step if self.pow2 else (member - step) % self.plane

    def perm(self, move):
        return [(i, self.device(*move(*self.place(i)))) for i in range(self.devices)]

    def core_perm(self):
        return self.perm(lambda j, c, h: (j, (c + 1) % self.cores, h))

    def head_perm(self, shift):
        return self.perm(lambda j, c, h: (j, c, (h + shift) % self.heads))

    def scatter_perm(self, step):
        return self.perm(lambda j, c, h: (self.target(j, step), c, h))

    def gather_perm(self, step):
        return self.perm(lambda j, c, h: (self.origin(j, step), c, h))

    def owner_rounds(self):
        count = self.devices
        edges = []
        for i in range(count):
            j, c, h = self.place(i)
            for m in range(3):
                piece = (m * self.heads + h) * self.cores * self.plane + c * self.plane + j
                edges.append((i, piece // 3, m, piece % 3))
        left, rounds = list(edges), []
        for _ in range(3):
            out_edges = [[] for _ in range(count)]
            for edge in left:
                out_edges[edge[0]].append(edge)
            match = {}

            def place_one(i, seen):
                for edge in out_edges[i]:
                    if edge[1] in seen:
                        continue
                    seen.add(edge[1])
                    if edge[1] not in match or place_one(match[edge[1]][0], seen):
                        match[edge[1]] = edge
                        return True
                return False

            for i in range(count):
                place_one(i, set())
            chosen = sorted(match.values())
            rounds.append(chosen)
            left = [edge for edge in left if edge not in match.values()]
        return rounds


def split(lay, x):
    if not lay.packed:
        return (x,)
    high = x.astype(BF16)
    return high, (x - high.astype(F32)).astype(BF16)


def dot(a, b, dims, precision=None):
    return lax.dot_general(
        a, b, (dims, ((), ())), precision=precision, preferred_element_type=F32
    )


NN, NT = ((1,), (0,)), ((1,), (1,))


def dot_left(parts, exact, dims):
    if len(parts) == 1:
        return dot(parts[0], exact, dims, lax.Precision.HIGH)
    return dot(parts[0], exact, dims) + dot(parts[1], exact, dims)


def dot_both(a, b, dims):
    if len(a) == 1:
        return dot(a[0], b[0], dims, lax.Precision.HIGH)
    return dot(a[0], b[0], dims) + (dot(a[0], b[1], dims) + dot(a[1], b[0], dims))


def gates(act):
    sig = 1.0 / (1.0 + jnp.exp(-act))
    silu = act * sig
    rest = 1.0 - sig
    return sig, silu, rest, sig + silu * rest


def cat(parts, axis):
    return jnp.concatenate(parts, axis)


def pack(lay, body, extra):
    if not lay.packed:
        return cat([body, jnp.broadcast_to(extra, (SUBLANES, lay.head_dim))], 0)
    rows = body.shape[0]
    tail = body[:, LANES:]
    tail = cat([tail[: rows // 2], tail[rows // 2 :]], 1)
    return cat([body[:, :LANES], tail, jnp.broadcast_to(extra, (SUBLANES, LANES))], 0)


def unpack(lay, payload):
    rows = 3 * lay.slot
    if not lay.packed:
        return payload[:rows], payload[rows : rows + 1, :1]
    tail = payload[rows : rows + rows // 2]
    half = LANES // 2
    tail = cat([tail[:, :half], tail[:, half:]], 0)
    return cat([payload[:rows], tail], 1), payload[rows + rows // 2 : rows + rows // 2 + 1, :1]


def pack_all(lay, grads, extra):
    outs = []
    for step in range(lay.plane):
        take = slice(step * lay.slot, (step + 1) * lay.slot)
        outs.append(pack(lay, cat([g[take] for g in grads], 0), extra))
    return outs


def unpack_all(lay, payloads):
    bodies = [unpack(lay, p)[0] for p in payloads]
    slot = lay.slot
    return [cat([b[m * slot : (m + 1) * slot] for b in bodies], 0) for m in range(3)]


def select_heads(lay, pieces, head_ids, shift):
    wanted = lax.rem(head_ids[0:1, :] + shift, lay.heads)
    result = pieces[0]
    for h in range(1, lay.heads):
        result = jnp.where(wanted == h, pieces[h], result)
    return result


def spread_rows(lay, with_rates, first, second, *rest):
    dim = lay.head_dim
    head_ids = rest[-1]
    turned = [x.astype(F32).T for x in (first, second)]
    pieces = [[t[h * dim : (h + 1) * dim] for h in range(lay.heads)] for t in turned]
    if with_rates:
        rates = rest[0]
        rows = rates.shape[1]
        pieces.append(
            [jnp.broadcast_to(rates[h : h + 1], (SUBLANES, rows)) for h in range(lay.heads)]
        )
    return [
        cat([select_heads(lay, p, head_ids, shift) for p in pieces], 0)
        for shift in range(lay.heads)
    ]


def join_rows(lay, slabs):
    dim = lay.head_dim
    kind = BF16 if lay.packed else F32
    first = cat([s[:dim] for s in slabs], 1).astype(kind)
    second = cat([s[dim : 2 * dim] for s in slabs], 1).astype(kind)
    return first, second


def join_rates(lay, slabs):
    dim = lay.head_dim
    return cat([s[2 * dim : 2 * dim + 1] for s in slabs], 1)


def update_fn(lay, *args):
    slabs, weights = args[:-1], args[-1]
    keys, values = join_rows(lay, slabs)
    rates = join_rates(lay, slabs)
    gate, up, down = (split(lay, weights[m]) for m in range(3))
    a = dot_left(gate, keys, NN)
    b = dot_left(up, keys, NN)
    u = dot_left(down, values, NN)
    _, silu, _, slope = gates(a)
    mu = -rates * u
    d_gate = dot_left(split(lay, mu * b * slope), keys, NT)
    d_up = dot_left(split(lay, mu * silu), keys, NT)
    d_down = dot_left(split(lay, -rates * (silu * b)), values, NT)
    total = jnp.sum(rates, 1, keepdims=True)
    return pack_all(lay, (d_gate, d_up, d_down), total)


def norms(initial, moved):
    norm = jnp.sqrt(jnp.sum(initial * initial, 1, keepdims=True) + epsilon)
    inverse = lax.rsqrt(jnp.sum(moved * moved, 1, keepdims=True) + epsilon)
    return norm, inverse


def own_weights(lay, weights):
    return cat([weights[m][: lay.slot] for m in range(3)], 0)


def renorm_fn(lay, coefficient, *args):
    payloads, initial = args[:-1], args[-1]
    body, total = unpack(lay, functools.reduce(jnp.add, payloads))
    grad = body * (coefficient / total)
    moved = initial - grad
    norm, inverse = norms(initial, moved)
    return [pack(lay, moved * (norm * inverse), total), grad, moved]


def apply_fn(lay, *args):
    count = lay.plane
    payloads, slabs = args[:count], args[count:]
    queries, cotangents = join_rows(lay, slabs)
    weights = unpack_all(lay, payloads)
    gate, up, down = (split(lay, w) for w in weights)
    a = dot_left(gate, queries, NN)
    b = dot_left(up, queries, NN)
    u = dot_left(down, cotangents, NN)
    _, silu, _, slope = gates(a)
    da = split(lay, u * b * slope)
    db = split(lay, u * silu)
    h = split(lay, silu * b)
    d_gate = dot_left(da, queries, NT)
    d_up = dot_left(db, queries, NT)
    d_down = dot_left(h, cotangents, NT)
    outs = pack_all(lay, (d_gate, d_up, d_down), jnp.zeros((1, 1), F32))
    turned = split(lay, cat([weights[0], weights[1]], 0).T)
    both = tuple(cat([x, y], 0) for x, y in zip(da, db))
    d_query = dot_both(turned, both, NN)
    rows = slabs[0].shape[1]
    cut = [d_query[:, i * rows : (i + 1) * rows] for i in range(len(slabs))]
    heads = lay.heads
    return outs + cut[:heads] + ([stack(cut[heads:])] if lay.cores > 1 else [])


def stack(parts):
    return cat([p[None] for p in parts], 0)


def renorm_back_fn(lay, coefficient, *args):
    payloads = args[: lay.plane]
    total_payload, initial, grad, moved = args[lay.plane :]
    d_new, _ = unpack(lay, functools.reduce(jnp.add, payloads))
    _, total = unpack(lay, total_payload)
    norm, inverse = norms(initial, moved)
    dots = jnp.sum(d_new * moved, 1, keepdims=True)
    d_moved = d_new * (norm * inverse) - moved * (dots * norm * inverse * inverse * inverse)
    direct = d_moved + initial * (dots * inverse / norm)
    d_update = -d_moved
    part = jnp.sum(jnp.sum(d_update * grad, 1, keepdims=True), 0, keepdims=True)
    return [pack(lay, d_update * (coefficient / total), -part / total), direct]


def pull_fn(lay, *args):
    count = lay.plane
    payloads, slabs, weights = args[:count], args[count:-1], args[-1]
    keys, values = join_rows(lay, slabs)
    rates = join_rates(lay, slabs)
    moves = unpack_all(lay, payloads)
    d_totals = functools.reduce(jnp.add, [unpack(lay, p)[1] for p in payloads])
    gate, up, down = (split(lay, weights[m]) for m in range(3))
    gate_move, up_move, down_move = (split(lay, w) for w in moves)
    a = dot_left(gate, keys, NN)
    b = dot_left(up, keys, NN)
    u = dot_left(down, values, NN)
    ta = dot_left(gate_move, keys, NN)
    tb = dot_left(up_move, keys, NN)
    w = dot_left(down_move, values, NN)
    sig, silu, rest, slope = gates(a)
    bend = sig * rest * (2.0 + a * (rest - sig))
    hidden = silu * b
    hidden_dot = slope * ta * b + silu * tb
    rate_part = -jnp.sum(w * hidden + u * hidden_dot, 0, keepdims=True)
    mu = -rates
    wm, um = mu * w, mu * u
    ga = split(lay, wm * b * slope + um * (bend * ta * b + slope * tb))
    gb = split(lay, wm * silu + um * slope * ta)
    gta = split(lay, um * slope * b)
    gtb = split(lay, um * silu)
    mh = split(lay, mu * hidden)
    md = split(lay, mu * hidden_dot)
    d_gate = dot_left(ga, keys, NT)
    d_up = dot_left(gb, keys, NT)
    d_down = dot_left(md, values, NT)
    outs = pack_all(lay, (d_gate, d_up, d_down), jnp.zeros((1, 1), F32))
    turned = split(lay, cat([weights[0], weights[1], moves[0], moves[1]], 0).T)
    stacked = tuple(cat(x, 0) for x in zip(ga, gb, gta, gtb))
    d_key = dot_both(turned, stacked, NN)
    turned = split(lay, cat([moves[2], weights[2]], 0).T)
    d_value = dot_both(turned, tuple(cat(x, 0) for x in zip(mh, md)), NN)
    rate_part = rate_part + d_totals
    rows = slabs[0].shape[1]
    cut = []
    for i in range(len(slabs)):
        take = slice(i * rows, (i + 1) * rows)
        rate_rows = jnp.broadcast_to(rate_part[:, take], (SUBLANES, rows))
        cut.append(cat([d_key[:, take], d_value[:, take], rate_rows], 0))
    heads = lay.heads
    return outs + cut[:heads] + ([stack(cut[heads:])] if lay.cores > 1 else [])


def finish_fn(lay, count, *args):
    slabs, head_ids = args[:-1], args[-1]
    dim = lay.head_dim
    outs = []
    for n in range(count):
        pieces = [s[n * dim : (n + 1) * dim] for s in slabs]
        ordered = [
            select_heads(lay, pieces, lay.heads - head_ids, h) for h in range(lay.heads)
        ]
        outs.append(cat(ordered, 0).T.astype(BF16))
    if slabs[0].shape[0] > count * dim:
        pieces = [s[count * dim : count * dim + 1] for s in slabs]
        rows = [select_heads(lay, pieces, lay.heads - head_ids, h) for h in range(lay.heads)]
        outs.append(cat(rows, 0))
    return outs


def add_fn(lay, *args):
    return [part + args[-1][i] for i, part in enumerate(args[:-1])]


def choose(pieces, index):
    result = pieces[0]
    for i in range(1, len(pieces)):
        result = jnp.where(index == i, pieces[i], result)
    return result


def total_fn(lay, scale, *args):
    payloads, direct, places = args[: lay.plane], args[-2], args[-1]
    body, _ = unpack(lay, functools.reduce(jnp.add, payloads))
    final = (body + direct) / scale
    pieces = [final[m * lay.slot : (m + 1) * lay.slot] for m in range(3)]
    return [choose(pieces, places[0:1, t : t + 1]) for t in range(3)]


def place_fn(lay, *args):
    pieces, places = args[:3], args[3]
    return [cat([choose(pieces, places[0:1, 3 + q : 4 + q]) for q in range(3)], 0)]


VMEM_LIMIT = 24 * 1024 * 1024


def run(lay, name, fn, args, always=False, deps=()):
    if not (lay.packed or always):
        return fn(*args)
    shapes = jax.eval_shape(fn, *args)
    deps = [x[: min(SUBLANES, x.shape[0])] for x in deps]
    count = len(args)

    def kernel(*refs):
        ins, outs = refs[:count], refs[count + len(deps) :]
        for ref, value in zip(outs, fn(*[r[...] for r in ins])):
            ref[...] = value

    vmem = pl.BlockSpec(memory_space=pltpu.VMEM)
    return pl.pallas_call(
        kernel,
        out_shape=[jax.ShapeDtypeStruct(s.shape, s.dtype) for s in shapes],
        in_specs=[vmem] * (count + len(deps)),
        out_specs=[vmem] * len(shapes),
        compiler_params=pltpu.CompilerParams(vmem_limit_bytes=VMEM_LIMIT),
        name=name,
    )(*args, *deps)


def tie(lay, name, arrays, deps):
    if not lay.packed:
        return arrays
    deps = [x[:SUBLANES] for x in deps]
    vmem = pl.BlockSpec(memory_space=pltpu.VMEM)
    return list(
        pl.pallas_call(
            lambda *refs: None,
            out_shape=[jax.ShapeDtypeStruct(a.shape, a.dtype) for a in arrays],
            in_specs=[vmem] * (len(arrays) + len(deps)),
            out_specs=[vmem] * len(arrays),
            input_output_aliases={i: i for i in range(len(arrays))},
            compiler_params=pltpu.CompilerParams(vmem_limit_bytes=VMEM_LIMIT),
            name=name,
        )(*arrays, *deps)
    )


def on_device(lay, queries, key_rows, value_rows, step_rates, fast_init, out_grad):
    head_dim, columns = fast_init.shape
    heads, slot, plane = lay.heads, lay.slot, lay.plane
    coefficient = step_size * math.sqrt(queries.shape[0] * lay.devices)
    view, patch = lax.axis_index("view"), lax.axis_index("patch")
    core = lax.rem(view, lay.cores)
    head = patch // lay.sub
    member = view // lay.cores * lay.sub + lax.rem(patch, lay.sub)
    me = view * lay.patches + patch
    head_ids = jnp.full((SUBLANES, LANES), head, jnp.int32)

    def send(x, perm):
        return lax.ppermute(x, AXES, perm)

    def over_heads(slabs):
        return [slabs[0]] + [send(slabs[t], lay.head_perm(t)) for t in range(1, heads)]

    def over_cores(slabs):
        return [send(x, lay.core_perm()) for x in slabs] if lay.cores > 1 else []

    def total_rows(name, parts):
        if lay.cores == 1:
            return parts
        return run(lay, name, fn(add_fn, lay), (*parts[:heads], send(parts[heads], lay.core_perm())))

    def back_home(slabs):
        return [slabs[0]] + [send(slabs[t], lay.head_perm(heads - t)) for t in range(1, heads)]

    def scatter(payloads):
        moved = [send(payloads[r], lay.scatter_perm(r)) for r in range(1, plane)]
        return [payloads[0]] + moved

    def gather(payload):
        return [payload] + [send(payload, lay.gather_perm(r)) for r in range(1, plane)]

    fn = functools.partial
    scale = math.sqrt(queries.shape[0] * lay.devices)
    kv = over_heads(
        run(
            lay,
            "spread_kv",
            fn(spread_rows, lay, True),
            (key_rows, value_rows, step_rates.T, head_ids),
            always=True,
        )
    )
    qg = over_heads(
        run(
            lay,
            "spread_qg",
            fn(spread_rows, lay, False),
            (queries, out_grad, head_ids),
            always=True,
            deps=(kv[1],),
        )
    )
    kv = kv + over_cores(kv)

    owner_perms, table = owner_plan(lay)
    places = lax.dynamic_slice_in_dim(jnp.array(table, jnp.int32), me, 1, 0)
    first = head * lay.hidden + core * lay.half
    order = jnp.stack([lay.target(member, r) for r in range(plane)])
    turned = []
    for m in range(3):
        part = lax.dynamic_slice_in_dim(fast_init, m * heads * lay.hidden + first, lay.half, 1)
        turned.append(part.T.reshape(plane, slot, head_dim)[order].reshape(lay.half, head_dim))
    weights = jnp.stack(turned)
    own = jnp.concatenate([t[:slot] for t in turned], 0)

    sums = scatter(run(lay, "update", fn(update_fn, lay), (*kv, weights), deps=(own, places)))
    payload, grad, moved = run(lay, "renorm", fn(renorm_fn, lay, coefficient), (*sums, own))
    renewed = gather(payload)
    qg = tie(lay, "hold_qg", qg, (renewed[-1],))
    qg = qg + over_cores(qg)
    applied = run(lay, "apply", fn(apply_fn, lay), (*renewed, *qg))
    sums = scatter(applied[:plane])
    query_home = total_rows("add_query", applied[plane:])
    d_payload, direct = run(
        lay,
        "renorm_back",
        fn(renorm_back_fn, lay, coefficient),
        (*sums, payload, own, grad, moved),
        deps=tuple(query_home),
    )
    query_home = back_home(query_home)
    pulled = run(
        lay, "pull", fn(pull_fn, lay), (*gather(d_payload), *kv, weights), deps=tuple(query_home)
    )
    key_home = total_rows("add_key", pulled[plane:])
    sums = scatter(pulled[:plane])
    pieces = run(
        lay, "total", fn(total_fn, lay, scale), (*sums, direct, places), deps=tuple(key_home)
    )
    key_home = back_home(key_home)
    (query_grad,) = run(
        lay,
        "finish_query",
        fn(finish_fn, lay, 1),
        (*query_home, head_ids),
        always=True,
        deps=tuple(pulled[:1]),
    )
    arrived = [send(x, perm) for x, perm in zip(pieces, owner_perms)]
    (fast_grad,) = run(lay, "place", fn(place_fn, lay), (*arrived, places))
    key_grad, value_grad, rate_grad = run(
        lay, "finish_key", fn(finish_fn, lay, 2), (*key_home, head_ids), always=True
    )
    return query_grad, key_grad, value_grad, rate_grad.T, fast_grad.T


def owner_plan(lay):
    rounds = lay.owner_rounds()
    table = [[0] * LANES for _ in range(lay.devices)]
    for t, chosen in enumerate(rounds):
        for source, owner, m, spot in chosen:
            table[source][t] = m
            table[owner][3 + spot] = t
    return [[(i, o) for i, o, _, _ in chosen] for chosen in rounds], table


def solution(mesh):
    rows = P(AXES, None)

    def whole(queries, key_rows, value_rows, step_rates, fast_init, out_grad):
        heads = step_rates.shape[1]
        head_dim, columns = fast_init.shape
        lay = Layout(
            mesh.shape["view"], mesh.shape["patch"], heads, columns // (3 * heads), head_dim
        )
        return jax.shard_map(
            functools.partial(on_device, lay),
            mesh=mesh,
            in_specs=(rows, rows, rows, rows, P(), rows),
            out_specs=(rows, rows, rows, rows, P(None, AXES)),
            check_vma=False,
        )(queries, key_rows, value_rows, step_rates, fast_init, out_grad)

    return whole
```

```python
import functools
import math

import jax
import jax.numpy as jnp
from jax import lax
from jax.experimental import pallas as pl
from jax.experimental.pallas import tpu as pltpu
from jax.sharding import PartitionSpec as P


AXES = ("view", "patch")
step_size = 0.2
epsilon = 1e-06
F32, BF16 = jnp.float32, jnp.bfloat16
LANES, SUBLANES = 128, 8


class Layout:
    def __init__(self, views, patches, heads, hidden, head_dim):
        self.heads, self.head_dim, self.hidden = heads, head_dim, hidden
        self.cores = 2 if views % 2 == 0 else 1
        self.patches, self.devices = patches, views * patches
        self.sub = patches // heads
        self.plane = (views // self.cores) * self.sub
        self.half = hidden // self.cores
        self.slot = self.half // self.plane
        self.pow2 = self.plane & (self.plane - 1) == 0
        rows = 3 * self.slot
        self.packed = (
            head_dim == LANES + LANES // 2
            and rows % (2 * SUBLANES) == 0
            and (3 * self.half) % (4 * SUBLANES) == 0
            and self.pow2
            and self.plane > 1
        )

    def place(self, device):
        view, patch = divmod(device, self.patches)
        outer, core = divmod(view, self.cores)
        head, sub = divmod(patch, self.sub)
        return outer * self.sub + sub, core, head

    def device(self, member, core, head):
        outer, sub = divmod(member, self.sub)
        return (outer * self.cores + core) * self.patches + head * self.sub + sub

    def target(self, member, step):
        return member ^ step if self.pow2 else (member + step) % self.plane

    def origin(self, member, step):
        return member ^ step if self.pow2 else (member - step) % self.plane

    def perm(self, move):
        return [(i, self.device(*move(*self.place(i)))) for i in range(self.devices)]

    def core_perm(self):
        return self.perm(lambda j, c, h: (j, (c + 1) % self.cores, h))

    def head_perm(self, shift):
        return self.perm(lambda j, c, h: (j, c, (h + shift) % self.heads))

    def scatter_perm(self, step):
        return self.perm(lambda j, c, h: (self.target(j, step), c, h))

    def gather_perm(self, step):
        return self.perm(lambda j, c, h: (self.origin(j, step), c, h))

    def flip_perm(self, bit):
        return self.perm(lambda j, c, h: (j ^ bit, c, h))

    def owner_rounds(self):
        count = self.devices
        edges = []
        for i in range(count):
            j, c, h = self.place(i)
            for m in range(3):
                piece = (m * self.heads + h) * self.cores * self.plane + c * self.plane + j
                edges.append((i, piece // 3, m, piece % 3))
        left, rounds = list(edges), []
        for _ in range(3):
            out_edges = [[] for _ in range(count)]
            for edge in left:
                out_edges[edge[0]].append(edge)
            match = {}

            def place_one(i, seen):
                for edge in out_edges[i]:
                    if edge[1] in seen:
                        continue
                    seen.add(edge[1])
                    if edge[1] not in match or place_one(match[edge[1]][0], seen):
                        match[edge[1]] = edge
                        return True
                return False

            for i in range(count):
                place_one(i, set())
            chosen = sorted(match.values())
            rounds.append(chosen)
            left = [edge for edge in left if edge not in match.values()]
        return rounds


def split(lay, x):
    if not lay.packed:
        return (x,)
    high = x.astype(BF16)
    return high, (x - high.astype(F32)).astype(BF16)


def dot(a, b, dims, precision=None):
    return lax.dot_general(
        a, b, (dims, ((), ())), precision=precision, preferred_element_type=F32
    )


NN, NT = ((1,), (0,)), ((1,), (1,))


def dot_left(parts, exact, dims):
    if len(parts) == 1:
        return dot(parts[0], exact, dims, lax.Precision.HIGH)
    return dot(parts[0], exact, dims) + dot(parts[1], exact, dims)


def dot_both(a, b, dims):
    if len(a) == 1:
        return dot(a[0], b[0], dims, lax.Precision.HIGH)
    return dot(a[0], b[0], dims) + (dot(a[0], b[1], dims) + dot(a[1], b[0], dims))


def gates(act):
    sig = 1.0 / (1.0 + jnp.exp(-act))
    silu = act * sig
    rest = 1.0 - sig
    return sig, silu, rest, sig + silu * rest


def cat(parts, axis):
    return jnp.concatenate(parts, axis)


def pack(lay, body, extra):
    if not lay.packed:
        return cat([body, jnp.broadcast_to(extra, (SUBLANES, lay.head_dim))], 0)
    rows = body.shape[0]
    tail = body[:, LANES:]
    tail = cat([tail[: rows // 2], tail[rows // 2 :]], 1)
    return cat([body[:, :LANES], tail, jnp.broadcast_to(extra, (SUBLANES, LANES))], 0)


def unpack(lay, payload, rows=None):
    rows = 3 * lay.slot if rows is None else rows
    if not lay.packed:
        return payload[:rows], payload[rows : rows + 1, :1]
    tail = payload[rows : rows + rows // 2]
    half = LANES // 2
    tail = cat([tail[:, :half], tail[:, half:]], 0)
    return cat([payload[:rows], tail], 1), payload[rows + rows // 2 : rows + rows // 2 + 1, :1]


def pack_halves(lay, grads, extra):
    body = cat(grads, 0)
    rows = body.shape[0] // 2
    return [pack(lay, body[:rows], extra), pack(lay, body[rows:], extra)]


def unpack_halves(lay, first, first_in, second, second_in):
    rows = 3 * lay.half // 2
    top, extra = unpack(lay, first + first_in, rows)
    bottom, _ = unpack(lay, second + second_in, rows)
    return cat([top, bottom], 0), extra


def in_slots(lay, parts):
    slot = lay.slot
    return [cat([p[k * slot : (k + 1) * slot] for p in parts], 0) for k in range(lay.plane)]


def member_id(places):
    return places[0:1, 6:7]


def choose(pieces, index):
    result = pieces[0]
    for i in range(1, len(pieces)):
        result = jnp.where(index == i, pieces[i], result)
    return result


def in_three(lay, body):
    return [body[m * lay.half : (m + 1) * lay.half] for m in range(3)]


def pack_all(lay, grads, extra):
    outs = []
    for step in range(lay.plane):
        take = slice(step * lay.slot, (step + 1) * lay.slot)
        outs.append(pack(lay, cat([g[take] for g in grads], 0), extra))
    return outs


def unpack_all(lay, payloads):
    bodies = [unpack(lay, p)[0] for p in payloads]
    slot = lay.slot
    return [cat([b[m * slot : (m + 1) * slot] for b in bodies], 0) for m in range(3)]


def select_heads(lay, pieces, head_ids, shift):
    wanted = lax.rem(head_ids[0:1, :] + shift, lay.heads)
    result = pieces[0]
    for h in range(1, lay.heads):
        result = jnp.where(wanted == h, pieces[h], result)
    return result


def spread_rows(lay, with_rates, first, second, *rest):
    dim = lay.head_dim
    head_ids = rest[-1]
    turned = [x.astype(F32).T for x in (first, second)]
    pieces = [[t[h * dim : (h + 1) * dim] for h in range(lay.heads)] for t in turned]
    if with_rates:
        rates = rest[0]
        rows = rates.shape[1]
        pieces.append(
            [jnp.broadcast_to(rates[h : h + 1], (SUBLANES, rows)) for h in range(lay.heads)]
        )
    return [
        cat([select_heads(lay, p, head_ids, shift) for p in pieces], 0)
        for shift in range(lay.heads)
    ]


def join_rows(lay, slabs):
    dim = lay.head_dim
    kind = BF16 if lay.packed else F32
    first = cat([s[:dim] for s in slabs], 1).astype(kind)
    second = cat([s[dim : 2 * dim] for s in slabs], 1).astype(kind)
    return first, second


def join_rates(lay, slabs):
    dim = lay.head_dim
    return cat([s[2 * dim : 2 * dim + 1] for s in slabs], 1)


def update_math(lay, slabs, weights):
    keys, values = join_rows(lay, slabs)
    rates = join_rates(lay, slabs)
    gate, up, down = (split(lay, w) for w in in_three(lay, weights))
    a = dot_left(gate, keys, NN)
    b = dot_left(up, keys, NN)
    u = dot_left(down, values, NN)
    _, silu, _, slope = gates(a)
    mu = -rates * u
    d_gate = dot_left(split(lay, mu * b * slope), keys, NT)
    d_up = dot_left(split(lay, mu * silu), keys, NT)
    d_down = dot_left(split(lay, -rates * (silu * b)), values, NT)
    return [d_gate, d_up, d_down], jnp.sum(rates, 1, keepdims=True)


def update_fn(lay, weights, *slabs):
    grads, total = update_math(lay, slabs, weights)
    return pack_all(lay, grads, total)


def update_near_fn(lay, weights, *slabs):
    grads, total = update_math(lay, slabs, weights)
    return [cat(grads, 0), jnp.broadcast_to(total, (SUBLANES, LANES))]


def update_rest_fn(lay, weights, before, total_before, *slabs):
    grads, total = update_math(lay, slabs, weights)
    grads = [g + b for g, b in zip(grads, in_three(lay, before))]
    return pack_halves(lay, grads, total + total_before[0:1, 0:1])


def norms(initial, moved):
    norm = jnp.sqrt(jnp.sum(initial * initial, 1, keepdims=True) + epsilon)
    inverse = lax.rsqrt(jnp.sum(moved * moved, 1, keepdims=True) + epsilon)
    return norm, inverse


def renormed(coefficient, body, total, initial):
    grad = body * (coefficient / total)
    moved = initial - grad
    norm, inverse = norms(initial, moved)
    return moved * (norm * inverse), grad, moved


def renorm_fn(lay, coefficient, *args):
    payloads, initial = args[:-1], args[-1]
    body, total = unpack(lay, functools.reduce(jnp.add, payloads))
    new, grad, moved = renormed(coefficient, body, total, initial)
    return [pack(lay, new, total), grad, moved]


def renorm_all_fn(lay, coefficient, *args):
    body, total = unpack_halves(lay, *args[:4])
    new, grad, moved = renormed(coefficient, body, total, args[4])
    return [new, grad, moved, jnp.broadcast_to(total, (SUBLANES, LANES))]


def apply_fn(lay, *args):
    if lay.packed:
        weights, slabs = in_three(lay, args[0]), args[1:]
    else:
        weights, slabs = unpack_all(lay, args[: lay.plane]), args[lay.plane :]
    queries, cotangents = join_rows(lay, slabs)
    gate, up, down = (split(lay, w) for w in weights)
    a = dot_left(gate, queries, NN)
    b = dot_left(up, queries, NN)
    u = dot_left(down, cotangents, NN)
    _, silu, _, slope = gates(a)
    da = split(lay, u * b * slope)
    db = split(lay, u * silu)
    h = split(lay, silu * b)
    d_gate = dot_left(da, queries, NT)
    d_up = dot_left(db, queries, NT)
    d_down = dot_left(h, cotangents, NT)
    outs = (pack_halves if lay.packed else pack_all)(
        lay, (d_gate, d_up, d_down), jnp.zeros((1, 1), F32)
    )
    turned = split(lay, cat([weights[0], weights[1]], 0).T)
    both = tuple(cat([x, y], 0) for x, y in zip(da, db))
    d_query = dot_both(turned, both, NN)
    rows = slabs[0].shape[1]
    cut = [d_query[:, i * rows : (i + 1) * rows] for i in range(len(slabs))]
    heads = lay.heads
    return outs + cut[:heads] + ([stack(cut[heads:])] if lay.cores > 1 else [])


def stack(parts):
    return cat([p[None] for p in parts], 0)


def renormed_back(coefficient, d_new, total, initial, grad, moved):
    norm, inverse = norms(initial, moved)
    dots = jnp.sum(d_new * moved, 1, keepdims=True)
    d_moved = d_new * (norm * inverse) - moved * (dots * norm * inverse * inverse * inverse)
    direct = d_moved + initial * (dots * inverse / norm)
    d_update = -d_moved
    part = jnp.sum(jnp.sum(d_update * grad, 1, keepdims=True), 0, keepdims=True)
    return d_update * (coefficient / total), -part / total, direct


def renorm_back_fn(lay, coefficient, *args):
    payloads = args[: lay.plane]
    total_payload, initial, grad, moved = args[lay.plane :]
    d_new, _ = unpack(lay, functools.reduce(jnp.add, payloads))
    _, total = unpack(lay, total_payload)
    move, d_total, direct = renormed_back(coefficient, d_new, total, initial, grad, moved)
    return [pack(lay, move, d_total), direct]


def renorm_back_all_fn(lay, coefficient, *args):
    d_new, _ = unpack_halves(lay, *args[:4])
    initial, grad, moved, total, places = args[4:]
    move, d_total, direct = renormed_back(
        coefficient, d_new, total[0:1, 0:1], initial, grad, moved
    )
    own = choose(in_slots(lay, in_three(lay, direct)), member_id(places))
    return [move, jnp.broadcast_to(d_total, (SUBLANES, LANES)), own]


def pull_math(lay, slabs, weights, moves, d_total):
    keys, values = join_rows(lay, slabs)
    rates = join_rates(lay, slabs)
    gate, up, down = (split(lay, w) for w in weights)
    gate_move, up_move, down_move = (split(lay, w) for w in moves)
    a = dot_left(gate, keys, NN)
    b = dot_left(up, keys, NN)
    u = dot_left(down, values, NN)
    ta = dot_left(gate_move, keys, NN)
    tb = dot_left(up_move, keys, NN)
    w = dot_left(down_move, values, NN)
    sig, silu, rest, slope = gates(a)
    bend = sig * rest * (2.0 + a * (rest - sig))
    hidden = silu * b
    hidden_dot = slope * ta * b + silu * tb
    rate_part = -jnp.sum(w * hidden + u * hidden_dot, 0, keepdims=True) + d_total
    mu = -rates
    wm, um = mu * w, mu * u
    ga = split(lay, wm * b * slope + um * (bend * ta * b + slope * tb))
    gb = split(lay, wm * silu + um * slope * ta)
    gta = split(lay, um * slope * b)
    gtb = split(lay, um * silu)
    mh = split(lay, mu * hidden)
    md = split(lay, mu * hidden_dot)
    grads = [dot_left(ga, keys, NT), dot_left(gb, keys, NT), dot_left(md, values, NT)]
    turned = split(lay, cat([weights[0], weights[1], moves[0], moves[1]], 0).T)
    d_key = dot_both(turned, tuple(cat(x, 0) for x in zip(ga, gb, gta, gtb)), NN)
    turned = split(lay, cat([moves[2], weights[2]], 0).T)
    d_value = dot_both(turned, tuple(cat(x, 0) for x in zip(mh, md)), NN)
    rows = slabs[0].shape[1]
    parts = []
    for i in range(len(slabs)):
        take = slice(i * rows, (i + 1) * rows)
        rate_rows = jnp.broadcast_to(rate_part[:, take], (SUBLANES, rows))
        parts.append(cat([d_key[:, take], d_value[:, take], rate_rows], 0))
    return grads, parts


def pull_fn(lay, *args):
    payloads, slabs, weights = args[: lay.plane], args[lay.plane : -1], args[-1]
    d_total = functools.reduce(jnp.add, [unpack(lay, p)[1] for p in payloads])
    grads, parts = pull_math(
        lay, slabs, in_three(lay, weights), unpack_all(lay, payloads), d_total
    )
    outs = pack_all(lay, grads, jnp.zeros((1, 1), F32))
    heads = lay.heads
    return outs + parts[:heads] + ([stack(parts[heads:])] if lay.cores > 1 else [])


def pull_other_fn(lay, *args):
    moves, d_total, weights, slabs = args[0], args[1], args[2], args[3:]
    grads, parts = pull_math(
        lay, slabs, in_three(lay, weights), in_three(lay, moves), d_total[0:1, 0:1]
    )
    return [stack(parts), cat(grads, 0)]


def pull_own_fn(lay, *args):
    moves, d_total, weights, before, places, slabs = *args[:5], args[5:]
    grads, parts = pull_math(
        lay, slabs, in_three(lay, weights), in_three(lay, moves), d_total[0:1, 0:1]
    )
    grads = [g + b for g, b in zip(grads, in_three(lay, before))]
    slots, member = in_slots(lay, grads), member_id(places)
    zero = jnp.zeros((1, 1), F32)
    return [pack(lay, choose(slots, member ^ r), zero) for r in range(lay.plane)] + parts


def add_two_fn(first, first_in, second, second_in):
    return [first + first_in, second + second_in]


def finish_fn(lay, count, *args):
    slabs, head_ids = args[:-1], args[-1]
    dim = lay.head_dim
    outs = []
    for n in range(count):
        pieces = [s[n * dim : (n + 1) * dim] for s in slabs]
        ordered = [
            select_heads(lay, pieces, lay.heads - head_ids, h) for h in range(lay.heads)
        ]
        outs.append(cat(ordered, 0).T.astype(BF16))
    if slabs[0].shape[0] > count * dim:
        pieces = [s[count * dim : count * dim + 1] for s in slabs]
        rows = [select_heads(lay, pieces, lay.heads - head_ids, h) for h in range(lay.heads)]
        outs.append(cat(rows, 0))
    return outs


def add_fn(*args):
    return [part + args[-1][i] for i, part in enumerate(args[:-1])]


def total_fn(lay, scale, *args):
    payloads, direct, places = args[: lay.plane], args[-2], args[-1]
    body, _ = unpack(lay, functools.reduce(jnp.add, payloads))
    final = (body + direct) / scale
    pieces = [final[m * lay.slot : (m + 1) * lay.slot] for m in range(3)]
    return [choose(pieces, places[0:1, t : t + 1]) for t in range(3)]


def place_fn(*args):
    pieces, places = args[:3], args[3]
    return [cat([choose(pieces, places[0:1, 3 + q : 4 + q]) for q in range(3)], 0)]


VMEM_LIMIT = 24 * 1024 * 1024


def run(lay, fn, args, always=False, deps=()):
    if not (lay.packed or always):
        return fn(*args)
    shapes = jax.eval_shape(fn, *args)
    deps = [x[: min(SUBLANES, x.shape[0])] for x in deps]
    count = len(args)

    def kernel(*refs):
        ins, outs = refs[:count], refs[count + len(deps) :]
        for ref, value in zip(outs, fn(*[r[...] for r in ins])):
            ref[...] = value

    vmem = pl.BlockSpec(memory_space=pltpu.VMEM)
    return pl.pallas_call(
        kernel,
        out_shape=[jax.ShapeDtypeStruct(s.shape, s.dtype) for s in shapes],
        in_specs=[vmem] * (count + len(deps)),
        out_specs=[vmem] * len(shapes),
        compiler_params=pltpu.CompilerParams(vmem_limit_bytes=VMEM_LIMIT),
    )(*args, *deps)


def tie(lay, arrays, deps):
    if not lay.packed:
        return arrays
    deps = [x[:SUBLANES] for x in deps]
    vmem = pl.BlockSpec(memory_space=pltpu.VMEM)
    return list(
        pl.pallas_call(
            lambda *refs: None,
            out_shape=[jax.ShapeDtypeStruct(a.shape, a.dtype) for a in arrays],
            in_specs=[vmem] * (len(arrays) + len(deps)),
            out_specs=[vmem] * len(arrays),
            input_output_aliases={i: i for i in range(len(arrays))},
            compiler_params=pltpu.CompilerParams(vmem_limit_bytes=VMEM_LIMIT),
        )(*arrays, *deps)
    )


def on_device(lay, queries, key_rows, value_rows, step_rates, fast_init, out_grad):
    head_dim, _ = fast_init.shape
    heads, slot, plane = lay.heads, lay.slot, lay.plane
    coefficient = step_size * math.sqrt(queries.shape[0] * lay.devices)
    view, patch = lax.axis_index("view"), lax.axis_index("patch")
    core = lax.rem(view, lay.cores)
    head = patch // lay.sub
    member = view // lay.cores * lay.sub + lax.rem(patch, lay.sub)
    me = view * lay.patches + patch
    head_ids = jnp.full((SUBLANES, LANES), head, jnp.int32)

    def send(x, perm):
        return lax.ppermute(x, AXES, perm)

    def over_heads(slabs):
        return [slabs[0]] + [send(slabs[t], lay.head_perm(t)) for t in range(1, heads)]

    def over_cores(slabs):
        return [send(x, lay.core_perm()) for x in slabs] if lay.cores > 1 else []

    def total_rows(parts):
        if lay.cores == 1:
            return parts
        return run(lay, add_fn, (*parts[:heads], send(parts[heads], lay.core_perm())))

    def back_home(slabs):
        return [slabs[0]] + [send(slabs[t], lay.head_perm(heads - t)) for t in range(1, heads)]

    def scatter(payloads):
        moved = [send(payloads[r], lay.scatter_perm(r)) for r in range(1, plane)]
        return [payloads[0]] + moved

    def gather(payload):
        return [payload] + [send(payload, lay.gather_perm(r)) for r in range(1, plane)]

    fn = functools.partial
    scale = math.sqrt(queries.shape[0] * lay.devices)
    kv = over_heads(
        run(
            lay,
            fn(spread_rows, lay, True),
            (key_rows, value_rows, step_rates.T, head_ids),
            always=True,
        )
    )
    qg = run(
        lay, fn(spread_rows, lay, False), (queries, out_grad, head_ids), always=True, deps=(kv[1],)
    )
    qg = over_heads(qg)
    kv = kv + over_cores(kv)

    owner_perms, table = owner_plan(lay)
    places = lax.dynamic_slice_in_dim(jnp.array(table, jnp.int32), me, 1, 0)
    first = head * lay.hidden + core * lay.half
    turned = []
    for m in range(3):
        part = lax.dynamic_slice_in_dim(fast_init, m * heads * lay.hidden + first, lay.half, 1)
        turned.append(part.T)
    if not lay.packed:
        order = jnp.stack([lay.target(member, r) for r in range(plane)])
        turned = [
            t.reshape(plane, slot, head_dim)[order].reshape(lay.half, head_dim) for t in turned
        ]
    weights = jnp.concatenate(turned, 0)

    def exchange(first, second):
        bits = [1 << i for i in range(plane.bit_length() - 1)]
        turned_bits = bits[1:] + bits[:1]
        for i, (one, two) in enumerate(zip(bits, turned_bits)):
            if i:
                first, second = run(lay, add_two_fn, (first, first_in, second, second_in))
            first_in = send(first, lay.flip_perm(one))
            second_in = send(second, lay.flip_perm(two))
        return first, first_in, second, second_in

    if lay.packed:
        near = (heads + 1) // 2
        before = run(lay, fn(update_near_fn, lay), (weights, *kv[:near]), deps=(places,))
        rest = run(lay, fn(update_rest_fn, lay), (weights, *before, *kv[near:]))
        sums = exchange(*rest)
        qg = tie(lay, qg, (sums[0],))
        qg = qg + over_cores(qg)
        renewed, grad, moved, total = run(
            lay, fn(renorm_all_fn, lay, coefficient), (*sums, weights)
        )
        applied = run(lay, fn(apply_fn, lay), (renewed, *qg))
        query_home = total_rows(applied[2:])
        sums = exchange(*applied[:2])
        move, d_total, direct = run(
            lay,
            fn(renorm_back_all_fn, lay, coefficient),
            (*sums, weights, grad, moved, total, places),
        )
        query_home = back_home(query_home)
        if lay.cores > 1:
            other, before = run(lay, fn(pull_other_fn, lay), (move, d_total, weights, *kv[heads:]))
        else:
            other, before = None, jnp.zeros_like(weights)
        pulled = run(
            lay, fn(pull_own_fn, lay), (move, d_total, weights, before, places, *kv[:heads])
        )
        pulled = [*pulled, other]
    else:
        own = jnp.concatenate([t[:slot] for t in turned], 0)
        sums = scatter(run(lay, fn(update_fn, lay), (weights, *kv)))
        payload, grad, moved = run(lay, fn(renorm_fn, lay, coefficient), (*sums, own))
        qg = qg + over_cores(qg)
        applied = run(lay, fn(apply_fn, lay), (*gather(payload), *qg))
        sums = scatter(applied[:plane])
        query_home = back_home(total_rows(applied[plane:]))
        d_payload, direct = run(
            lay, fn(renorm_back_fn, lay, coefficient), (*sums, payload, own, grad, moved)
        )
        pulled = run(lay, fn(pull_fn, lay), (*gather(d_payload), *kv, weights))
    key_home = total_rows(pulled[plane:])
    sums = scatter(pulled[:plane])
    pieces = run(lay, fn(total_fn, lay, scale), (*sums, direct, places), deps=tuple(key_home))
    key_home = back_home(key_home)
    (query_grad,) = run(
        lay, fn(finish_fn, lay, 1), (*query_home, head_ids), always=True, deps=tuple(pulled[:1])
    )
    arrived = [send(x, perm) for x, perm in zip(pieces, owner_perms)]
    (fast_grad,) = run(lay, place_fn, (*arrived, places))
    key_grad, value_grad, rate_grad = run(
        lay, fn(finish_fn, lay, 2), (*key_home, head_ids), always=True
    )
    return query_grad, key_grad, value_grad, rate_grad.T, fast_grad.T


def owner_plan(lay):
    rounds = lay.owner_rounds()
    table = [[0] * LANES for _ in range(lay.devices)]
    for t, chosen in enumerate(rounds):
        for source, owner, m, spot in chosen:
            table[source][t] = m
            table[owner][3 + spot] = t
            table[source][6] = lay.place(source)[0]
    return [[(i, o) for i, o, _, _ in chosen] for chosen in rounds], table


def solution(mesh):
    rows = P(AXES, None)

    def whole(queries, key_rows, value_rows, step_rates, fast_init, out_grad):
        heads = step_rates.shape[1]
        head_dim, columns = fast_init.shape
        lay = Layout(
            mesh.shape["view"], mesh.shape["patch"], heads, columns // (3 * heads), head_dim
        )

        def body(*args):
            return on_device(lay, *args)

        return jax.shard_map(
            body,
            mesh=mesh,
            in_specs=(rows, rows, rows, rows, P(), rows),
            out_specs=(rows, rows, rows, rows, P(None, AXES)),
            check_vma=False,
        )(queries, key_rows, value_rows, step_rates, fast_init, out_grad)

    return whole
```

```python
import functools
import math

import jax
import jax.numpy as jnp
from jax import lax
from jax.experimental import pallas as pl
from jax.experimental.pallas import tpu as pltpu
from jax.sharding import PartitionSpec as P


AXES = ("view", "patch")
step_size = 0.2
epsilon = 1e-06
F32, BF16 = jnp.float32, jnp.bfloat16
LANES, SUBLANES = 128, 8


class Layout:
    def __init__(self, views, patches, heads, hidden, head_dim):
        self.heads, self.head_dim, self.hidden = heads, head_dim, hidden
        self.cores = 2 if views % 2 == 0 else 1
        self.patches, self.devices = patches, views * patches
        self.sub = patches // heads
        self.plane = (views // self.cores) * self.sub
        self.half = hidden // self.cores
        self.slot = self.half // self.plane
        self.pow2 = self.plane & (self.plane - 1) == 0
        rows = 3 * self.slot
        self.packed = (
            head_dim == LANES + LANES // 2
            and rows % (2 * SUBLANES) == 0
            and (3 * self.half) % (4 * SUBLANES) == 0
            and self.pow2
            and self.plane > 1
        )

    def place(self, device):
        view, patch = divmod(device, self.patches)
        outer, core = divmod(view, self.cores)
        head, sub = divmod(patch, self.sub)
        return outer * self.sub + sub, core, head

    def device(self, member, core, head):
        outer, sub = divmod(member, self.sub)
        return (outer * self.cores + core) * self.patches + head * self.sub + sub

    def target(self, member, step):
        return member ^ step if self.pow2 else (member + step) % self.plane

    def origin(self, member, step):
        return member ^ step if self.pow2 else (member - step) % self.plane

    def perm(self, move):
        return [(i, self.device(*move(*self.place(i)))) for i in range(self.devices)]

    def core_perm(self):
        return self.perm(lambda j, c, h: (j, (c + 1) % self.cores, h))

    def other_head(self, head, step):
        return head ^ step if self.heads & (self.heads - 1) == 0 else (step - head) % self.heads

    def head_perm(self, step):
        return self.perm(lambda j, c, h: (j, c, self.other_head(h, step)))

    def scatter_perm(self, step):
        return self.perm(lambda j, c, h: (self.target(j, step), c, h))

    def gather_perm(self, step):
        return self.perm(lambda j, c, h: (self.origin(j, step), c, h))

    def flip_perm(self, bit):
        return self.perm(lambda j, c, h: (j ^ bit, c, h))

    def owner_rounds(self):
        count = self.devices
        edges = []
        for i in range(count):
            j, c, h = self.place(i)
            for m in range(3):
                piece = (m * self.heads + h) * self.cores * self.plane + c * self.plane + j
                edges.append((i, piece // 3, m, piece % 3))
        left, rounds = list(edges), []
        for _ in range(3):
            out_edges = [[] for _ in range(count)]
            for edge in left:
                out_edges[edge[0]].append(edge)
            match = {}

            def place_one(i, seen):
                for edge in out_edges[i]:
                    if edge[1] in seen:
                        continue
                    seen.add(edge[1])
                    if edge[1] not in match or place_one(match[edge[1]][0], seen):
                        match[edge[1]] = edge
                        return True
                return False

            for i in range(count):
                place_one(i, set())
            chosen = sorted(match.values())
            rounds.append(chosen)
            left = [edge for edge in left if edge not in match.values()]
        return rounds


def split(lay, x):
    if not lay.packed:
        return (x,)
    high = x.astype(BF16)
    return high, (x - high.astype(F32)).astype(BF16)


def dot(a, b, dims, precision=None):
    return lax.dot_general(
        a, b, (dims, ((), ())), precision=precision, preferred_element_type=F32
    )


NN, NT = ((1,), (0,)), ((1,), (1,))


def dot_left(parts, exact, dims):
    if len(parts) == 1:
        return dot(parts[0], exact, dims, lax.Precision.HIGH)
    return dot(parts[0], exact, dims) + dot(parts[1], exact, dims)


def dots_left(lefts, exact, dims):
    if len(lefts[0]) == 1:
        return [dot_left(left, exact, dims) for left in lefts]
    rows = lefts[0][0].shape[0]
    flat = dot(cat([part for left in lefts for part in left], 0), exact, dims)
    cuts = [flat[i * rows : (i + 1) * rows] for i in range(2 * len(lefts))]
    return [cuts[2 * i] + cuts[2 * i + 1] for i in range(len(lefts))]


def dot_both(a, b, dims):
    if len(a) == 1:
        return dot(a[0], b[0], dims, lax.Precision.HIGH)
    rows = a[0].shape[0]
    both = dot(cat(a, 0), b[0], dims)
    return both[:rows] + (dot(a[0], b[1], dims) + both[rows:])


def gates(act):
    sig = 1.0 / (1.0 + jnp.exp(-act))
    silu = act * sig
    rest = 1.0 - sig
    return sig, silu, rest, sig + silu * rest


def cat(parts, axis):
    return jnp.concatenate(parts, axis)


def pack(lay, body, extra):
    if not lay.packed:
        return cat([body, jnp.broadcast_to(extra, (SUBLANES, lay.head_dim))], 0)
    rows = body.shape[0]
    tail = body[:, LANES:]
    tail = cat([tail[: rows // 2], tail[rows // 2 :]], 1)
    return cat([body[:, :LANES], tail, jnp.broadcast_to(extra, (SUBLANES, LANES))], 0)


def unpack(lay, payload, rows=None):
    rows = 3 * lay.slot if rows is None else rows
    if not lay.packed:
        return payload[:rows], payload[rows : rows + 1, :1]
    tail = payload[rows : rows + rows // 2]
    half = LANES // 2
    tail = cat([tail[:, :half], tail[:, half:]], 0)
    return cat([payload[:rows], tail], 1), payload[rows + rows // 2 : rows + rows // 2 + 1, :1]


def pack_halves(lay, grads, extra):
    body = cat(grads, 0)
    rows = body.shape[0] // 2
    return [pack(lay, body[:rows], extra), pack(lay, body[rows:], extra)]


def unpack_halves(lay, first, first_in, second, second_in):
    rows = 3 * lay.half // 2
    top, extra = unpack(lay, first + first_in, rows)
    bottom, _ = unpack(lay, second + second_in, rows)
    return cat([top, bottom], 0), extra


def in_slots(lay, parts):
    slot = lay.slot
    return [cat([p[k * slot : (k + 1) * slot] for p in parts], 0) for k in range(lay.plane)]


def member_id(places):
    return places[0:1, 6:7]


def choose(pieces, index):
    result = pieces[0]
    for i in range(1, len(pieces)):
        result = jnp.where(index == i, pieces[i], result)
    return result


def in_three(lay, body):
    return [body[m * lay.half : (m + 1) * lay.half] for m in range(3)]


def pack_all(lay, grads, extra):
    outs = []
    for step in range(lay.plane):
        take = slice(step * lay.slot, (step + 1) * lay.slot)
        outs.append(pack(lay, cat([g[take] for g in grads], 0), extra))
    return outs


def unpack_all(lay, payloads):
    bodies = [unpack(lay, p)[0] for p in payloads]
    slot = lay.slot
    return [cat([b[m * slot : (m + 1) * slot] for b in bodies], 0) for m in range(3)]


def select_heads(lay, pieces, head_ids, step):
    own = head_ids[0:1, :]
    result = pieces[0]
    for i in range(1, lay.heads):
        result = jnp.where(own == lay.other_head(i, step), pieces[i], result)
    return result


def select_steps(lay, pieces, head_ids, head):
    own = head_ids[0:1, :]
    result = pieces[0]
    for step in range(1, lay.heads):
        result = jnp.where(own == lay.other_head(head, step), pieces[step], result)
    return result


def spread_rows(lay, with_rates, first, second, *rest):
    dim = lay.head_dim
    head_ids = rest[-1]
    turned = [x.astype(F32).T for x in (first, second)]
    pieces = [[t[h * dim : (h + 1) * dim] for h in range(lay.heads)] for t in turned]
    if with_rates:
        rates = rest[0]
        rows = rates.shape[1]
        pieces.append(
            [jnp.broadcast_to(rates[h : h + 1], (SUBLANES, rows)) for h in range(lay.heads)]
        )
    return [
        cat([select_heads(lay, p, head_ids, shift) for p in pieces], 0)
        for shift in range(lay.heads)
    ]


def join_rows(lay, slabs):
    dim = lay.head_dim
    kind = BF16 if lay.packed else F32
    first = cat([s[:dim] for s in slabs], 1).astype(kind)
    second = cat([s[dim : 2 * dim] for s in slabs], 1).astype(kind)
    return first, second


def join_rates(lay, slabs):
    dim = lay.head_dim
    return cat([s[2 * dim : 2 * dim + 1] for s in slabs], 1)


def update_math(lay, slabs, weights):
    keys, values = join_rows(lay, slabs)
    rates = join_rates(lay, slabs)
    gate, up, down = (split(lay, w) for w in in_three(lay, weights))
    a, b = dots_left((gate, up), keys, NN)
    (u,) = dots_left((down,), values, NN)
    _, silu, _, slope = gates(a)
    mu = -rates * u
    d_gate, d_up = dots_left(
        (split(lay, mu * b * slope), split(lay, mu * silu)), keys, NT
    )
    (d_down,) = dots_left((split(lay, -rates * (silu * b)),), values, NT)
    return [d_gate, d_up, d_down], jnp.sum(rates, 1, keepdims=True)


def update_fn(lay, weights, *slabs):
    grads, total = update_math(lay, slabs, weights)
    return pack_all(lay, grads, total)


def update_near_fn(lay, weights, *slabs):
    grads, total = update_math(lay, slabs, weights)
    return [cat(grads, 0), jnp.broadcast_to(total, (SUBLANES, LANES))]


def update_rest_fn(lay, weights, before, total_before, *slabs):
    grads, total = update_math(lay, slabs, weights)
    grads = [g + b for g, b in zip(grads, in_three(lay, before))]
    return pack_halves(lay, grads, total + total_before[0:1, 0:1])


def norms(initial, moved):
    norm = jnp.sqrt(jnp.sum(initial * initial, 1, keepdims=True) + epsilon)
    inverse = lax.rsqrt(jnp.sum(moved * moved, 1, keepdims=True) + epsilon)
    return norm, inverse


def renormed(coefficient, body, total, initial):
    grad = body * (coefficient / total)
    moved = initial - grad
    norm, inverse = norms(initial, moved)
    return moved * (norm * inverse), grad, moved


def renorm_fn(lay, coefficient, *args):
    payloads, initial = args[:-1], args[-1]
    body, total = unpack(lay, functools.reduce(jnp.add, payloads))
    new, grad, moved = renormed(coefficient, body, total, initial)
    return [pack(lay, new, total), grad, moved]


def renorm_all_fn(lay, coefficient, *args):
    body, total = unpack_halves(lay, *args[:4])
    new, grad, moved = renormed(coefficient, body, total, args[4])
    return [new, grad, moved, jnp.broadcast_to(total, (SUBLANES, LANES))]


def apply_fn(lay, *args):
    if lay.packed:
        weights, slabs = in_three(lay, args[0]), args[1:]
    else:
        weights, slabs = unpack_all(lay, args[: lay.plane]), args[lay.plane :]
    queries, cotangents = join_rows(lay, slabs)
    gate, up, down = (split(lay, w) for w in weights)
    a, b = dots_left((gate, up), queries, NN)
    (u,) = dots_left((down,), cotangents, NN)
    _, silu, _, slope = gates(a)
    da = split(lay, u * b * slope)
    db = split(lay, u * silu)
    h = split(lay, silu * b)
    d_gate, d_up = dots_left((da, db), queries, NT)
    (d_down,) = dots_left((h,), cotangents, NT)
    outs = (pack_halves if lay.packed else pack_all)(
        lay, (d_gate, d_up, d_down), jnp.zeros((1, 1), F32)
    )
    turned = split(lay, cat([weights[0], weights[1]], 0).T)
    both = tuple(cat([x, y], 0) for x, y in zip(da, db))
    d_query = dot_both(turned, both, NN)
    rows = slabs[0].shape[1]
    cut = [d_query[:, i * rows : (i + 1) * rows] for i in range(len(slabs))]
    heads = lay.heads
    return outs + cut[:heads] + ([stack(cut[heads:])] if lay.cores > 1 else [])


def stack(parts):
    return cat([p[None] for p in parts], 0)


def renormed_back(coefficient, d_new, total, initial, grad, moved):
    norm, inverse = norms(initial, moved)
    dots = jnp.sum(d_new * moved, 1, keepdims=True)
    d_moved = d_new * (norm * inverse) - moved * (dots * norm * inverse * inverse * inverse)
    direct = d_moved + initial * (dots * inverse / norm)
    d_update = -d_moved
    part = jnp.sum(jnp.sum(d_update * grad, 1, keepdims=True), 0, keepdims=True)
    return d_update * (coefficient / total), -part / total, direct


def renorm_back_fn(lay, coefficient, *args):
    payloads = args[: lay.plane]
    total_payload, initial, grad, moved = args[lay.plane :]
    d_new, _ = unpack(lay, functools.reduce(jnp.add, payloads))
    _, total = unpack(lay, total_payload)
    move, d_total, direct = renormed_back(coefficient, d_new, total, initial, grad, moved)
    return [pack(lay, move, d_total), direct]


def renorm_back_all_fn(lay, coefficient, *args):
    d_new, _ = unpack_halves(lay, *args[:4])
    initial, grad, moved, total, places = args[4:]
    move, d_total, direct = renormed_back(
        coefficient, d_new, total[0:1, 0:1], initial, grad, moved
    )
    own = choose(in_slots(lay, in_three(lay, direct)), member_id(places))
    return [move, jnp.broadcast_to(d_total, (SUBLANES, LANES)), own]


def pull_math(lay, slabs, weights, moves, d_total):
    keys, values = join_rows(lay, slabs)
    rates = join_rates(lay, slabs)
    gate, up, down = (split(lay, w) for w in weights)
    gate_move, up_move, down_move = (split(lay, w) for w in moves)
    a, b, ta, tb = dots_left((gate, up, gate_move, up_move), keys, NN)
    u, w = dots_left((down, down_move), values, NN)
    sig, silu, rest, slope = gates(a)
    bend = sig * rest * (2.0 + a * (rest - sig))
    hidden = silu * b
    hidden_dot = slope * ta * b + silu * tb
    rate_part = -jnp.sum(w * hidden + u * hidden_dot, 0, keepdims=True) + d_total
    mu = -rates
    wm, um = mu * w, mu * u
    ga = split(lay, wm * b * slope + um * (bend * ta * b + slope * tb))
    gb = split(lay, wm * silu + um * slope * ta)
    gta = split(lay, um * slope * b)
    gtb = split(lay, um * silu)
    mh = split(lay, mu * hidden)
    md = split(lay, mu * hidden_dot)
    grads = dots_left((ga, gb), keys, NT) + dots_left((md,), values, NT)
    turned = split(lay, cat([weights[0], weights[1], moves[0], moves[1]], 0).T)
    d_key = dot_both(turned, tuple(cat(x, 0) for x in zip(ga, gb, gta, gtb)), NN)
    turned = split(lay, cat([moves[2], weights[2]], 0).T)
    d_value = dot_both(turned, tuple(cat(x, 0) for x in zip(mh, md)), NN)
    rows = slabs[0].shape[1]
    parts = []
    for i in range(len(slabs)):
        take = slice(i * rows, (i + 1) * rows)
        rate_rows = jnp.broadcast_to(rate_part[:, take], (SUBLANES, rows))
        parts.append(cat([d_key[:, take], d_value[:, take], rate_rows], 0))
    return grads, parts


def pull_fn(lay, *args):
    payloads, slabs, weights = args[: lay.plane], args[lay.plane : -1], args[-1]
    d_total = functools.reduce(jnp.add, [unpack(lay, p)[1] for p in payloads])
    grads, parts = pull_math(
        lay, slabs, in_three(lay, weights), unpack_all(lay, payloads), d_total
    )
    outs = pack_all(lay, grads, jnp.zeros((1, 1), F32))
    heads = lay.heads
    return outs + parts[:heads] + ([stack(parts[heads:])] if lay.cores > 1 else [])


def pull_other_fn(lay, *args):
    moves, d_total, weights, slabs = args[0], args[1], args[2], args[3:]
    grads, parts = pull_math(
        lay, slabs, in_three(lay, weights), in_three(lay, moves), d_total[0:1, 0:1]
    )
    return [stack(parts), cat(grads, 0)]


def pull_own_fn(lay, *args):
    moves, d_total, weights, before, places, slabs = *args[:5], args[5:]
    grads, parts = pull_math(
        lay, slabs, in_three(lay, weights), in_three(lay, moves), d_total[0:1, 0:1]
    )
    grads = [g + b for g, b in zip(grads, in_three(lay, before))]
    slots, member = in_slots(lay, grads), member_id(places)
    zero = jnp.zeros((1, 1), F32)
    return [pack(lay, choose(slots, member ^ r), zero) for r in range(lay.plane)] + parts


def add_two_fn(first, first_in, second, second_in):
    return [first + first_in, second + second_in]


def finish_fn(lay, count, *args):
    slabs, head_ids = args[:-1], args[-1]
    dim = lay.head_dim
    outs = []
    for n in range(count):
        pieces = [s[n * dim : (n + 1) * dim] for s in slabs]
        ordered = [
            select_steps(lay, pieces, head_ids, h) for h in range(lay.heads)
        ]
        outs.append(cat(ordered, 0).T.astype(BF16))
    if slabs[0].shape[0] > count * dim:
        pieces = [s[count * dim : count * dim + 1] for s in slabs]
        rows = [select_steps(lay, pieces, head_ids, h) for h in range(lay.heads)]
        outs.append(cat(rows, 0))
    return outs


def add_fn(*args):
    return [part + args[-1][i] for i, part in enumerate(args[:-1])]


def total_fn(lay, scale, *args):
    payloads, direct, places = args[: lay.plane], args[-2], args[-1]
    body, _ = unpack(lay, functools.reduce(jnp.add, payloads))
    final = (body + direct) / scale
    pieces = [final[m * lay.slot : (m + 1) * lay.slot] for m in range(3)]
    return [choose(pieces, places[0:1, t : t + 1]) for t in range(3)]


def place_fn(*args):
    pieces, places = args[:3], args[3]
    return [cat([choose(pieces, places[0:1, 3 + q : 4 + q]) for q in range(3)], 0)]


VMEM_LIMIT = 24 * 1024 * 1024


def run(lay, fn, args, always=False, deps=()):
    if not (lay.packed or always):
        return fn(*args)
    shapes = jax.eval_shape(fn, *args)
    deps = [x[: min(SUBLANES, x.shape[0])] for x in deps]
    count = len(args)

    def kernel(*refs):
        ins, outs = refs[:count], refs[count + len(deps) :]
        for ref, value in zip(outs, fn(*[r[...] for r in ins])):
            ref[...] = value

    vmem = pl.BlockSpec(memory_space=pltpu.VMEM)
    return pl.pallas_call(
        kernel,
        out_shape=[jax.ShapeDtypeStruct(s.shape, s.dtype) for s in shapes],
        in_specs=[vmem] * (count + len(deps)),
        out_specs=[vmem] * len(shapes),
        compiler_params=pltpu.CompilerParams(vmem_limit_bytes=VMEM_LIMIT),
    )(*args, *deps)


def tie(lay, arrays, deps):
    if not lay.packed:
        return arrays
    deps = [x[:SUBLANES] for x in deps]
    vmem = pl.BlockSpec(memory_space=pltpu.VMEM)
    return list(
        pl.pallas_call(
            lambda *refs: None,
            out_shape=[jax.ShapeDtypeStruct(a.shape, a.dtype) for a in arrays],
            in_specs=[vmem] * (len(arrays) + len(deps)),
            out_specs=[vmem] * len(arrays),
            input_output_aliases={i: i for i in range(len(arrays))},
            compiler_params=pltpu.CompilerParams(vmem_limit_bytes=VMEM_LIMIT),
        )(*arrays, *deps)
    )


def on_device(lay, queries, key_rows, value_rows, step_rates, fast_init, out_grad):
    head_dim, _ = fast_init.shape
    heads, slot, plane = lay.heads, lay.slot, lay.plane
    coefficient = step_size * math.sqrt(queries.shape[0] * lay.devices)
    view, patch = lax.axis_index("view"), lax.axis_index("patch")
    core = lax.rem(view, lay.cores)
    head = patch // lay.sub
    member = view // lay.cores * lay.sub + lax.rem(patch, lay.sub)
    me = view * lay.patches + patch
    head_ids = jnp.full((SUBLANES, LANES), head, jnp.int32)

    def send(x, perm):
        return lax.ppermute(x, AXES, perm)

    def over_heads(slabs, hold=()):
        close = [send(slabs[t], lay.head_perm(t)) for t in range(1, min(2, heads))]
        away = slabs[2:]
        if hold:
            away = tie(lay, away, hold)
        away = [send(x, lay.head_perm(t)) for t, x in enumerate(away, 2)]
        return [slabs[0]] + close + away

    def over_cores(slabs):
        return [send(x, lay.core_perm()) for x in slabs] if lay.cores > 1 else []

    def total_rows(parts):
        if lay.cores == 1:
            return parts
        return run(lay, add_fn, (*parts[:heads], send(parts[heads], lay.core_perm())))

    def back_home(slabs):
        return [slabs[0]] + [send(slabs[t], lay.head_perm(t)) for t in range(1, heads)]

    def scatter(payloads):
        moved = [send(payloads[r], lay.scatter_perm(r)) for r in range(1, plane)]
        return [payloads[0]] + moved

    def gather(payload):
        return [payload] + [send(payload, lay.gather_perm(r)) for r in range(1, plane)]

    fn = functools.partial
    scale = math.sqrt(queries.shape[0] * lay.devices)
    kv = run(
        lay, fn(spread_rows, lay, True), (key_rows, value_rows, step_rates.T, head_ids), always=True
    )
    kv = over_heads(kv)
    qg = run(
        lay, fn(spread_rows, lay, False), (queries, out_grad, head_ids), always=True, deps=(kv[1],)
    )
    qg = over_heads(qg, tuple(kv[2:]))
    kv = kv + over_cores(kv)

    owner_perms, table = owner_plan(lay)
    places = lax.dynamic_slice_in_dim(jnp.array(table, jnp.int32), me, 1, 0)
    first = head * lay.hidden + core * lay.half
    turned = []
    for m in range(3):
        part = lax.dynamic_slice_in_dim(fast_init, m * heads * lay.hidden + first, lay.half, 1)
        turned.append(part.T)
    if not lay.packed:
        order = jnp.stack([lay.target(member, r) for r in range(plane)])
        turned = [
            t.reshape(plane, slot, head_dim)[order].reshape(lay.half, head_dim) for t in turned
        ]
    weights = jnp.concatenate(turned, 0)

    def exchange(first, second):
        bits = [1 << i for i in range(plane.bit_length() - 1)]
        turned_bits = bits[1:] + bits[:1]
        for i, (one, two) in enumerate(zip(bits, turned_bits)):
            if i:
                first, second = run(lay, add_two_fn, (first, first_in, second, second_in))
            first_in = send(first, lay.flip_perm(one))
            second_in = send(second, lay.flip_perm(two))
        return first, first_in, second, second_in

    if lay.packed:
        near = (heads + 1) // 2
        before = run(lay, fn(update_near_fn, lay), (weights, *kv[:near]), deps=(places,))
        rest = run(lay, fn(update_rest_fn, lay), (weights, *before, *kv[near:]))
        sums = exchange(*rest)
        qg = tie(lay, qg, (sums[0],))
        qg = qg + over_cores(qg)
        renewed, grad, moved, total = run(
            lay, fn(renorm_all_fn, lay, coefficient), (*sums, weights)
        )
        applied = run(lay, fn(apply_fn, lay), (renewed, *qg))
        query_home = total_rows(applied[2:])
        sums = exchange(*applied[:2])
        move, d_total, direct = run(
            lay,
            fn(renorm_back_all_fn, lay, coefficient),
            (*sums, weights, grad, moved, total, places),
        )
        query_home = back_home(query_home)
        if lay.cores > 1:
            other, before = run(lay, fn(pull_other_fn, lay), (move, d_total, weights, *kv[heads:]))
        else:
            other, before = None, jnp.zeros_like(weights)
        pulled = run(
            lay, fn(pull_own_fn, lay), (move, d_total, weights, before, places, *kv[:heads])
        )
        pulled = [*pulled, other]
    else:
        own = jnp.concatenate([t[:slot] for t in turned], 0)
        sums = scatter(run(lay, fn(update_fn, lay), (weights, *kv)))
        payload, grad, moved = run(lay, fn(renorm_fn, lay, coefficient), (*sums, own))
        qg = qg + over_cores(qg)
        applied = run(lay, fn(apply_fn, lay), (*gather(payload), *qg))
        sums = scatter(applied[:plane])
        query_home = back_home(total_rows(applied[plane:]))
        d_payload, direct = run(
            lay, fn(renorm_back_fn, lay, coefficient), (*sums, payload, own, grad, moved)
        )
        pulled = run(lay, fn(pull_fn, lay), (*gather(d_payload), *kv, weights))
    key_home = total_rows(pulled[plane:])
    sums = scatter(pulled[:plane])
    pieces = run(lay, fn(total_fn, lay, scale), (*sums, direct, places), deps=tuple(key_home))
    key_home = back_home(key_home)
    (query_grad,) = run(
        lay, fn(finish_fn, lay, 1), (*query_home, head_ids), always=True, deps=tuple(pulled[:1])
    )
    arrived = [send(x, perm) for x, perm in zip(pieces, owner_perms)]
    (fast_grad,) = run(lay, place_fn, (*arrived, places))
    key_grad, value_grad, rate_grad = run(
        lay, fn(finish_fn, lay, 2), (*key_home, head_ids), always=True
    )
    return query_grad, key_grad, value_grad, rate_grad.T, fast_grad.T


def owner_plan(lay):
    rounds = lay.owner_rounds()
    table = [[0] * LANES for _ in range(lay.devices)]
    for t, chosen in enumerate(rounds):
        for source, owner, m, spot in chosen:
            table[source][t] = m
            table[owner][3 + spot] = t
            table[source][6] = lay.place(source)[0]
    return [[(i, o) for i, o, _, _ in chosen] for chosen in rounds], table


def solution(mesh):
    rows = P(AXES, None)

    def whole(queries, key_rows, value_rows, step_rates, fast_init, out_grad):
        heads = step_rates.shape[1]
        head_dim, columns = fast_init.shape
        lay = Layout(
            mesh.shape["view"], mesh.shape["patch"], heads, columns // (3 * heads), head_dim
        )

        def body(*args):
            return on_device(lay, *args)

        return jax.shard_map(
            body,
            mesh=mesh,
            in_specs=(rows, rows, rows, rows, P(), rows),
            out_specs=(rows, rows, rows, rows, P(None, AXES)),
            check_vma=False,
        )(queries, key_rows, value_rows, step_rates, fast_init, out_grad)

    return whole
```

```python
import functools
import math

import jax
import jax.numpy as jnp
from jax import lax
from jax.experimental import pallas as pl
from jax.experimental.pallas import tpu as pltpu
from jax.sharding import PartitionSpec as P


AXES = ("view", "patch")
step_size = 0.2
epsilon = 1e-06
F32, BF16 = jnp.float32, jnp.bfloat16
LANES, SUBLANES = 128, 8


class Layout:
    def __init__(self, views, patches, heads, hidden, head_dim):
        self.heads, self.head_dim, self.hidden = heads, head_dim, hidden
        self.cores = 2 if views % 2 == 0 else 1
        self.patches, self.devices = patches, views * patches
        self.sub = patches // heads
        self.plane = (views // self.cores) * self.sub
        self.half = hidden // self.cores
        self.slot = self.half // self.plane
        self.pow2 = self.plane & (self.plane - 1) == 0
        rows = 3 * self.slot
        self.packed = (
            head_dim == LANES + LANES // 2
            and rows % (2 * SUBLANES) == 0
            and (3 * self.half) % (2 * SUBLANES) == 0
            and self.pow2
            and self.plane > 1
            and self.cores == 2
            and heads > 2
        )

    def place(self, device):
        view, patch = divmod(device, self.patches)
        outer, core = divmod(view, self.cores)
        head, sub = divmod(patch, self.sub)
        return outer * self.sub + sub, core, head

    def device(self, member, core, head):
        outer, sub = divmod(member, self.sub)
        return (outer * self.cores + core) * self.patches + head * self.sub + sub

    def target(self, member, step):
        return member ^ step if self.pow2 else (member + step) % self.plane

    def origin(self, member, step):
        return member ^ step if self.pow2 else (member - step) % self.plane

    def perm(self, move):
        return [(i, self.device(*move(*self.place(i)))) for i in range(self.devices)]

    def core_perm(self):
        return self.perm(lambda j, c, h: (j, (c + 1) % self.cores, h))

    def other_head(self, head, step):
        return head ^ step if self.heads & (self.heads - 1) == 0 else (step - head) % self.heads

    def head_perm(self, step):
        return self.perm(lambda j, c, h: (j, c, self.other_head(h, step)))

    def scatter_perm(self, step):
        return self.perm(lambda j, c, h: (self.target(j, step), c, h))

    def gather_perm(self, step):
        return self.perm(lambda j, c, h: (self.origin(j, step), c, h))

    def flip_perm(self, bit):
        return self.perm(lambda j, c, h: (j ^ bit, c, h))

    def owner_rounds(self):
        count = self.devices
        edges = []
        for i in range(count):
            j, c, h = self.place(i)
            for m in range(3):
                piece = (m * self.heads + h) * self.cores * self.plane + c * self.plane + j
                edges.append((i, piece // 3, m, piece % 3))
        left, rounds = list(edges), []
        for _ in range(3):
            out_edges = [[] for _ in range(count)]
            for edge in left:
                out_edges[edge[0]].append(edge)
            match = {}

            def place_one(i, seen):
                for edge in out_edges[i]:
                    if edge[1] in seen:
                        continue
                    seen.add(edge[1])
                    if edge[1] not in match or place_one(match[edge[1]][0], seen):
                        match[edge[1]] = edge
                        return True
                return False

            for i in range(count):
                place_one(i, set())
            chosen = sorted(match.values())
            rounds.append(chosen)
            left = [edge for edge in left if edge not in match.values()]
        return rounds


def split(lay, x):
    if not lay.packed:
        return (x,)
    high = x.astype(BF16)
    return high, (x - high.astype(F32)).astype(BF16)


def dot(a, b, dims, precision=None):
    return lax.dot_general(
        a, b, (dims, ((), ())), precision=precision, preferred_element_type=F32
    )


NN, NT = ((1,), (0,)), ((1,), (1,))


def dot_left(parts, exact, dims):
    if len(parts) == 1:
        return dot(parts[0], exact, dims, lax.Precision.HIGH)
    return dot(parts[0], exact, dims) + dot(parts[1], exact, dims)


def dots_left(lefts, exact, dims):
    if len(lefts[0]) == 1:
        return [dot_left(left, exact, dims) for left in lefts]
    rows = lefts[0][0].shape[0]
    flat = dot(cat([part for left in lefts for part in left], 0), exact, dims)
    cuts = [flat[i * rows : (i + 1) * rows] for i in range(2 * len(lefts))]
    return [cuts[2 * i] + cuts[2 * i + 1] for i in range(len(lefts))]


def dot_both(a, b, dims):
    if len(a) == 1:
        return dot(a[0], b[0], dims, lax.Precision.HIGH)
    rows = a[0].shape[0]
    both = dot(cat(a, 0), b[0], dims)
    return both[:rows] + (dot(a[0], b[1], dims) + both[rows:])


def gates(act):
    sig = 1.0 / (1.0 + jnp.exp(-act))
    silu = act * sig
    rest = 1.0 - sig
    return sig, silu, rest, sig + silu * rest


def cat(parts, axis):
    return jnp.concatenate(parts, axis)


def pack(lay, body, extra):
    if not lay.packed:
        return cat([body, jnp.broadcast_to(extra, (SUBLANES, lay.head_dim))], 0)
    rows = body.shape[0]
    tail = body[:, LANES:]
    tail = cat([tail[: rows // 2], tail[rows // 2 :]], 1)
    return cat([body[:, :LANES], tail, jnp.broadcast_to(extra, (SUBLANES, LANES))], 0)


def unpack(lay, payload, rows=None):
    rows = 3 * lay.slot if rows is None else rows
    if not lay.packed:
        return payload[:rows], payload[rows : rows + 1, :1]
    tail = payload[rows : rows + rows // 2]
    half = LANES // 2
    tail = cat([tail[:, :half], tail[:, half:]], 0)
    return cat([payload[:rows], tail], 1), payload[rows + rows // 2 : rows + rows // 2 + 1, :1]


def wide_rows(lay):
    step = 2 * SUBLANES
    total = 3 * lay.half
    return total - total * 5 // 12 // step * step


def pack_parts(lay, grads, extra):
    body, rows = cat(grads, 0), wide_rows(lay)
    return [pack(lay, body[:rows], extra), pack(lay, body[rows:], extra)]


def unpack_parts(lay, first, first_in, second, second_in):
    rows = wide_rows(lay)
    top, extra = unpack(lay, first + first_in, rows)
    bottom, _ = unpack(lay, second + second_in, 3 * lay.half - rows)
    return cat([top, bottom], 0), extra


def in_slots(lay, parts):
    slot = lay.slot
    return [cat([p[k * slot : (k + 1) * slot] for p in parts], 0) for k in range(lay.plane)]


def member_id(places):
    return places[0:1, 6:7]


def choose(pieces, index):
    result = pieces[0]
    for i in range(1, len(pieces)):
        result = jnp.where(index == i, pieces[i], result)
    return result


def in_three(lay, body):
    return [body[m * lay.half : (m + 1) * lay.half] for m in range(3)]


def pack_all(lay, grads, extra):
    outs = []
    for step in range(lay.plane):
        take = slice(step * lay.slot, (step + 1) * lay.slot)
        outs.append(pack(lay, cat([g[take] for g in grads], 0), extra))
    return outs


def unpack_all(lay, payloads):
    bodies = [unpack(lay, p)[0] for p in payloads]
    slot = lay.slot
    return [cat([b[m * slot : (m + 1) * slot] for b in bodies], 0) for m in range(3)]


def select_heads(lay, pieces, head_ids, step):
    own = head_ids[0:1, :]
    result = pieces[0]
    for i in range(1, lay.heads):
        result = jnp.where(own == lay.other_head(i, step), pieces[i], result)
    return result


def select_steps(lay, pieces, head_ids, head):
    own = head_ids[0:1, :]
    result = pieces[0]
    for step in range(1, lay.heads):
        result = jnp.where(own == lay.other_head(head, step), pieces[step], result)
    return result


def spread_rows(lay, with_rates, first, second, *rest):
    dim = lay.head_dim
    head_ids = rest[-1]
    turned = [x.astype(F32).T for x in (first, second)]
    pieces = [[t[h * dim : (h + 1) * dim] for h in range(lay.heads)] for t in turned]
    if with_rates:
        rates = rest[0]
        rows = rates.shape[1]
        pieces.append(
            [jnp.broadcast_to(rates[h : h + 1], (SUBLANES, rows)) for h in range(lay.heads)]
        )
    return [
        cat([select_heads(lay, p, head_ids, shift) for p in pieces], 0)
        for shift in range(lay.heads)
    ]


def join_rows(lay, slabs):
    dim = lay.head_dim
    kind = BF16 if lay.packed else F32
    first = cat([s[:dim] for s in slabs], 1).astype(kind)
    second = cat([s[dim : 2 * dim] for s in slabs], 1).astype(kind)
    return first, second


def join_rates(lay, slabs):
    dim = lay.head_dim
    return cat([s[2 * dim : 2 * dim + 1] for s in slabs], 1)


def update_math(lay, slabs, weights):
    keys, values = join_rows(lay, slabs)
    rates = join_rates(lay, slabs)
    gate, up, down = (split(lay, w) for w in in_three(lay, weights))
    a, b = dots_left((gate, up), keys, NN)
    (u,) = dots_left((down,), values, NN)
    _, silu, _, slope = gates(a)
    mu = -rates * u
    d_gate, d_up = dots_left(
        (split(lay, mu * b * slope), split(lay, mu * silu)), keys, NT
    )
    (d_down,) = dots_left((split(lay, -rates * (silu * b)),), values, NT)
    return [d_gate, d_up, d_down], jnp.sum(rates, 1, keepdims=True)


def update_fn(lay, weights, *slabs):
    grads, total = update_math(lay, slabs, weights)
    return pack_all(lay, grads, total)


def update_near_fn(lay, weights, *slabs):
    grads, total = update_math(lay, slabs, weights)
    return [cat(grads, 0), jnp.broadcast_to(total, (SUBLANES, LANES))]


def update_rest_fn(lay, weights, before, total_before, *slabs):
    grads, total = update_math(lay, slabs, weights)
    grads = [g + b for g, b in zip(grads, in_three(lay, before))]
    return pack_parts(lay, grads, total + total_before[0:1, 0:1])


def norms(initial, moved):
    norm = jnp.sqrt(jnp.sum(initial * initial, 1, keepdims=True) + epsilon)
    inverse = lax.rsqrt(jnp.sum(moved * moved, 1, keepdims=True) + epsilon)
    return norm, inverse


def renormed(coefficient, body, total, initial):
    grad = body * (coefficient / total)
    moved = initial - grad
    norm, inverse = norms(initial, moved)
    return moved * (norm * inverse), grad, moved


def renorm_fn(lay, coefficient, *args):
    payloads, initial = args[:-1], args[-1]
    body, total = unpack(lay, functools.reduce(jnp.add, payloads))
    new, grad, moved = renormed(coefficient, body, total, initial)
    return [pack(lay, new, total), grad, moved]


def renorm_all_fn(lay, coefficient, *args):
    body, total = unpack_parts(lay, *args[:4])
    new, grad, moved = renormed(coefficient, body, total, args[4])
    return [new, grad, moved, jnp.broadcast_to(total, (SUBLANES, LANES))]


def apply_math(lay, slabs, weights):
    queries, cotangents = join_rows(lay, slabs)
    gate, up, down = (split(lay, w) for w in weights)
    a, b = dots_left((gate, up), queries, NN)
    (u,) = dots_left((down,), cotangents, NN)
    _, silu, _, slope = gates(a)
    da = split(lay, u * b * slope)
    db = split(lay, u * silu)
    h = split(lay, silu * b)
    grads = dots_left((da, db), queries, NT) + dots_left((h,), cotangents, NT)
    turned = split(lay, cat([weights[0], weights[1]], 0).T)
    both = tuple(cat([x, y], 0) for x, y in zip(da, db))
    d_query = dot_both(turned, both, NN)
    rows = slabs[0].shape[1]
    return grads, [d_query[:, i * rows : (i + 1) * rows] for i in range(len(slabs))]


def apply_fn(lay, *args):
    weights, slabs = unpack_all(lay, args[: lay.plane]), args[lay.plane :]
    grads, parts = apply_math(lay, slabs, weights)
    outs = pack_all(lay, grads, jnp.zeros((1, 1), F32))
    heads = lay.heads
    return outs + parts[:heads] + ([stack(parts[heads:])] if lay.cores > 1 else [])


def apply_near_fn(lay, count, new, *slabs):
    grads, parts = apply_math(lay, slabs, in_three(lay, new))
    return [cat(grads, 0), *parts[:count], stack(parts[count:])]


def apply_far_fn(lay, count, new, before, *slabs):
    grads, parts = apply_math(lay, slabs, in_three(lay, new))
    grads = [g + b for g, b in zip(grads, in_three(lay, before))]
    outs = pack_parts(lay, grads, jnp.zeros((1, 1), F32))
    return outs + [*parts[:count], stack(parts[count:])]


def stack(parts):
    return cat([p[None] for p in parts], 0)


def renormed_back(coefficient, d_new, total, initial, grad, moved):
    norm, inverse = norms(initial, moved)
    dots = jnp.sum(d_new * moved, 1, keepdims=True)
    d_moved = d_new * (norm * inverse) - moved * (dots * norm * inverse * inverse * inverse)
    direct = d_moved + initial * (dots * inverse / norm)
    d_update = -d_moved
    part = jnp.sum(jnp.sum(d_update * grad, 1, keepdims=True), 0, keepdims=True)
    return d_update * (coefficient / total), -part / total, direct


def renorm_back_fn(lay, coefficient, *args):
    payloads = args[: lay.plane]
    total_payload, initial, grad, moved = args[lay.plane :]
    d_new, _ = unpack(lay, functools.reduce(jnp.add, payloads))
    _, total = unpack(lay, total_payload)
    move, d_total, direct = renormed_back(coefficient, d_new, total, initial, grad, moved)
    return [pack(lay, move, d_total), direct]


def renorm_back_all_fn(lay, coefficient, *args):
    d_new, _ = unpack_parts(lay, *args[:4])
    initial, grad, moved, total, places = args[4:]
    move, d_total, direct = renormed_back(
        coefficient, d_new, total[0:1, 0:1], initial, grad, moved
    )
    own = choose(in_slots(lay, in_three(lay, direct)), member_id(places))
    return [move, jnp.broadcast_to(d_total, (SUBLANES, LANES)), own]


def pull_math(lay, slabs, weights, moves, d_total):
    keys, values = join_rows(lay, slabs)
    rates = join_rates(lay, slabs)
    gate, up, down = (split(lay, w) for w in weights)
    gate_move, up_move, down_move = (split(lay, w) for w in moves)
    a, b, ta, tb = dots_left((gate, up, gate_move, up_move), keys, NN)
    u, w = dots_left((down, down_move), values, NN)
    sig, silu, rest, slope = gates(a)
    bend = sig * rest * (2.0 + a * (rest - sig))
    hidden = silu * b
    hidden_dot = slope * ta * b + silu * tb
    rate_part = -jnp.sum(w * hidden + u * hidden_dot, 0, keepdims=True) + d_total
    mu = -rates
    wm, um = mu * w, mu * u
    ga = split(lay, wm * b * slope + um * (bend * ta * b + slope * tb))
    gb = split(lay, wm * silu + um * slope * ta)
    gta = split(lay, um * slope * b)
    gtb = split(lay, um * silu)
    mh = split(lay, mu * hidden)
    md = split(lay, mu * hidden_dot)
    grads = dots_left((ga, gb), keys, NT) + dots_left((md,), values, NT)
    turned = split(lay, cat([weights[0], weights[1], moves[0], moves[1]], 0).T)
    d_key = dot_both(turned, tuple(cat(x, 0) for x in zip(ga, gb, gta, gtb)), NN)
    turned = split(lay, cat([moves[2], weights[2]], 0).T)
    d_value = dot_both(turned, tuple(cat(x, 0) for x in zip(mh, md)), NN)
    rows = slabs[0].shape[1]
    parts = []
    for i in range(len(slabs)):
        take = slice(i * rows, (i + 1) * rows)
        rate_rows = jnp.broadcast_to(rate_part[:, take], (SUBLANES, rows))
        parts.append(cat([d_key[:, take], d_value[:, take], rate_rows], 0))
    return grads, parts


def pull_fn(lay, *args):
    payloads, slabs, weights = args[: lay.plane], args[lay.plane : -1], args[-1]
    d_total = functools.reduce(jnp.add, [unpack(lay, p)[1] for p in payloads])
    grads, parts = pull_math(
        lay, slabs, in_three(lay, weights), unpack_all(lay, payloads), d_total
    )
    outs = pack_all(lay, grads, jnp.zeros((1, 1), F32))
    heads = lay.heads
    return outs + parts[:heads] + ([stack(parts[heads:])] if lay.cores > 1 else [])


def pull_other_fn(lay, moves, d_total, weights, *slabs):
    grads, parts = pull_math(
        lay, slabs, in_three(lay, weights), in_three(lay, moves), d_total[0:1, 0:1]
    )
    return [stack(parts), cat(grads, 0)]


def pull_own_fn(lay, moves, d_total, weights, before, *slabs):
    grads, parts = pull_math(
        lay, slabs, in_three(lay, weights), in_three(lay, moves), d_total[0:1, 0:1]
    )
    return [cat(grads, 0) + before, *parts]


def pull_last_fn(lay, count, moves, d_total, weights, before, places, *slabs):
    grads, parts = pull_math(
        lay, slabs, in_three(lay, weights), in_three(lay, moves), d_total[0:1, 0:1]
    )
    grads = [g + b for g, b in zip(grads, in_three(lay, before))]
    slots, member = in_slots(lay, grads), member_id(places)
    zero = jnp.zeros((1, 1), F32)
    outs = [pack(lay, choose(slots, member ^ r), zero) for r in range(lay.plane)]
    return outs + [*parts[:count], stack(parts[count:])]


def add_two_fn(first, first_in, second, second_in):
    return [first + first_in, second + second_in]


def finish_fn(lay, count, *args):
    slabs, head_ids = args[:-1], args[-1]
    dim = lay.head_dim
    outs = []
    for n in range(count):
        pieces = [s[n * dim : (n + 1) * dim] for s in slabs]
        ordered = [
            select_steps(lay, pieces, head_ids, h) for h in range(lay.heads)
        ]
        outs.append(cat(ordered, 0).T.astype(BF16))
    if slabs[0].shape[0] > count * dim:
        pieces = [s[count * dim : count * dim + 1] for s in slabs]
        rows = [select_steps(lay, pieces, head_ids, h) for h in range(lay.heads)]
        outs.append(cat(rows, 0))
    return outs


def add_fn(*args):
    return [part + args[-1][i] for i, part in enumerate(args[:-1])]


def total_fn(lay, scale, *args):
    payloads, direct, places = args[: lay.plane], args[-2], args[-1]
    body, _ = unpack(lay, functools.reduce(jnp.add, payloads))
    final = (body + direct) / scale
    pieces = [final[m * lay.slot : (m + 1) * lay.slot] for m in range(3)]
    return [choose(pieces, places[0:1, t : t + 1]) for t in range(3)]


def place_fn(*args):
    pieces, places = args[:3], args[3]
    return [cat([choose(pieces, places[0:1, 3 + q : 4 + q]) for q in range(3)], 0)]


VMEM_LIMIT = 24 * 1024 * 1024


def run(lay, fn, args, always=False, deps=()):
    if not (lay.packed or always):
        return fn(*args)
    shapes = jax.eval_shape(fn, *args)
    deps = [x[: min(SUBLANES, x.shape[0])] for x in deps]
    count = len(args)

    def kernel(*refs):
        ins, outs = refs[:count], refs[count + len(deps) :]
        for ref, value in zip(outs, fn(*[r[...] for r in ins])):
            ref[...] = value

    vmem = pl.BlockSpec(memory_space=pltpu.VMEM)
    return pl.pallas_call(
        kernel,
        out_shape=[jax.ShapeDtypeStruct(s.shape, s.dtype) for s in shapes],
        in_specs=[vmem] * (count + len(deps)),
        out_specs=[vmem] * len(shapes),
        compiler_params=pltpu.CompilerParams(vmem_limit_bytes=VMEM_LIMIT),
    )(*args, *deps)


def tie(lay, arrays, deps):
    if not lay.packed:
        return arrays
    deps = [x[:SUBLANES] for x in deps]
    vmem = pl.BlockSpec(memory_space=pltpu.VMEM)
    return list(
        pl.pallas_call(
            lambda *refs: None,
            out_shape=[jax.ShapeDtypeStruct(a.shape, a.dtype) for a in arrays],
            in_specs=[vmem] * (len(arrays) + len(deps)),
            out_specs=[vmem] * len(arrays),
            input_output_aliases={i: i for i in range(len(arrays))},
            compiler_params=pltpu.CompilerParams(vmem_limit_bytes=VMEM_LIMIT),
        )(*arrays, *deps)
    )


def on_device(lay, queries, key_rows, value_rows, step_rates, fast_init, out_grad):
    head_dim, _ = fast_init.shape
    heads, slot, plane = lay.heads, lay.slot, lay.plane
    coefficient = step_size * math.sqrt(queries.shape[0] * lay.devices)
    view, patch = lax.axis_index("view"), lax.axis_index("patch")
    core = lax.rem(view, lay.cores)
    head = patch // lay.sub
    member = view // lay.cores * lay.sub + lax.rem(patch, lay.sub)
    me = view * lay.patches + patch
    head_ids = jnp.full((SUBLANES, LANES), head, jnp.int32)

    def send(x, perm):
        return lax.ppermute(x, AXES, perm)

    def over_heads(slabs, hold=()):
        close = [send(slabs[t], lay.head_perm(t)) for t in range(1, min(2, heads))]
        away = slabs[2:]
        if hold:
            away = tie(lay, away, hold)
        away = [send(x, lay.head_perm(t)) for t, x in enumerate(away, 2)]
        return [slabs[0]] + close + away

    def over_cores(slabs):
        return [send(x, lay.core_perm()) for x in slabs] if lay.cores > 1 else []

    def total_rows(parts):
        if lay.cores == 1:
            return parts
        return run(lay, add_fn, (*parts[:heads], send(parts[heads], lay.core_perm())))

    def add_home(parts, away):
        return list(run(lay, add_fn, (*parts, send(away, lay.core_perm()))))

    def back_home(slabs):
        away = [send(slabs[t], lay.head_perm(t)) for t in range(2, heads)]
        close = [send(slabs[t], lay.head_perm(t)) for t in range(1, min(2, heads))]
        return [slabs[0]] + close + away

    def scatter(payloads):
        moved = [send(payloads[r], lay.scatter_perm(r)) for r in range(1, plane)]
        return [payloads[0]] + moved

    def gather(payload):
        return [payload] + [send(payload, lay.gather_perm(r)) for r in range(1, plane)]

    fn = functools.partial
    scale = math.sqrt(queries.shape[0] * lay.devices)
    kv = run(
        lay, fn(spread_rows, lay, True), (key_rows, value_rows, step_rates.T, head_ids), always=True
    )
    kv = over_heads(kv)
    qg = run(
        lay, fn(spread_rows, lay, False), (queries, out_grad, head_ids), always=True, deps=(kv[1],)
    )
    qg = over_heads(qg, tuple(kv[2:]))
    kv = kv + over_cores(kv)

    owner_perms, table = owner_plan(lay)
    places = lax.dynamic_slice_in_dim(jnp.array(table, jnp.int32), me, 1, 0)
    first = head * lay.hidden + core * lay.half
    turned = []
    for m in range(3):
        part = lax.dynamic_slice_in_dim(fast_init, m * heads * lay.hidden + first, lay.half, 1)
        turned.append(part.T)
    if not lay.packed:
        order = jnp.stack([lay.target(member, r) for r in range(plane)])
        turned = [
            t.reshape(plane, slot, head_dim)[order].reshape(lay.half, head_dim) for t in turned
        ]
    weights = jnp.concatenate(turned, 0)

    def exchange(first, second):
        bits = [1 << i for i in range(plane.bit_length() - 1)]
        turned_bits = bits[1:] + bits[:1]
        for i, (one, two) in enumerate(zip(bits, turned_bits)):
            if i:
                first, second = run(lay, add_two_fn, (first, first_in, second, second_in))
            first_in = send(first, lay.flip_perm(one))
            second_in = send(second, lay.flip_perm(two))
        return first, first_in, second, second_in

    if lay.packed:
        near = (heads + 1) // 2
        before = run(lay, fn(update_near_fn, lay), (weights, *kv[:near]), deps=(places,))
        rest = run(lay, fn(update_rest_fn, lay), (weights, *before, *kv[near:]))
        sums = exchange(*rest)
        close, away = qg[:2], tie(lay, qg[2:], (sums[0],))
        close, away = close + over_cores(close), away + over_cores(away)
        renewed, grad, moved, total = run(
            lay, fn(renorm_all_fn, lay, coefficient), (*sums, weights)
        )
        before, *query_close = run(lay, fn(apply_near_fn, lay, 2), (renewed, *close))
        applied = run(lay, fn(apply_far_fn, lay, heads - 2), (renewed, before, *away))
        query_home = add_home(query_close[:-1], query_close[-1]) + add_home(
            applied[2:-1], applied[-1]
        )
        sums = exchange(*applied[:2])
        move, d_total, direct = run(
            lay,
            fn(renorm_back_all_fn, lay, coefficient),
            (*sums, weights, grad, moved, total, places),
        )
        query_home = back_home(query_home)
        other, before = run(lay, fn(pull_other_fn, lay), (move, d_total, weights, *kv[heads + 2 :]))
        before, *key_far = run(
            lay, fn(pull_own_fn, lay), (move, d_total, weights, before, *kv[2:heads])
        )
        key_far = add_home(key_far, other)
        pulled = run(
            lay,
            fn(pull_last_fn, lay, 2),
            (move, d_total, weights, before, places, *kv[:2], *kv[heads : heads + 2]),
        )
        key_home = add_home(pulled[plane : plane + 2], pulled[-1]) + key_far
    else:
        own = jnp.concatenate([t[:slot] for t in turned], 0)
        sums = scatter(run(lay, fn(update_fn, lay), (weights, *kv)))
        payload, grad, moved = run(lay, fn(renorm_fn, lay, coefficient), (*sums, own))
        qg = qg + over_cores(qg)
        applied = run(lay, fn(apply_fn, lay), (*gather(payload), *qg))
        sums = scatter(applied[:plane])
        query_home = back_home(total_rows(applied[plane:]))
        d_payload, direct = run(
            lay, fn(renorm_back_fn, lay, coefficient), (*sums, payload, own, grad, moved)
        )
        pulled = run(lay, fn(pull_fn, lay), (*gather(d_payload), *kv, weights))
        key_home = total_rows(pulled[plane:])
    sums = scatter(pulled[:plane])
    pieces = run(lay, fn(total_fn, lay, scale), (*sums, direct, places), deps=tuple(key_home))
    key_home = back_home(key_home)
    (query_grad,) = run(
        lay, fn(finish_fn, lay, 1), (*query_home, head_ids), always=True, deps=tuple(pulled[:1])
    )
    arrived = [send(x, perm) for x, perm in zip(pieces, owner_perms)]
    (fast_grad,) = run(lay, place_fn, (*arrived, places))
    key_grad, value_grad, rate_grad = run(
        lay, fn(finish_fn, lay, 2), (*key_home, head_ids), always=True
    )
    return query_grad, key_grad, value_grad, rate_grad.T, fast_grad.T


def owner_plan(lay):
    rounds = lay.owner_rounds()
    table = [[0] * LANES for _ in range(lay.devices)]
    for t, chosen in enumerate(rounds):
        for source, owner, m, spot in chosen:
            table[source][t] = m
            table[owner][3 + spot] = t
            table[source][6] = lay.place(source)[0]
    return [[(i, o) for i, o, _, _ in chosen] for chosen in rounds], table


def solution(mesh):
    rows = P(AXES, None)

    def whole(queries, key_rows, value_rows, step_rates, fast_init, out_grad):
        heads = step_rates.shape[1]
        head_dim, columns = fast_init.shape
        lay = Layout(
            mesh.shape["view"], mesh.shape["patch"], heads, columns // (3 * heads), head_dim
        )

        def body(*args):
            return on_device(lay, *args)

        return jax.shard_map(
            body,
            mesh=mesh,
            in_specs=(rows, rows, rows, rows, P(), rows),
            out_specs=(rows, rows, rows, rows, P(None, AXES)),
            check_vma=False,
        )(queries, key_rows, value_rows, step_rates, fast_init, out_grad)

    return whole
```

```python
import functools
import itertools
import math

import jax
import jax.numpy as jnp
from jax import lax
from jax.experimental import pallas as pl
from jax.experimental.pallas import tpu as pltpu
from jax.sharding import PartitionSpec as P


AXES = ("view", "patch")
step_size = 0.2
epsilon = 1e-06
F32, BF16 = jnp.float32, jnp.bfloat16
LANES, SUBLANES = 128, 8


class Layout:
    def __init__(self, views, patches, heads, hidden, head_dim):
        self.heads, self.head_dim, self.hidden = heads, head_dim, hidden
        self.cores = 2 if views % 2 == 0 else 1
        self.patches, self.devices = patches, views * patches
        self.sub = patches // heads
        self.plane = (views // self.cores) * self.sub
        self.half = hidden // self.cores
        self.slot = self.half // self.plane
        self.pow2 = self.plane & (self.plane - 1) == 0
        rows = 3 * self.slot
        self.packed = (
            head_dim == LANES + LANES // 2
            and rows % (2 * SUBLANES) == 0
            and (3 * self.half) % (2 * SUBLANES) == 0
            and self.pow2
            and self.plane == 4
            and self.cores == 2
            and heads > 2
        )

    def place(self, device):
        view, patch = divmod(device, self.patches)
        outer, core = divmod(view, self.cores)
        head, sub = divmod(patch, self.sub)
        return outer * self.sub + sub, core, head

    def device(self, member, core, head):
        outer, sub = divmod(member, self.sub)
        return (outer * self.cores + core) * self.patches + head * self.sub + sub

    def target(self, member, step):
        return member ^ step if self.pow2 else (member + step) % self.plane

    def origin(self, member, step):
        return member ^ step if self.pow2 else (member - step) % self.plane

    def perm(self, move):
        return [(i, self.device(*move(*self.place(i)))) for i in range(self.devices)]

    def core_perm(self):
        return self.perm(lambda j, c, h: (j, (c + 1) % self.cores, h))

    def other_head(self, head, step):
        return head ^ step if self.heads & (self.heads - 1) == 0 else (step - head) % self.heads

    def head_perm(self, step):
        return self.perm(lambda j, c, h: (j, c, self.other_head(h, step)))

    def scatter_perm(self, step):
        return self.perm(lambda j, c, h: (self.target(j, step), c, h))

    def gather_perm(self, step):
        return self.perm(lambda j, c, h: (self.origin(j, step), c, h))

    def flip_perm(self, bit):
        return self.perm(lambda j, c, h: (j ^ bit, c, h))

    def owner_rounds(self):
        count = self.devices
        edges = []
        for i in range(count):
            j, c, h = self.place(i)
            for m in range(3):
                piece = (m * self.heads + h) * self.cores * self.plane + c * self.plane + j
                edges.append((i, piece // 3, m, piece % 3))
        left, rounds = list(edges), []
        for _ in range(3):
            out_edges = [[] for _ in range(count)]
            for edge in left:
                out_edges[edge[0]].append(edge)
            match = {}

            def place_one(i, seen):
                for edge in out_edges[i]:
                    if edge[1] in seen:
                        continue
                    seen.add(edge[1])
                    if edge[1] not in match or place_one(match[edge[1]][0], seen):
                        match[edge[1]] = edge
                        return True
                return False

            for i in range(count):
                place_one(i, set())
            chosen = sorted(match.values())
            rounds.append(chosen)
            left = [edge for edge in left if edge not in match.values()]
        return rounds


def direct_plan(lay):
    table = [[0] * LANES for _ in range(lay.devices)]
    first, second = [], []
    spots = {}
    for head in range(lay.heads):
        for core in range(lay.cores):
            runs = {}
            for m in range(3):
                for j in range(lay.plane):
                    base = (m * lay.heads + head) * lay.cores * lay.plane + core * lay.plane
                    runs.setdefault((m, (base + j) // 3), []).append((m * lay.plane + j, (base + j) % 3))
            runs = sorted(runs.items(), key=lambda item: -len(item[1]))
            long_runs, singles = runs[: lay.plane], runs[lay.plane :]

            def hops(member, owner):
                other, _, there = lay.place(owner)
                here, away = divmod(member, lay.sub), divmod(other, lay.sub)
                return abs(here[0] - away[0]) + abs(here[1] - away[1]) + 2 * abs(head - there)

            best = None
            for order in itertools.permutations(range(lay.plane)):
                for swap in (singles, singles[::-1]):
                    roles = [[long_runs[k]] for k in range(lay.plane)]
                    short = [k for k in range(lay.plane) if len(long_runs[k][1]) == 2]
                    for k, single in zip(short, swap):
                        roles[k].append(single)
                    cost = sum(
                        len(run[1]) * hops(order[k], run[0][1]) ** 2
                        for k in range(lay.plane)
                        for run in roles[k]
                    )
                    if best is None or cost < best[0]:
                        best = cost, order, roles
            _, order, roles = best
            held = {}
            for member, role in zip(order, roles):
                source = lay.device(member, core, head)
                held[member] = [piece for run in role for piece, _ in run[1]]
                for n, ((_, owner), run) in enumerate(role):
                    (second if n else first).append((source, owner))
                    for t, (_, spot) in enumerate(run):
                        spots[owner, spot] = 3 if n else t
            for member in range(lay.plane):
                row = table[lay.device(member, core, head)]
                for r in range(lay.plane):
                    row[8 + 3 * r : 11 + 3 * r] = held[lay.target(member, r)]
    for (owner, spot), index in spots.items():
        table[owner][3 + spot] = index
    return (first, second), table


def split(lay, x):
    if not lay.packed:
        return (x,)
    high = x.astype(BF16)
    return high, (x - high.astype(F32)).astype(BF16)


def dot(a, b, dims, precision=None):
    return lax.dot_general(
        a, b, (dims, ((), ())), precision=precision, preferred_element_type=F32
    )


NN, NT = ((1,), (0,)), ((1,), (1,))


def dot_left(parts, exact, dims):
    if len(parts) == 1:
        return dot(parts[0], exact, dims, lax.Precision.HIGH)
    return dot(parts[0], exact, dims) + dot(parts[1], exact, dims)


def dots_left(lefts, exact, dims):
    if len(lefts[0]) == 1:
        return [dot_left(left, exact, dims) for left in lefts]
    rows = lefts[0][0].shape[0]
    flat = dot(cat([part for left in lefts for part in left], 0), exact, dims)
    cuts = [flat[i * rows : (i + 1) * rows] for i in range(2 * len(lefts))]
    return [cuts[2 * i] + cuts[2 * i + 1] for i in range(len(lefts))]


def dot_both(a, b, dims):
    if len(a) == 1:
        return dot(a[0], b[0], dims, lax.Precision.HIGH)
    rows = a[0].shape[0]
    both = dot(cat(a, 0), b[0], dims)
    return both[:rows] + (dot(a[0], b[1], dims) + both[rows:])


def gates(act):
    sig = 1.0 / (1.0 + jnp.exp(-act))
    silu = act * sig
    rest = 1.0 - sig
    return sig, silu, rest, sig + silu * rest


def cat(parts, axis):
    return jnp.concatenate(parts, axis)


def pack(lay, body, extra):
    if not lay.packed:
        return cat([body, jnp.broadcast_to(extra, (SUBLANES, lay.head_dim))], 0)
    rows = body.shape[0]
    tail = body[:, LANES:]
    tail = cat([tail[: rows // 2], tail[rows // 2 :]], 1)
    return cat([body[:, :LANES], tail, jnp.broadcast_to(extra, (SUBLANES, LANES))], 0)


def unpack(lay, payload, rows=None):
    rows = 3 * lay.slot if rows is None else rows
    if not lay.packed:
        return payload[:rows], payload[rows : rows + 1, :1]
    tail = payload[rows : rows + rows // 2]
    half = LANES // 2
    tail = cat([tail[:, :half], tail[:, half:]], 0)
    return cat([payload[:rows], tail], 1), payload[rows + rows // 2 : rows + rows // 2 + 1, :1]


def wide_rows(lay):
    step = 2 * SUBLANES
    total = 3 * lay.half
    return total - total * 5 // 12 // step * step


def pack_parts(lay, grads, extra):
    body, rows = cat(grads, 0), wide_rows(lay)
    return [pack(lay, body[:rows], extra), pack(lay, body[rows:], extra)]


def unpack_parts(lay, first, first_in, second, second_in):
    rows = wide_rows(lay)
    top, extra = unpack(lay, first + first_in, rows)
    bottom, _ = unpack(lay, second + second_in, 3 * lay.half - rows)
    return cat([top, bottom], 0), extra


def in_pieces(lay, parts):
    slot = lay.slot
    return [p[j * slot : (j + 1) * slot] for p in parts for j in range(lay.plane)]


def held_pieces(places, pieces, step):
    first = 8 + 3 * step
    return cat([choose(pieces, places[0:1, t : t + 1]) for t in range(first, first + 3)], 0)


def choose(pieces, index):
    result = pieces[0]
    for i in range(1, len(pieces)):
        result = jnp.where(index == i, pieces[i], result)
    return result


def in_three(lay, body):
    return [body[m * lay.half : (m + 1) * lay.half] for m in range(3)]


def pack_all(lay, grads, extra):
    outs = []
    for step in range(lay.plane):
        take = slice(step * lay.slot, (step + 1) * lay.slot)
        outs.append(pack(lay, cat([g[take] for g in grads], 0), extra))
    return outs


def unpack_all(lay, payloads):
    bodies = [unpack(lay, p)[0] for p in payloads]
    slot = lay.slot
    return [cat([b[m * slot : (m + 1) * slot] for b in bodies], 0) for m in range(3)]


def select_heads(lay, pieces, head_ids, step):
    own = head_ids[0:1, :]
    result = pieces[0]
    for i in range(1, lay.heads):
        result = jnp.where(own == lay.other_head(i, step), pieces[i], result)
    return result


def select_steps(lay, pieces, head_ids, head):
    own = head_ids[0:1, :]
    result = pieces[0]
    for step in range(1, lay.heads):
        result = jnp.where(own == lay.other_head(head, step), pieces[step], result)
    return result


def spread_rows(lay, with_rates, first, second, *rest):
    dim = lay.head_dim
    head_ids = rest[-1]
    turned = [x.astype(F32).T for x in (first, second)]
    pieces = [[t[h * dim : (h + 1) * dim] for h in range(lay.heads)] for t in turned]
    if with_rates:
        rates = rest[0]
        rows = rates.shape[1]
        pieces.append(
            [jnp.broadcast_to(rates[h : h + 1], (SUBLANES, rows)) for h in range(lay.heads)]
        )
    return [
        cat([select_heads(lay, p, head_ids, shift) for p in pieces], 0)
        for shift in range(lay.heads)
    ]


def join_rows(lay, slabs):
    dim = lay.head_dim
    kind = BF16 if lay.packed else F32
    first = cat([s[:dim] for s in slabs], 1).astype(kind)
    second = cat([s[dim : 2 * dim] for s in slabs], 1).astype(kind)
    return first, second


def join_rates(lay, slabs):
    dim = lay.head_dim
    return cat([s[2 * dim : 2 * dim + 1] for s in slabs], 1)


def update_math(lay, slabs, weights):
    keys, values = join_rows(lay, slabs)
    rates = join_rates(lay, slabs)
    gate, up, down = (split(lay, w) for w in in_three(lay, weights))
    a, b = dots_left((gate, up), keys, NN)
    (u,) = dots_left((down,), values, NN)
    _, silu, _, slope = gates(a)
    mu = -rates * u
    d_gate, d_up = dots_left(
        (split(lay, mu * b * slope), split(lay, mu * silu)), keys, NT
    )
    (d_down,) = dots_left((split(lay, -rates * (silu * b)),), values, NT)
    return [d_gate, d_up, d_down], jnp.sum(rates, 1, keepdims=True)


def update_fn(lay, weights, *slabs):
    grads, total = update_math(lay, slabs, weights)
    return pack_all(lay, grads, total)


def update_near_fn(lay, weights, *slabs):
    grads, total = update_math(lay, slabs, weights)
    return [cat(grads, 0), jnp.broadcast_to(total, (SUBLANES, LANES))]


def update_rest_fn(lay, weights, before, total_before, *slabs):
    grads, total = update_math(lay, slabs, weights)
    grads = [g + b for g, b in zip(grads, in_three(lay, before))]
    return pack_parts(lay, grads, total + total_before[0:1, 0:1])


def norms(initial, moved):
    norm = jnp.sqrt(jnp.sum(initial * initial, 1, keepdims=True) + epsilon)
    inverse = lax.rsqrt(jnp.sum(moved * moved, 1, keepdims=True) + epsilon)
    return norm, inverse


def renormed(coefficient, body, total, initial):
    grad = body * (coefficient / total)
    moved = initial - grad
    norm, inverse = norms(initial, moved)
    return moved * (norm * inverse), grad, moved


def renorm_fn(lay, coefficient, *args):
    payloads, initial = args[:-1], args[-1]
    body, total = unpack(lay, functools.reduce(jnp.add, payloads))
    new, grad, moved = renormed(coefficient, body, total, initial)
    return [pack(lay, new, total), grad, moved]


def renorm_all_fn(lay, coefficient, *args):
    body, total = unpack_parts(lay, *args[:4])
    new, grad, moved = renormed(coefficient, body, total, args[4])
    return [new, grad, moved, jnp.broadcast_to(total, (SUBLANES, LANES))]


def apply_math(lay, slabs, weights):
    queries, cotangents = join_rows(lay, slabs)
    gate, up, down = (split(lay, w) for w in weights)
    a, b = dots_left((gate, up), queries, NN)
    (u,) = dots_left((down,), cotangents, NN)
    _, silu, _, slope = gates(a)
    da = split(lay, u * b * slope)
    db = split(lay, u * silu)
    h = split(lay, silu * b)
    grads = dots_left((da, db), queries, NT) + dots_left((h,), cotangents, NT)
    turned = split(lay, cat([weights[0], weights[1]], 0).T)
    both = tuple(cat([x, y], 0) for x, y in zip(da, db))
    d_query = dot_both(turned, both, NN)
    rows = slabs[0].shape[1]
    return grads, [d_query[:, i * rows : (i + 1) * rows] for i in range(len(slabs))]


def apply_fn(lay, *args):
    weights, slabs = unpack_all(lay, args[: lay.plane]), args[lay.plane :]
    grads, parts = apply_math(lay, slabs, weights)
    outs = pack_all(lay, grads, jnp.zeros((1, 1), F32))
    heads = lay.heads
    return outs + parts[:heads] + ([stack(parts[heads:])] if lay.cores > 1 else [])


def apply_near_fn(lay, count, new, *slabs):
    grads, parts = apply_math(lay, slabs, in_three(lay, new))
    return [cat(grads, 0), *parts[:count], stack(parts[count:])]


def apply_far_fn(lay, count, new, before, *slabs):
    grads, parts = apply_math(lay, slabs, in_three(lay, new))
    grads = [g + b for g, b in zip(grads, in_three(lay, before))]
    outs = pack_parts(lay, grads, jnp.zeros((1, 1), F32))
    return outs + [*parts[:count], stack(parts[count:])]


def stack(parts):
    return cat([p[None] for p in parts], 0)


def renormed_back(coefficient, d_new, total, initial, grad, moved):
    norm, inverse = norms(initial, moved)
    dots = jnp.sum(d_new * moved, 1, keepdims=True)
    d_moved = d_new * (norm * inverse) - moved * (dots * norm * inverse * inverse * inverse)
    direct = d_moved + initial * (dots * inverse / norm)
    d_update = -d_moved
    part = jnp.sum(jnp.sum(d_update * grad, 1, keepdims=True), 0, keepdims=True)
    return d_update * (coefficient / total), -part / total, direct


def renorm_back_fn(lay, coefficient, *args):
    payloads = args[: lay.plane]
    total_payload, initial, grad, moved = args[lay.plane :]
    d_new, _ = unpack(lay, functools.reduce(jnp.add, payloads))
    _, total = unpack(lay, total_payload)
    move, d_total, direct = renormed_back(coefficient, d_new, total, initial, grad, moved)
    return [pack(lay, move, d_total), direct]


def renorm_back_all_fn(lay, coefficient, *args):
    d_new, _ = unpack_parts(lay, *args[:4])
    initial, grad, moved, total, places = args[4:]
    move, d_total, direct = renormed_back(
        coefficient, d_new, total[0:1, 0:1], initial, grad, moved
    )
    own = held_pieces(places, in_pieces(lay, in_three(lay, direct)), 0)
    return [move, jnp.broadcast_to(d_total, (SUBLANES, LANES)), own]


def pull_math(lay, slabs, weights, moves, d_total):
    keys, values = join_rows(lay, slabs)
    rates = join_rates(lay, slabs)
    gate, up, down = (split(lay, w) for w in weights)
    gate_move, up_move, down_move = (split(lay, w) for w in moves)
    a, b, ta, tb = dots_left((gate, up, gate_move, up_move), keys, NN)
    u, w = dots_left((down, down_move), values, NN)
    sig, silu, rest, slope = gates(a)
    bend = sig * rest * (2.0 + a * (rest - sig))
    hidden = silu * b
    hidden_dot = slope * ta * b + silu * tb
    rate_part = -jnp.sum(w * hidden + u * hidden_dot, 0, keepdims=True) + d_total
    mu = -rates
    wm, um = mu * w, mu * u
    ga = split(lay, wm * b * slope + um * (bend * ta * b + slope * tb))
    gb = split(lay, wm * silu + um * slope * ta)
    gta = split(lay, um * slope * b)
    gtb = split(lay, um * silu)
    mh = split(lay, mu * hidden)
    md = split(lay, mu * hidden_dot)
    grads = dots_left((ga, gb), keys, NT) + dots_left((md,), values, NT)
    turned = split(lay, cat([weights[0], weights[1], moves[0], moves[1]], 0).T)
    d_key = dot_both(turned, tuple(cat(x, 0) for x in zip(ga, gb, gta, gtb)), NN)
    turned = split(lay, cat([moves[2], weights[2]], 0).T)
    d_value = dot_both(turned, tuple(cat(x, 0) for x in zip(mh, md)), NN)
    rows = slabs[0].shape[1]
    parts = []
    for i in range(len(slabs)):
        take = slice(i * rows, (i + 1) * rows)
        rate_rows = jnp.broadcast_to(rate_part[:, take], (SUBLANES, rows))
        parts.append(cat([d_key[:, take], d_value[:, take], rate_rows], 0))
    return grads, parts


def pull_fn(lay, *args):
    payloads, slabs, weights = args[: lay.plane], args[lay.plane : -1], args[-1]
    d_total = functools.reduce(jnp.add, [unpack(lay, p)[1] for p in payloads])
    grads, parts = pull_math(
        lay, slabs, in_three(lay, weights), unpack_all(lay, payloads), d_total
    )
    outs = pack_all(lay, grads, jnp.zeros((1, 1), F32))
    heads = lay.heads
    return outs + parts[:heads] + ([stack(parts[heads:])] if lay.cores > 1 else [])


def pull_other_fn(lay, moves, d_total, weights, *slabs):
    grads, parts = pull_math(
        lay, slabs, in_three(lay, weights), in_three(lay, moves), d_total[0:1, 0:1]
    )
    return [stack(parts), cat(grads, 0)]


def pull_own_fn(lay, moves, d_total, weights, before, *slabs):
    grads, parts = pull_math(
        lay, slabs, in_three(lay, weights), in_three(lay, moves), d_total[0:1, 0:1]
    )
    return [cat(grads, 0) + before, *parts]


def pull_last_fn(lay, count, moves, d_total, weights, before, places, *slabs):
    grads, parts = pull_math(
        lay, slabs, in_three(lay, weights), in_three(lay, moves), d_total[0:1, 0:1]
    )
    grads = [g + b for g, b in zip(grads, in_three(lay, before))]
    pieces = in_pieces(lay, grads)
    zero = jnp.zeros((1, 1), F32)
    outs = [pack(lay, held_pieces(places, pieces, r), zero) for r in range(lay.plane)]
    return outs + [*parts[:count], stack(parts[count:])]


def add_two_fn(first, first_in, second, second_in):
    return [first + first_in, second + second_in]


def finish_fn(lay, count, *args):
    slabs, head_ids = args[:-1], args[-1]
    dim = lay.head_dim
    outs = []
    for n in range(count):
        pieces = [s[n * dim : (n + 1) * dim] for s in slabs]
        ordered = [
            select_steps(lay, pieces, head_ids, h) for h in range(lay.heads)
        ]
        outs.append(cat(ordered, 0).T.astype(BF16))
    if slabs[0].shape[0] > count * dim:
        pieces = [s[count * dim : count * dim + 1] for s in slabs]
        rows = [select_steps(lay, pieces, head_ids, h) for h in range(lay.heads)]
        outs.append(cat(rows, 0))
    return outs


def add_fn(*args):
    return [part + args[-1][i] for i, part in enumerate(args[:-1])]


def total_fn(lay, scale, *args):
    payloads, direct, places = args[: lay.plane], args[-2], args[-1]
    body, _ = unpack(lay, functools.reduce(jnp.add, payloads))
    final = (body + direct) / scale
    pieces = [final[m * lay.slot : (m + 1) * lay.slot] for m in range(3)]
    return [choose(pieces, places[0:1, t : t + 1]) for t in range(3)]


def place_fn(*args):
    pieces, places = args[:3], args[3]
    return [cat([choose(pieces, places[0:1, 3 + q : 4 + q]) for q in range(3)], 0)]


def total_two_fn(lay, scale, *args):
    payloads, direct = args[: lay.plane], args[-1]
    body, extra = unpack(lay, functools.reduce(jnp.add, payloads))
    final = (body + direct) / scale
    return [pack(lay, final, extra), final[2 * lay.slot :]]


def finish_all_fn(lay, *args):
    first, second, places, slabs = args[0], args[1], args[2], args[3:]
    body, _ = unpack(lay, first)
    pieces = [body[t * lay.slot : (t + 1) * lay.slot] for t in range(3)] + [second]
    placed = cat([choose(pieces, places[0:1, t : t + 1]) for t in range(3, 6)], 0)
    return [placed, *finish_fn(lay, 2, *slabs)]


VMEM_LIMIT = 24 * 1024 * 1024


def run(lay, fn, args, always=False, deps=()):
    if not (lay.packed or always):
        return fn(*args)
    shapes = jax.eval_shape(fn, *args)
    deps = [x[: min(SUBLANES, x.shape[0])] for x in deps]
    count = len(args)

    def kernel(*refs):
        ins, outs = refs[:count], refs[count + len(deps) :]
        for ref, value in zip(outs, fn(*[r[...] for r in ins])):
            ref[...] = value

    vmem = pl.BlockSpec(memory_space=pltpu.VMEM)
    return pl.pallas_call(
        kernel,
        out_shape=[jax.ShapeDtypeStruct(s.shape, s.dtype) for s in shapes],
        in_specs=[vmem] * (count + len(deps)),
        out_specs=[vmem] * len(shapes),
        compiler_params=pltpu.CompilerParams(vmem_limit_bytes=VMEM_LIMIT),
    )(*args, *deps)


def tie(lay, arrays, deps):
    if not lay.packed:
        return arrays
    deps = [x[:SUBLANES] for x in deps]
    vmem = pl.BlockSpec(memory_space=pltpu.VMEM)
    return list(
        pl.pallas_call(
            lambda *refs: None,
            out_shape=[jax.ShapeDtypeStruct(a.shape, a.dtype) for a in arrays],
            in_specs=[vmem] * (len(arrays) + len(deps)),
            out_specs=[vmem] * len(arrays),
            input_output_aliases={i: i for i in range(len(arrays))},
            compiler_params=pltpu.CompilerParams(vmem_limit_bytes=VMEM_LIMIT),
        )(*arrays, *deps)
    )


def on_device(lay, queries, key_rows, value_rows, step_rates, fast_init, out_grad):
    head_dim, _ = fast_init.shape
    heads, slot, plane = lay.heads, lay.slot, lay.plane
    coefficient = step_size * math.sqrt(queries.shape[0] * lay.devices)
    view, patch = lax.axis_index("view"), lax.axis_index("patch")
    core = lax.rem(view, lay.cores)
    head = patch // lay.sub
    member = view // lay.cores * lay.sub + lax.rem(patch, lay.sub)
    me = view * lay.patches + patch
    head_ids = jnp.full((SUBLANES, LANES), head, jnp.int32)

    def send(x, perm):
        return lax.ppermute(x, AXES, perm)

    def over_heads(slabs, hold=()):
        close = [send(slabs[t], lay.head_perm(t)) for t in range(1, min(2, heads))]
        away = slabs[2:]
        if hold:
            away = tie(lay, away, hold)
        away = [send(x, lay.head_perm(t)) for t, x in enumerate(away, 2)]
        return [slabs[0]] + close + away

    def over_cores(slabs):
        return [send(x, lay.core_perm()) for x in slabs] if lay.cores > 1 else []

    def total_rows(parts):
        if lay.cores == 1:
            return parts
        return run(lay, add_fn, (*parts[:heads], send(parts[heads], lay.core_perm())))

    def add_home(parts, away):
        return list(run(lay, add_fn, (*parts, send(away, lay.core_perm()))))

    def back_home(slabs):
        away = [send(slabs[t], lay.head_perm(t)) for t in range(2, heads)]
        close = [send(slabs[t], lay.head_perm(t)) for t in range(1, min(2, heads))]
        return [slabs[0]] + close + away

    def scatter(payloads):
        moved = [send(payloads[r], lay.scatter_perm(r)) for r in range(1, plane)]
        return [payloads[0]] + moved

    def gather(payload):
        return [payload] + [send(payload, lay.gather_perm(r)) for r in range(1, plane)]

    fn = functools.partial
    scale = math.sqrt(queries.shape[0] * lay.devices)
    kv = run(
        lay, fn(spread_rows, lay, True), (key_rows, value_rows, step_rates.T, head_ids), always=True
    )
    kv = over_heads(kv)
    qg = run(
        lay, fn(spread_rows, lay, False), (queries, out_grad, head_ids), always=True, deps=(kv[1],)
    )
    qg = over_heads(qg, tuple(kv[2:]))
    kv = kv + over_cores(kv)

    owner_perms, table = (direct_plan if lay.packed else owner_plan)(lay)
    places = lax.dynamic_slice_in_dim(jnp.array(table, jnp.int32), me, 1, 0)
    first = head * lay.hidden + core * lay.half
    turned = []
    for m in range(3):
        part = lax.dynamic_slice_in_dim(fast_init, m * heads * lay.hidden + first, lay.half, 1)
        turned.append(part.T)
    if not lay.packed:
        order = jnp.stack([lay.target(member, r) for r in range(plane)])
        turned = [
            t.reshape(plane, slot, head_dim)[order].reshape(lay.half, head_dim) for t in turned
        ]
    weights = jnp.concatenate(turned, 0)

    def exchange(first, second):
        bits = [1 << i for i in range(plane.bit_length() - 1)]
        turned_bits = bits[1:] + bits[:1]
        for i, (one, two) in enumerate(zip(bits, turned_bits)):
            if i:
                first, second = run(lay, add_two_fn, (first, first_in, second, second_in))
            first_in = send(first, lay.flip_perm(one))
            second_in = send(second, lay.flip_perm(two))
        return first, first_in, second, second_in

    if lay.packed:
        near = (heads + 1) // 2
        before = run(lay, fn(update_near_fn, lay), (weights, *kv[:near]), deps=(places,))
        rest = run(lay, fn(update_rest_fn, lay), (weights, *before, *kv[near:]))
        sums = exchange(*rest)
        close, away = qg[:2], tie(lay, qg[2:], (sums[0],))
        close, away = close + over_cores(close), away + over_cores(away)
        renewed, grad, moved, total = run(
            lay, fn(renorm_all_fn, lay, coefficient), (*sums, weights)
        )
        before, *query_close = run(lay, fn(apply_near_fn, lay, 2), (renewed, *close))
        applied = run(lay, fn(apply_far_fn, lay, heads - 2), (renewed, before, *away))
        query_home = add_home(query_close[:-1], query_close[-1]) + add_home(
            applied[2:-1], applied[-1]
        )
        sums = exchange(*applied[:2])
        move, d_total, direct = run(
            lay,
            fn(renorm_back_all_fn, lay, coefficient),
            (*sums, weights, grad, moved, total, places),
        )
        query_home = back_home(query_home)
        other, before = run(lay, fn(pull_other_fn, lay), (move, d_total, weights, *kv[heads + 2 :]))
        before, *key_far = run(
            lay, fn(pull_own_fn, lay), (move, d_total, weights, before, *kv[2:heads])
        )
        key_far = add_home(key_far, other)
        pulled = run(
            lay,
            fn(pull_last_fn, lay, 2),
            (move, d_total, weights, before, places, *kv[:2], *kv[heads : heads + 2]),
        )
        key_home = add_home(pulled[plane : plane + 2], pulled[-1]) + key_far
    else:
        own = jnp.concatenate([t[:slot] for t in turned], 0)
        sums = scatter(run(lay, fn(update_fn, lay), (weights, *kv)))
        payload, grad, moved = run(lay, fn(renorm_fn, lay, coefficient), (*sums, own))
        qg = qg + over_cores(qg)
        applied = run(lay, fn(apply_fn, lay), (*gather(payload), *qg))
        sums = scatter(applied[:plane])
        query_home = back_home(total_rows(applied[plane:]))
        d_payload, direct = run(
            lay, fn(renorm_back_fn, lay, coefficient), (*sums, payload, own, grad, moved)
        )
        pulled = run(lay, fn(pull_fn, lay), (*gather(d_payload), *kv, weights))
        key_home = total_rows(pulled[plane:])
    sums = scatter(pulled[:plane])
    key_slabs = back_home(key_home)
    (query_grad,) = run(
        lay, fn(finish_fn, lay, 1), (*query_home, head_ids), always=True, deps=tuple(pulled[:1])
    )
    if lay.packed:
        ready = run(lay, fn(total_two_fn, lay, scale), (*sums, direct), deps=tuple(key_home))
        arrived = [send(x, perm) for x, perm in zip(ready, owner_perms)]
        fast_grad, key_grad, value_grad, rate_grad = run(
            lay, fn(finish_all_fn, lay), (*arrived, places, *key_slabs, head_ids)
        )
    else:
        pieces = run(lay, fn(total_fn, lay, scale), (*sums, direct, places))
        arrived = [send(x, perm) for x, perm in zip(pieces, owner_perms)]
        (fast_grad,) = run(lay, place_fn, (*arrived, places))
        key_grad, value_grad, rate_grad = run(
            lay, fn(finish_fn, lay, 2), (*key_slabs, head_ids), always=True
        )
    return query_grad, key_grad, value_grad, rate_grad.T, fast_grad.T


def owner_plan(lay):
    rounds = lay.owner_rounds()
    table = [[0] * LANES for _ in range(lay.devices)]
    for t, chosen in enumerate(rounds):
        for source, owner, m, spot in chosen:
            table[source][t] = m
            table[owner][3 + spot] = t
    return [[(i, o) for i, o, _, _ in chosen] for chosen in rounds], table


def solution(mesh):
    rows = P(AXES, None)

    def whole(queries, key_rows, value_rows, step_rates, fast_init, out_grad):
        heads = step_rates.shape[1]
        head_dim, columns = fast_init.shape
        lay = Layout(
            mesh.shape["view"], mesh.shape["patch"], heads, columns // (3 * heads), head_dim
        )

        def body(*args):
            return on_device(lay, *args)

        return jax.shard_map(
            body,
            mesh=mesh,
            in_specs=(rows, rows, rows, rows, P(), rows),
            out_specs=(rows, rows, rows, rows, P(None, AXES)),
            check_vma=False,
        )(queries, key_rows, value_rows, step_rates, fast_init, out_grad)

    return whole
```

```python
import functools
import itertools
import math

import jax
import jax.numpy as jnp
from jax import lax
from jax.experimental import pallas as pl
from jax.experimental.pallas import tpu as pltpu
from jax.sharding import PartitionSpec as P


AXES = ("view", "patch")
step_size = 0.2
epsilon = 1e-06
F32, BF16 = jnp.float32, jnp.bfloat16
LANES, SUBLANES = 128, 8


class Layout:
    def __init__(self, views, patches, heads, hidden, head_dim):
        self.heads, self.head_dim, self.hidden = heads, head_dim, hidden
        self.cores = 2 if views % 2 == 0 else 1
        self.patches, self.devices = patches, views * patches
        self.sub = patches // heads
        self.plane = (views // self.cores) * self.sub
        self.half = hidden // self.cores
        self.slot = self.half // self.plane
        self.pow2 = self.plane & (self.plane - 1) == 0
        rows = 3 * self.slot
        self.packed = (
            head_dim == LANES + LANES // 2
            and rows % (2 * SUBLANES) == 0
            and (3 * self.half) % (2 * SUBLANES) == 0
            and self.pow2
            and self.plane == 4
            and self.cores == 2
            and heads > 2
        )

    def place(self, device):
        view, patch = divmod(device, self.patches)
        outer, core = divmod(view, self.cores)
        head, sub = divmod(patch, self.sub)
        return outer * self.sub + sub, core, head

    def device(self, member, core, head):
        outer, sub = divmod(member, self.sub)
        return (outer * self.cores + core) * self.patches + head * self.sub + sub

    def target(self, member, step):
        return member ^ step if self.pow2 else (member + step) % self.plane

    def origin(self, member, step):
        return member ^ step if self.pow2 else (member - step) % self.plane

    def perm(self, move):
        return [(i, self.device(*move(*self.place(i)))) for i in range(self.devices)]

    def core_perm(self):
        return self.perm(lambda j, c, h: (j, (c + 1) % self.cores, h))

    def other_head(self, head, step):
        return head ^ step if self.heads & (self.heads - 1) == 0 else (step - head) % self.heads

    def head_perm(self, step):
        return self.perm(lambda j, c, h: (j, c, self.other_head(h, step)))

    def scatter_perm(self, step):
        return self.perm(lambda j, c, h: (self.target(j, step), c, h))

    def gather_perm(self, step):
        return self.perm(lambda j, c, h: (self.origin(j, step), c, h))

    def flip_perm(self, bit):
        return self.perm(lambda j, c, h: (j ^ bit, c, h))

    def owner_rounds(self):
        count = self.devices
        edges = []
        for i in range(count):
            j, c, h = self.place(i)
            for m in range(3):
                piece = (m * self.heads + h) * self.cores * self.plane + c * self.plane + j
                edges.append((i, piece // 3, m, piece % 3))
        left, rounds = list(edges), []
        for _ in range(3):
            out_edges = [[] for _ in range(count)]
            for edge in left:
                out_edges[edge[0]].append(edge)
            match = {}

            def place_one(i, seen):
                for edge in out_edges[i]:
                    if edge[1] in seen:
                        continue
                    seen.add(edge[1])
                    if edge[1] not in match or place_one(match[edge[1]][0], seen):
                        match[edge[1]] = edge
                        return True
                return False

            for i in range(count):
                place_one(i, set())
            chosen = sorted(match.values())
            rounds.append(chosen)
            left = [edge for edge in left if edge not in match.values()]
        return rounds


def direct_plan(lay):
    table = [[0] * LANES for _ in range(lay.devices)]
    first, second = [], []
    spots = {}
    for head in range(lay.heads):
        for core in range(lay.cores):
            runs = {}
            for m in range(3):
                for j in range(lay.plane):
                    base = (m * lay.heads + head) * lay.cores * lay.plane + core * lay.plane
                    runs.setdefault((m, (base + j) // 3), []).append((m * lay.plane + j, (base + j) % 3))
            runs = sorted(runs.items(), key=lambda item: -len(item[1]))
            long_runs, singles = runs[: lay.plane], runs[lay.plane :]

            def hops(member, owner):
                other, _, there = lay.place(owner)
                here, away = divmod(member, lay.sub), divmod(other, lay.sub)
                return abs(here[0] - away[0]) + abs(here[1] - away[1]) + 2 * abs(head - there)

            best = None
            for order in itertools.permutations(range(lay.plane)):
                for swap in (singles, singles[::-1]):
                    roles = [[long_runs[k]] for k in range(lay.plane)]
                    short = [k for k in range(lay.plane) if len(long_runs[k][1]) == 2]
                    for k, single in zip(short, swap):
                        roles[k].append(single)
                    cost = sum(
                        len(run[1]) * hops(order[k], run[0][1]) ** 2
                        for k in range(lay.plane)
                        for run in roles[k]
                    )
                    if best is None or cost < best[0]:
                        best = cost, order, roles
            _, order, roles = best
            held = {}
            for member, role in zip(order, roles):
                source = lay.device(member, core, head)
                held[member] = [piece for run in role for piece, _ in run[1]]
                for n, ((_, owner), run) in enumerate(role):
                    (second if n else first).append((source, owner))
                    for t, (_, spot) in enumerate(run):
                        spots[owner, spot] = 3 if n else t
            for member in range(lay.plane):
                row = table[lay.device(member, core, head)]
                for r in range(lay.plane):
                    row[8 + 3 * r : 11 + 3 * r] = held[lay.target(member, r)]
    for (owner, spot), index in spots.items():
        table[owner][3 + spot] = index
    return (first, second), table


def split(lay, x):
    if not lay.packed:
        return (x,)
    high = x.astype(BF16)
    return high, (x - high.astype(F32)).astype(BF16)


def dot(a, b, dims, precision=None):
    return lax.dot_general(
        a, b, (dims, ((), ())), precision=precision, preferred_element_type=F32
    )


NN, NT = ((1,), (0,)), ((1,), (1,))


def dot_left(parts, exact, dims):
    if len(parts) == 1:
        return dot(parts[0], exact, dims, lax.Precision.HIGH)
    return dot(parts[0], exact, dims) + dot(parts[1], exact, dims)


def dots_left(lefts, exact, dims):
    if len(lefts[0]) == 1:
        return [dot_left(left, exact, dims) for left in lefts]
    rows = lefts[0][0].shape[0]
    flat = dot(cat([part for left in lefts for part in left], 0), exact, dims)
    cuts = [flat[i * rows : (i + 1) * rows] for i in range(2 * len(lefts))]
    return [cuts[2 * i] + cuts[2 * i + 1] for i in range(len(lefts))]


def dot_both(a, b, dims):
    if len(a) == 1:
        return dot(a[0], b[0], dims, lax.Precision.HIGH)
    rows = a[0].shape[0]
    both = dot(cat(a, 0), b[0], dims)
    return both[:rows] + (dot(a[0], b[1], dims) + both[rows:])


def gates(act):
    sig = 1.0 / (1.0 + jnp.exp(-act))
    silu = act * sig
    rest = 1.0 - sig
    return sig, silu, rest, sig + silu * rest


def cat(parts, axis):
    return jnp.concatenate(parts, axis)


def pack(lay, body, extra):
    if not lay.packed:
        return cat([body, jnp.broadcast_to(extra, (SUBLANES, lay.head_dim))], 0)
    rows = body.shape[0]
    tail = body[:, LANES:]
    tail = cat([tail[: rows // 2], tail[rows // 2 :]], 1)
    return cat([body[:, :LANES], tail, jnp.broadcast_to(extra, (SUBLANES, LANES))], 0)


def unpack(lay, payload, rows=None):
    rows = 3 * lay.slot if rows is None else rows
    if not lay.packed:
        return payload[:rows], payload[rows : rows + 1, :1]
    tail = payload[rows : rows + rows // 2]
    half = LANES // 2
    tail = cat([tail[:, :half], tail[:, half:]], 0)
    return cat([payload[:rows], tail], 1), payload[rows + rows // 2 : rows + rows // 2 + 1, :1]


def wide_rows(lay):
    step = 2 * SUBLANES
    total = 3 * lay.half
    return total - total * 17 // 36 // step * step


def pack_parts(lay, grads, extra):
    body, rows = cat(grads, 0), wide_rows(lay)
    return [pack(lay, body[:rows], extra), pack(lay, body[rows:], extra)]


def unpack_parts(lay, first, first_in, second, second_in):
    rows = wide_rows(lay)
    top, extra = unpack(lay, first + first_in, rows)
    bottom, _ = unpack(lay, second + second_in, 3 * lay.half - rows)
    return cat([top, bottom], 0), extra


def in_pieces(lay, parts):
    slot = lay.slot
    return [p[j * slot : (j + 1) * slot] for p in parts for j in range(lay.plane)]


def held_pieces(places, pieces, step):
    first = 8 + 3 * step
    return cat([choose(pieces, places[0:1, t : t + 1]) for t in range(first, first + 3)], 0)


def choose(pieces, index):
    result = pieces[0]
    for i in range(1, len(pieces)):
        result = jnp.where(index == i, pieces[i], result)
    return result


def in_three(lay, body):
    return [body[m * lay.half : (m + 1) * lay.half] for m in range(3)]


def pack_all(lay, grads, extra):
    outs = []
    for step in range(lay.plane):
        take = slice(step * lay.slot, (step + 1) * lay.slot)
        outs.append(pack(lay, cat([g[take] for g in grads], 0), extra))
    return outs


def unpack_all(lay, payloads):
    bodies = [unpack(lay, p)[0] for p in payloads]
    slot = lay.slot
    return [cat([b[m * slot : (m + 1) * slot] for b in bodies], 0) for m in range(3)]


def select_heads(lay, pieces, head_ids, step):
    own = head_ids[0:1, :]
    result = pieces[0]
    for i in range(1, lay.heads):
        result = jnp.where(own == lay.other_head(i, step), pieces[i], result)
    return result


def select_steps(lay, pieces, head_ids, head):
    own = head_ids[0:1, :]
    result = pieces[0]
    for step in range(1, lay.heads):
        result = jnp.where(own == lay.other_head(head, step), pieces[step], result)
    return result


def spread_rows(lay, with_rates, first, second, *rest):
    dim = lay.head_dim
    head_ids = rest[-1]
    turned = [x.astype(F32).T for x in (first, second)]
    pieces = [[t[h * dim : (h + 1) * dim] for h in range(lay.heads)] for t in turned]
    if with_rates:
        rates = rest[0]
        rows = rates.shape[1]
        pieces.append(
            [jnp.broadcast_to(rates[h : h + 1], (SUBLANES, rows)) for h in range(lay.heads)]
        )
    return [
        cat([select_heads(lay, p, head_ids, shift) for p in pieces], 0)
        for shift in range(lay.heads)
    ]


def join_rows(lay, slabs):
    dim = lay.head_dim
    kind = BF16 if lay.packed else F32
    first = cat([s[:dim] for s in slabs], 1).astype(kind)
    second = cat([s[dim : 2 * dim] for s in slabs], 1).astype(kind)
    return first, second


def join_rates(lay, slabs):
    dim = lay.head_dim
    return cat([s[2 * dim : 2 * dim + 1] for s in slabs], 1)


def update_math(lay, slabs, weights):
    keys, values = join_rows(lay, slabs)
    rates = join_rates(lay, slabs)
    gate, up, down = (split(lay, w) for w in in_three(lay, weights))
    a, b = dots_left((gate, up), keys, NN)
    (u,) = dots_left((down,), values, NN)
    _, silu, _, slope = gates(a)
    mu = -rates * u
    d_gate, d_up = dots_left(
        (split(lay, mu * b * slope), split(lay, mu * silu)), keys, NT
    )
    (d_down,) = dots_left((split(lay, -rates * (silu * b)),), values, NT)
    return [d_gate, d_up, d_down], jnp.sum(rates, 1, keepdims=True)


def update_fn(lay, weights, *slabs):
    grads, total = update_math(lay, slabs, weights)
    return pack_all(lay, grads, total)


def update_near_fn(lay, weights, *slabs):
    grads, total = update_math(lay, slabs, weights)
    return [cat(grads, 0), jnp.broadcast_to(total, (SUBLANES, LANES))]


def update_rest_fn(lay, weights, before, total_before, *slabs):
    grads, total = update_math(lay, slabs, weights)
    grads = [g + b for g, b in zip(grads, in_three(lay, before))]
    return pack_parts(lay, grads, total + total_before[0:1, 0:1])


def norms(initial, moved):
    norm = jnp.sqrt(jnp.sum(initial * initial, 1, keepdims=True) + epsilon)
    inverse = lax.rsqrt(jnp.sum(moved * moved, 1, keepdims=True) + epsilon)
    return norm, inverse


def renormed(coefficient, body, total, initial):
    grad = body * (coefficient / total)
    moved = initial - grad
    norm, inverse = norms(initial, moved)
    return moved * (norm * inverse), grad, moved


def renorm_fn(lay, coefficient, *args):
    payloads, initial = args[:-1], args[-1]
    body, total = unpack(lay, functools.reduce(jnp.add, payloads))
    new, grad, moved = renormed(coefficient, body, total, initial)
    return [pack(lay, new, total), grad, moved]


def renorm_all_fn(lay, coefficient, *args):
    body, total = unpack_parts(lay, *args[:4])
    new, grad, moved = renormed(coefficient, body, total, args[4])
    return [new, grad, moved, jnp.broadcast_to(total, (SUBLANES, LANES))]


def apply_math(lay, slabs, weights):
    queries, cotangents = join_rows(lay, slabs)
    gate, up, down = (split(lay, w) for w in weights)
    a, b = dots_left((gate, up), queries, NN)
    (u,) = dots_left((down,), cotangents, NN)
    _, silu, _, slope = gates(a)
    da = split(lay, u * b * slope)
    db = split(lay, u * silu)
    h = split(lay, silu * b)
    grads = dots_left((da, db), queries, NT) + dots_left((h,), cotangents, NT)
    turned = split(lay, cat([weights[0], weights[1]], 0).T)
    both = tuple(cat([x, y], 0) for x, y in zip(da, db))
    d_query = dot_both(turned, both, NN)
    rows = slabs[0].shape[1]
    return grads, [d_query[:, i * rows : (i + 1) * rows] for i in range(len(slabs))]


def apply_fn(lay, *args):
    weights, slabs = unpack_all(lay, args[: lay.plane]), args[lay.plane :]
    grads, parts = apply_math(lay, slabs, weights)
    outs = pack_all(lay, grads, jnp.zeros((1, 1), F32))
    heads = lay.heads
    return outs + parts[:heads] + ([stack(parts[heads:])] if lay.cores > 1 else [])


def apply_near_fn(lay, count, new, *slabs):
    grads, parts = apply_math(lay, slabs, in_three(lay, new))
    return [cat(grads, 0), *parts[:count], stack(parts[count:])]


def apply_far_fn(lay, count, new, before, *slabs):
    grads, parts = apply_math(lay, slabs, in_three(lay, new))
    grads = [g + b for g, b in zip(grads, in_three(lay, before))]
    outs = pack_parts(lay, grads, jnp.zeros((1, 1), F32))
    return outs + [*parts[:count], stack(parts[count:])]


def stack(parts):
    return cat([p[None] for p in parts], 0)


def renormed_back(coefficient, d_new, total, initial, grad, moved):
    norm, inverse = norms(initial, moved)
    dots = jnp.sum(d_new * moved, 1, keepdims=True)
    d_moved = d_new * (norm * inverse) - moved * (dots * norm * inverse * inverse * inverse)
    direct = d_moved + initial * (dots * inverse / norm)
    d_update = -d_moved
    part = jnp.sum(jnp.sum(d_update * grad, 1, keepdims=True), 0, keepdims=True)
    return d_update * (coefficient / total), -part / total, direct


def renorm_back_fn(lay, coefficient, *args):
    payloads = args[: lay.plane]
    total_payload, initial, grad, moved = args[lay.plane :]
    d_new, _ = unpack(lay, functools.reduce(jnp.add, payloads))
    _, total = unpack(lay, total_payload)
    move, d_total, direct = renormed_back(coefficient, d_new, total, initial, grad, moved)
    return [pack(lay, move, d_total), direct]


def renorm_back_all_fn(lay, coefficient, *args):
    d_new, _ = unpack_parts(lay, *args[:4])
    initial, grad, moved, total = args[4:]
    move, d_total, _ = renormed_back(
        coefficient, d_new, total[0:1, 0:1], initial, grad, moved
    )
    return [move, jnp.broadcast_to(d_total, (SUBLANES, LANES))]


def direct_fn(lay, coefficient, *args):
    d_new, _ = unpack_parts(lay, *args[:4])
    initial, grad, moved, total, places = args[4:]
    direct = renormed_back(coefficient, d_new, total[0:1, 0:1], initial, grad, moved)[2]
    return [held_pieces(places, in_pieces(lay, in_three(lay, direct)), 0)]


def pull_math(lay, slabs, weights, moves, d_total):
    keys, values = join_rows(lay, slabs)
    rates = join_rates(lay, slabs)
    gate, up, down = (split(lay, w) for w in weights)
    gate_move, up_move, down_move = (split(lay, w) for w in moves)
    a, b, ta, tb = dots_left((gate, up, gate_move, up_move), keys, NN)
    u, w = dots_left((down, down_move), values, NN)
    sig, silu, rest, slope = gates(a)
    bend = sig * rest * (2.0 + a * (rest - sig))
    hidden = silu * b
    hidden_dot = slope * ta * b + silu * tb
    rate_part = -jnp.sum(w * hidden + u * hidden_dot, 0, keepdims=True) + d_total
    mu = -rates
    wm, um = mu * w, mu * u
    ga = split(lay, wm * b * slope + um * (bend * ta * b + slope * tb))
    gb = split(lay, wm * silu + um * slope * ta)
    gta = split(lay, um * slope * b)
    gtb = split(lay, um * silu)
    mh = split(lay, mu * hidden)
    md = split(lay, mu * hidden_dot)
    grads = dots_left((ga, gb), keys, NT) + dots_left((md,), values, NT)
    turned = split(lay, cat([weights[0], weights[1], moves[0], moves[1]], 0).T)
    d_key = dot_both(turned, tuple(cat(x, 0) for x in zip(ga, gb, gta, gtb)), NN)
    turned = split(lay, cat([moves[2], weights[2]], 0).T)
    d_value = dot_both(turned, tuple(cat(x, 0) for x in zip(mh, md)), NN)
    rows = slabs[0].shape[1]
    parts = []
    for i in range(len(slabs)):
        take = slice(i * rows, (i + 1) * rows)
        rate_rows = jnp.broadcast_to(rate_part[:, take], (SUBLANES, rows))
        parts.append(cat([d_key[:, take], d_value[:, take], rate_rows], 0))
    return grads, parts


def pull_fn(lay, *args):
    payloads, slabs, weights = args[: lay.plane], args[lay.plane : -1], args[-1]
    d_total = functools.reduce(jnp.add, [unpack(lay, p)[1] for p in payloads])
    grads, parts = pull_math(
        lay, slabs, in_three(lay, weights), unpack_all(lay, payloads), d_total
    )
    outs = pack_all(lay, grads, jnp.zeros((1, 1), F32))
    heads = lay.heads
    return outs + parts[:heads] + ([stack(parts[heads:])] if lay.cores > 1 else [])


def ready_fn(lay, weights, *slabs):
    keys, values = join_rows(lay, slabs)
    gate, up, down = (split(lay, w) for w in in_three(lay, weights))
    a, b = dots_left((gate, up), keys, NN)
    (u,) = dots_left((down,), values, NN)
    sig, silu, rest, slope = gates(a)
    mu = -join_rates(lay, slabs)
    hidden, um = silu * b, mu * u
    steep = slope * b
    bent = um * (sig * rest * (2.0 + a * (rest - sig))) * b
    wide = jnp.broadcast_to(mu, (SUBLANES, mu.shape[1]))
    outs = [keys, values, wide, steep, silu, hidden, u, bent, um * slope]
    return outs + [*split(lay, um * steep), *split(lay, um * silu), *split(lay, mu * hidden)]


def pull_ready(lay, ready, weights, moves, d_total):
    keys, values, mu, steep, silu, hidden, u, bent, ums = ready[:9]
    gta, gtb, mh = ready[9:11], ready[11:13], ready[13:15]
    mu = mu[0:1]
    gate_move, up_move, down_move = (split(lay, w) for w in moves)
    ta, tb = dots_left((gate_move, up_move), keys, NN)
    (w,) = dots_left((down_move,), values, NN)
    hidden_dot = steep * ta + silu * tb
    rate_part = -jnp.sum(w * hidden + u * hidden_dot, 0, keepdims=True) + d_total
    wm = mu * w
    ga = split(lay, wm * steep + bent * ta + ums * tb)
    gb = split(lay, wm * silu + ums * ta)
    md = split(lay, mu * hidden_dot)
    grads = dots_left((ga, gb), keys, NT) + dots_left((md,), values, NT)
    turned = split(lay, cat([weights[0], weights[1], moves[0], moves[1]], 0).T)
    d_key = dot_both(turned, tuple(cat(x, 0) for x in zip(ga, gb, gta, gtb)), NN)
    turned = split(lay, cat([moves[2], weights[2]], 0).T)
    d_value = dot_both(turned, tuple(cat(x, 0) for x in zip(mh, md)), NN)
    parts = []
    for i in range(keys.shape[1] // LANES):
        take = slice(i * LANES, (i + 1) * LANES)
        rate_rows = jnp.broadcast_to(rate_part[:, take], (SUBLANES, LANES))
        parts.append(cat([d_key[:, take], d_value[:, take], rate_rows], 0))
    return grads, parts


def pull_other_fn(lay, moves, d_total, weights, *ready):
    grads, parts = pull_ready(
        lay, ready, in_three(lay, weights), in_three(lay, moves), d_total[0:1, 0:1]
    )
    return [stack(parts), cat(grads, 0)]


def pull_own_fn(lay, moves, d_total, weights, before, *ready):
    grads, parts = pull_ready(
        lay, ready, in_three(lay, weights), in_three(lay, moves), d_total[0:1, 0:1]
    )
    return [cat(grads, 0) + before, *parts]


def pull_last_fn(lay, count, moves, d_total, weights, before, places, *ready):
    grads, parts = pull_ready(
        lay, ready, in_three(lay, weights), in_three(lay, moves), d_total[0:1, 0:1]
    )
    grads = [g + b for g, b in zip(grads, in_three(lay, before))]
    pieces = in_pieces(lay, grads)
    zero = jnp.zeros((1, 1), F32)
    outs = [pack(lay, held_pieces(places, pieces, r), zero) for r in range(lay.plane)]
    return outs + [*parts[:count], stack(parts[count:])]


def add_two_fn(first, first_in, second, second_in):
    return [first + first_in, second + second_in]


def finish_fn(lay, count, *args):
    slabs, head_ids = args[:-1], args[-1]
    dim = lay.head_dim
    outs = []
    for n in range(count):
        pieces = [s[n * dim : (n + 1) * dim] for s in slabs]
        ordered = [
            select_steps(lay, pieces, head_ids, h) for h in range(lay.heads)
        ]
        outs.append(cat(ordered, 0).T.astype(BF16))
    if slabs[0].shape[0] > count * dim:
        pieces = [s[count * dim : count * dim + 1] for s in slabs]
        rows = [select_steps(lay, pieces, head_ids, h) for h in range(lay.heads)]
        outs.append(cat(rows, 0))
    return outs


def add_fn(*args):
    return [part + args[-1][i] for i, part in enumerate(args[:-1])]


def total_fn(lay, scale, *args):
    payloads, direct, places = args[: lay.plane], args[-2], args[-1]
    body, _ = unpack(lay, functools.reduce(jnp.add, payloads))
    final = (body + direct) / scale
    pieces = [final[m * lay.slot : (m + 1) * lay.slot] for m in range(3)]
    return [choose(pieces, places[0:1, t : t + 1]) for t in range(3)]


def place_fn(*args):
    pieces, places = args[:3], args[3]
    return [cat([choose(pieces, places[0:1, 3 + q : 4 + q]) for q in range(3)], 0)]


def total_two_fn(lay, scale, *args):
    payloads, direct = args[: lay.plane], args[-1]
    body, extra = unpack(lay, functools.reduce(jnp.add, payloads))
    final = (body + direct) / scale
    return [pack(lay, final, extra), final[2 * lay.slot :]]


def finish_all_fn(lay, *args):
    first, second, places, slabs = args[0], args[1], args[2], args[3:]
    body, _ = unpack(lay, first)
    pieces = [body[t * lay.slot : (t + 1) * lay.slot] for t in range(3)] + [second]
    placed = cat([choose(pieces, places[0:1, t : t + 1]) for t in range(3, 6)], 0)
    return [placed, *finish_fn(lay, 2, *slabs)]


VMEM_LIMIT = 24 * 1024 * 1024


def run(lay, fn, args, always=False, deps=()):
    if not (lay.packed or always):
        return fn(*args)
    shapes = jax.eval_shape(fn, *args)
    deps = [x[: min(SUBLANES, x.shape[0])] for x in deps]
    count = len(args)

    def kernel(*refs):
        ins, outs = refs[:count], refs[count + len(deps) :]
        for ref, value in zip(outs, fn(*[r[...] for r in ins])):
            ref[...] = value

    vmem = pl.BlockSpec(memory_space=pltpu.VMEM)
    return pl.pallas_call(
        kernel,
        out_shape=[jax.ShapeDtypeStruct(s.shape, s.dtype) for s in shapes],
        in_specs=[vmem] * (count + len(deps)),
        out_specs=[vmem] * len(shapes),
        compiler_params=pltpu.CompilerParams(vmem_limit_bytes=VMEM_LIMIT),
    )(*args, *deps)


def tie(lay, arrays, deps):
    if not lay.packed:
        return arrays
    deps = [x[:SUBLANES] for x in deps]
    vmem = pl.BlockSpec(memory_space=pltpu.VMEM)
    return list(
        pl.pallas_call(
            lambda *refs: None,
            out_shape=[jax.ShapeDtypeStruct(a.shape, a.dtype) for a in arrays],
            in_specs=[vmem] * (len(arrays) + len(deps)),
            out_specs=[vmem] * len(arrays),
            input_output_aliases={i: i for i in range(len(arrays))},
            compiler_params=pltpu.CompilerParams(vmem_limit_bytes=VMEM_LIMIT),
        )(*arrays, *deps)
    )


def on_device(lay, queries, key_rows, value_rows, step_rates, fast_init, out_grad):
    head_dim, _ = fast_init.shape
    heads, slot, plane = lay.heads, lay.slot, lay.plane
    coefficient = step_size * math.sqrt(queries.shape[0] * lay.devices)
    view, patch = lax.axis_index("view"), lax.axis_index("patch")
    core = lax.rem(view, lay.cores)
    head = patch // lay.sub
    member = view // lay.cores * lay.sub + lax.rem(patch, lay.sub)
    me = view * lay.patches + patch
    head_ids = jnp.full((SUBLANES, LANES), head, jnp.int32)

    def send(x, perm):
        return lax.ppermute(x, AXES, perm)

    def over_heads(slabs, hold=()):
        close = [send(slabs[t], lay.head_perm(t)) for t in range(1, min(2, heads))]
        away = slabs[2:]
        if hold:
            away = tie(lay, away, hold)
        away = [send(x, lay.head_perm(t)) for t, x in enumerate(away, 2)]
        return [slabs[0]] + close + away

    def over_cores(slabs):
        return [send(x, lay.core_perm()) for x in slabs] if lay.cores > 1 else []

    def total_rows(parts):
        if lay.cores == 1:
            return parts
        return run(lay, add_fn, (*parts[:heads], send(parts[heads], lay.core_perm())))

    def add_home(parts, away):
        return list(run(lay, add_fn, (*parts, send(away, lay.core_perm()))))

    def back_home(slabs):
        away = [send(slabs[t], lay.head_perm(t)) for t in range(2, heads)]
        close = [send(slabs[t], lay.head_perm(t)) for t in range(1, min(2, heads))]
        return [slabs[0]] + close + away

    def scatter(payloads):
        moved = [send(payloads[r], lay.scatter_perm(r)) for r in range(1, plane)]
        return [payloads[0]] + moved

    def gather(payload):
        return [payload] + [send(payload, lay.gather_perm(r)) for r in range(1, plane)]

    fn = functools.partial
    scale = math.sqrt(queries.shape[0] * lay.devices)
    kv = run(
        lay, fn(spread_rows, lay, True), (key_rows, value_rows, step_rates.T, head_ids), always=True
    )
    kv = over_heads(kv)
    qg = run(
        lay, fn(spread_rows, lay, False), (queries, out_grad, head_ids), always=True, deps=(kv[1],)
    )
    qg = over_heads(qg, tuple(kv[2:]))
    kv = kv + over_cores(kv)

    owner_perms, table = (direct_plan if lay.packed else owner_plan)(lay)
    places = lax.dynamic_slice_in_dim(jnp.array(table, jnp.int32), me, 1, 0)
    first = head * lay.hidden + core * lay.half
    turned = []
    for m in range(3):
        part = lax.dynamic_slice_in_dim(fast_init, m * heads * lay.hidden + first, lay.half, 1)
        turned.append(part.T)
    if not lay.packed:
        order = jnp.stack([lay.target(member, r) for r in range(plane)])
        turned = [
            t.reshape(plane, slot, head_dim)[order].reshape(lay.half, head_dim) for t in turned
        ]
    weights = jnp.concatenate(turned, 0)

    def exchange(first, second):
        bits = [1 << i for i in range(plane.bit_length() - 1)]
        turned_bits = bits[1:] + bits[:1]
        for i, (one, two) in enumerate(zip(bits, turned_bits)):
            if i:
                first, second = run(lay, add_two_fn, (first, first_in, second, second_in))
            first_in = send(first, lay.flip_perm(one))
            second_in = send(second, lay.flip_perm(two))
        return first, first_in, second, second_in

    if lay.packed:
        near = (heads + 1) // 2
        before = run(lay, fn(update_near_fn, lay), (weights, *kv[:near]), deps=(places,))
        rest = run(lay, fn(update_rest_fn, lay), (weights, *before, *kv[near:]))
        sums = exchange(*rest)
        close, away = qg[:2], tie(lay, qg[2:], (sums[0],))
        close, away = close + over_cores(close), away + over_cores(away)
        renewed, grad, moved, total = run(
            lay, fn(renorm_all_fn, lay, coefficient), (*sums, weights)
        )
        before, *query_close = run(lay, fn(apply_near_fn, lay, 2), (renewed, *close))
        applied = run(lay, fn(apply_far_fn, lay, heads - 2), (renewed, before, *away))
        query_home = add_home(query_close[:-1], query_close[-1]) + add_home(
            applied[2:-1], applied[-1]
        )
        sums = exchange(*applied[:2])
        groups = (kv[heads + 2 :], kv[2:heads], kv[:2] + kv[heads : heads + 2])
        ready = [run(lay, fn(ready_fn, lay), (weights, *rows)) for rows in groups]
        state = (*sums, weights, grad, moved, total)
        move, d_total = run(lay, fn(renorm_back_all_fn, lay, coefficient), state)
        query_home = back_home(query_home)
        other, before = run(lay, fn(pull_other_fn, lay), (move, d_total, weights, *ready[0]))
        before, *key_far = run(
            lay, fn(pull_own_fn, lay), (move, d_total, weights, before, *ready[1])
        )
        key_far = add_home(key_far, other)
        pulled = run(
            lay, fn(pull_last_fn, lay, 2), (move, d_total, weights, before, places, *ready[2])
        )
        (direct,) = run(
            lay, fn(direct_fn, lay, coefficient), (*state, places), deps=tuple(pulled[:1])
        )
        key_home = add_home(pulled[plane : plane + 2], pulled[-1]) + key_far
    else:
        own = jnp.concatenate([t[:slot] for t in turned], 0)
        sums = scatter(run(lay, fn(update_fn, lay), (weights, *kv)))
        payload, grad, moved = run(lay, fn(renorm_fn, lay, coefficient), (*sums, own))
        qg = qg + over_cores(qg)
        applied = run(lay, fn(apply_fn, lay), (*gather(payload), *qg))
        sums = scatter(applied[:plane])
        query_home = back_home(total_rows(applied[plane:]))
        d_payload, direct = run(
            lay, fn(renorm_back_fn, lay, coefficient), (*sums, payload, own, grad, moved)
        )
        pulled = run(lay, fn(pull_fn, lay), (*gather(d_payload), *kv, weights))
        key_home = total_rows(pulled[plane:])
    sums = scatter(pulled[:plane])
    key_slabs = back_home(key_home)
    (query_grad,) = run(
        lay, fn(finish_fn, lay, 1), (*query_home, head_ids), always=True, deps=tuple(pulled[:1])
    )
    if lay.packed:
        ready = run(lay, fn(total_two_fn, lay, scale), (*sums, direct), deps=tuple(key_home))
        arrived = [send(x, perm) for x, perm in zip(ready, owner_perms)]
        fast_grad, key_grad, value_grad, rate_grad = run(
            lay, fn(finish_all_fn, lay), (*arrived, places, *key_slabs, head_ids)
        )
    else:
        pieces = run(lay, fn(total_fn, lay, scale), (*sums, direct, places))
        arrived = [send(x, perm) for x, perm in zip(pieces, owner_perms)]
        (fast_grad,) = run(lay, place_fn, (*arrived, places))
        key_grad, value_grad, rate_grad = run(
            lay, fn(finish_fn, lay, 2), (*key_slabs, head_ids), always=True
        )
    return query_grad, key_grad, value_grad, rate_grad.T, fast_grad.T


def owner_plan(lay):
    rounds = lay.owner_rounds()
    table = [[0] * LANES for _ in range(lay.devices)]
    for t, chosen in enumerate(rounds):
        for source, owner, m, spot in chosen:
            table[source][t] = m
            table[owner][3 + spot] = t
    return [[(i, o) for i, o, _, _ in chosen] for chosen in rounds], table


def solution(mesh):
    rows = P(AXES, None)

    def whole(queries, key_rows, value_rows, step_rates, fast_init, out_grad):
        heads = step_rates.shape[1]
        head_dim, columns = fast_init.shape
        lay = Layout(
            mesh.shape["view"], mesh.shape["patch"], heads, columns // (3 * heads), head_dim
        )

        def body(*args):
            return on_device(lay, *args)

        return jax.shard_map(
            body,
            mesh=mesh,
            in_specs=(rows, rows, rows, rows, P(), rows),
            out_specs=(rows, rows, rows, rows, P(None, AXES)),
            check_vma=False,
        )(queries, key_rows, value_rows, step_rates, fast_init, out_grad)

    return whole
```

```python
import functools
import itertools
import math

import jax
import jax.numpy as jnp
from jax import lax
from jax.experimental import pallas as pl
from jax.experimental.pallas import tpu as pltpu
from jax.sharding import PartitionSpec as P


AXES = ("view", "patch")
step_size = 0.2
epsilon = 1e-06
F32, BF16 = jnp.float32, jnp.bfloat16
LANES, SUBLANES = 128, 8


class Layout:
    def __init__(self, views, patches, heads, hidden, head_dim):
        self.heads, self.head_dim, self.hidden = heads, head_dim, hidden
        self.cores = 2 if views % 2 == 0 else 1
        self.patches, self.devices = patches, views * patches
        self.sub = patches // heads
        self.plane = (views // self.cores) * self.sub
        self.half = hidden // self.cores
        self.slot = self.half // self.plane
        self.pow2 = self.plane & (self.plane - 1) == 0
        rows = 3 * self.slot
        self.packed = (
            head_dim == LANES + LANES // 2
            and rows % (2 * SUBLANES) == 0
            and (3 * self.half) % (2 * SUBLANES) == 0
            and self.pow2
            and self.plane == 4
            and self.cores == 2
            and heads > 2
        )

    def place(self, device):
        view, patch = divmod(device, self.patches)
        outer, core = divmod(view, self.cores)
        head, sub = divmod(patch, self.sub)
        return outer * self.sub + sub, core, head

    def device(self, member, core, head):
        outer, sub = divmod(member, self.sub)
        return (outer * self.cores + core) * self.patches + head * self.sub + sub

    def target(self, member, step):
        return member ^ step if self.pow2 else (member + step) % self.plane

    def origin(self, member, step):
        return member ^ step if self.pow2 else (member - step) % self.plane

    def perm(self, move):
        return [(i, self.device(*move(*self.place(i)))) for i in range(self.devices)]

    def core_perm(self):
        return self.perm(lambda j, c, h: (j, (c + 1) % self.cores, h))

    def other_head(self, head, step):
        return head ^ step if self.heads & (self.heads - 1) == 0 else (step - head) % self.heads

    def head_perm(self, step):
        return self.perm(lambda j, c, h: (j, c, self.other_head(h, step)))

    def scatter_perm(self, step):
        return self.perm(lambda j, c, h: (self.target(j, step), c, h))

    def gather_perm(self, step):
        return self.perm(lambda j, c, h: (self.origin(j, step), c, h))

    def flip_perm(self, bit):
        return self.perm(lambda j, c, h: (j ^ bit, c, h))

    def owner_rounds(self):
        count = self.devices
        edges = []
        for i in range(count):
            j, c, h = self.place(i)
            for m in range(3):
                piece = (m * self.heads + h) * self.cores * self.plane + c * self.plane + j
                edges.append((i, piece // 3, m, piece % 3))
        left, rounds = list(edges), []
        for _ in range(3):
            out_edges = [[] for _ in range(count)]
            for edge in left:
                out_edges[edge[0]].append(edge)
            match = {}

            def place_one(i, seen):
                for edge in out_edges[i]:
                    if edge[1] in seen:
                        continue
                    seen.add(edge[1])
                    if edge[1] not in match or place_one(match[edge[1]][0], seen):
                        match[edge[1]] = edge
                        return True
                return False

            for i in range(count):
                place_one(i, set())
            chosen = sorted(match.values())
            rounds.append(chosen)
            left = [edge for edge in left if edge not in match.values()]
        return rounds


def direct_plan(lay):
    table = [[0] * LANES for _ in range(lay.devices)]
    first, second = [], []
    spots = {}
    for head in range(lay.heads):
        for core in range(lay.cores):
            runs = {}
            for m in range(3):
                for j in range(lay.plane):
                    base = (m * lay.heads + head) * lay.cores * lay.plane + core * lay.plane
                    runs.setdefault((m, (base + j) // 3), []).append((m * lay.plane + j, (base + j) % 3))
            runs = sorted(runs.items(), key=lambda item: -len(item[1]))
            long_runs, singles = runs[: lay.plane], runs[lay.plane :]

            def hops(member, owner):
                other, _, there = lay.place(owner)
                here, away = divmod(member, lay.sub), divmod(other, lay.sub)
                return abs(here[0] - away[0]) + abs(here[1] - away[1]) + 2 * abs(head - there)

            best = None
            for order in itertools.permutations(range(lay.plane)):
                for swap in (singles, singles[::-1]):
                    roles = [[long_runs[k]] for k in range(lay.plane)]
                    short = [k for k in range(lay.plane) if len(long_runs[k][1]) == 2]
                    for k, single in zip(short, swap):
                        roles[k].append(single)
                    cost = sum(
                        len(run[1]) * hops(order[k], run[0][1]) ** 2
                        for k in range(lay.plane)
                        for run in roles[k]
                    )
                    if best is None or cost < best[0]:
                        best = cost, order, roles
            _, order, roles = best
            held = {}
            for member, role in zip(order, roles):
                source = lay.device(member, core, head)
                held[member] = [piece for run in role for piece, _ in run[1]]
                for n, ((_, owner), run) in enumerate(role):
                    (second if n else first).append((source, owner))
                    for t, (_, spot) in enumerate(run):
                        spots[owner, spot] = 3 if n else t
            for member in range(lay.plane):
                row = table[lay.device(member, core, head)]
                for r in range(lay.plane):
                    row[8 + 3 * r : 11 + 3 * r] = held[lay.target(member, r)]
    for (owner, spot), index in spots.items():
        table[owner][3 + spot] = index
    return (first, second), table


def split(lay, x):
    if not lay.packed:
        return (x,)
    high = x.astype(BF16)
    return high, (x - high.astype(F32)).astype(BF16)


def dot(a, b, dims, precision=None):
    return lax.dot_general(
        a, b, (dims, ((), ())), precision=precision, preferred_element_type=F32
    )


NN, NT = ((1,), (0,)), ((1,), (1,))


def dot_left(parts, exact, dims):
    if len(parts) == 1:
        return dot(parts[0], exact, dims, lax.Precision.HIGH)
    return dot(parts[0], exact, dims) + dot(parts[1], exact, dims)


def dots_left(lefts, exact, dims):
    if len(lefts[0]) == 1:
        return [dot_left(left, exact, dims) for left in lefts]
    rows = lefts[0][0].shape[0]
    flat = dot(cat([part for left in lefts for part in left], 0), exact, dims)
    cuts = [flat[i * rows : (i + 1) * rows] for i in range(2 * len(lefts))]
    return [cuts[2 * i] + cuts[2 * i + 1] for i in range(len(lefts))]


def dot_both(a, b, dims):
    if len(a) == 1:
        return dot(a[0], b[0], dims, lax.Precision.HIGH)
    rows = a[0].shape[0]
    both = dot(cat(a, 0), b[0], dims)
    return both[:rows] + (dot(a[0], b[1], dims) + both[rows:])


def gates(act):
    sig = 1.0 / (1.0 + jnp.exp(-act))
    silu = act * sig
    rest = 1.0 - sig
    return sig, silu, rest, sig + silu * rest


def cat(parts, axis):
    return jnp.concatenate(parts, axis)


def pack(lay, body, extra):
    if not lay.packed:
        return cat([body, jnp.broadcast_to(extra, (SUBLANES, lay.head_dim))], 0)
    rows = body.shape[0]
    tail = body[:, LANES:]
    tail = cat([tail[: rows // 2], tail[rows // 2 :]], 1)
    return cat([body[:, :LANES], tail, jnp.broadcast_to(extra, (SUBLANES, LANES))], 0)


def unpack(lay, payload, rows=None):
    rows = 3 * lay.slot if rows is None else rows
    if not lay.packed:
        return payload[:rows], payload[rows : rows + 1, :1]
    tail = payload[rows : rows + rows // 2]
    half = LANES // 2
    tail = cat([tail[:, :half], tail[:, half:]], 0)
    return cat([payload[:rows], tail], 1), payload[rows + rows // 2 : rows + rows // 2 + 1, :1]


def wide_rows(lay):
    step = 2 * SUBLANES
    total = 3 * lay.half
    return total - total * 4 // 9 // step * step


def pack_parts(lay, grads, extra):
    body, rows = cat(grads, 0), wide_rows(lay)
    return [pack(lay, body[:rows], extra), pack(lay, body[rows:], extra)]


def unpack_parts(lay, first, first_in, second, second_in):
    rows = wide_rows(lay)
    top, extra = unpack(lay, first + first_in, rows)
    bottom, _ = unpack(lay, second + second_in, 3 * lay.half - rows)
    return cat([top, bottom], 0), extra


def in_pieces(lay, parts):
    slot = lay.slot
    return [p[j * slot : (j + 1) * slot] for p in parts for j in range(lay.plane)]


def held_pieces(places, pieces, step):
    first = 8 + 3 * step
    return cat([choose(pieces, places[0:1, t : t + 1]) for t in range(first, first + 3)], 0)


def choose(pieces, index):
    result = pieces[0]
    for i in range(1, len(pieces)):
        result = jnp.where(index == i, pieces[i], result)
    return result


def in_three(lay, body):
    return [body[m * lay.half : (m + 1) * lay.half] for m in range(3)]


def pack_all(lay, grads, extra):
    outs = []
    for step in range(lay.plane):
        take = slice(step * lay.slot, (step + 1) * lay.slot)
        outs.append(pack(lay, cat([g[take] for g in grads], 0), extra))
    return outs


def unpack_all(lay, payloads):
    bodies = [unpack(lay, p)[0] for p in payloads]
    slot = lay.slot
    return [cat([b[m * slot : (m + 1) * slot] for b in bodies], 0) for m in range(3)]


def select_heads(lay, pieces, head_ids, step):
    own = head_ids[0:1, :]
    result = pieces[0]
    for i in range(1, lay.heads):
        result = jnp.where(own == lay.other_head(i, step), pieces[i], result)
    return result


def select_steps(lay, pieces, head_ids, head):
    own = head_ids[0:1, :]
    result = pieces[0]
    for step in range(1, lay.heads):
        result = jnp.where(own == lay.other_head(head, step), pieces[step], result)
    return result


def spread_rows(lay, with_rates, both, *rest):
    dim = lay.head_dim
    head_ids = rest[-1]
    count = both.shape[0] // 2
    turned = [x.astype(F32).T for x in (both[:count], both[count:])]
    pieces = [[t[h * dim : (h + 1) * dim] for h in range(lay.heads)] for t in turned]
    if with_rates:
        rates = rest[0]
        rows = rates.shape[1]
        pieces.append(
            [jnp.broadcast_to(rates[h : h + 1], (SUBLANES, rows)) for h in range(lay.heads)]
        )
    return [
        cat([select_heads(lay, p, head_ids, shift) for p in pieces], 0)
        for shift in range(lay.heads)
    ]


def join_rows(lay, slabs):
    dim = lay.head_dim
    kind = BF16 if lay.packed else F32
    first = cat([s[:dim] for s in slabs], 1).astype(kind)
    second = cat([s[dim : 2 * dim] for s in slabs], 1).astype(kind)
    return first, second


def join_rates(lay, slabs):
    dim = lay.head_dim
    return cat([s[2 * dim : 2 * dim + 1] for s in slabs], 1)


def update_math(lay, slabs, weights):
    keys, values = join_rows(lay, slabs)
    rates = join_rates(lay, slabs)
    gate, up, down = (split(lay, w) for w in in_three(lay, weights))
    a, b = dots_left((gate, up), keys, NN)
    (u,) = dots_left((down,), values, NN)
    _, silu, _, slope = gates(a)
    mu = -rates * u
    d_gate, d_up = dots_left(
        (split(lay, mu * b * slope), split(lay, mu * silu)), keys, NT
    )
    (d_down,) = dots_left((split(lay, -rates * (silu * b)),), values, NT)
    return [d_gate, d_up, d_down], jnp.sum(rates, 1, keepdims=True)


def update_fn(lay, weights, *slabs):
    grads, total = update_math(lay, slabs, weights)
    return pack_all(lay, grads, total)


def update_near_fn(lay, weights, *slabs):
    grads, total = update_math(lay, slabs, weights)
    return [cat(grads, 0), jnp.broadcast_to(total, (SUBLANES, LANES))]


def update_rest_fn(lay, weights, before, total_before, *slabs):
    grads, total = update_math(lay, slabs, weights)
    grads = [g + b for g, b in zip(grads, in_three(lay, before))]
    return pack_parts(lay, grads, total + total_before[0:1, 0:1])


def norms(initial, moved):
    norm = jnp.sqrt(jnp.sum(initial * initial, 1, keepdims=True) + epsilon)
    inverse = lax.rsqrt(jnp.sum(moved * moved, 1, keepdims=True) + epsilon)
    return norm, inverse


def renormed(coefficient, body, total, initial):
    grad = body * (coefficient / total)
    moved = initial - grad
    norm, inverse = norms(initial, moved)
    return moved * (norm * inverse), grad, moved


def renorm_fn(lay, coefficient, *args):
    payloads, initial = args[:-1], args[-1]
    body, total = unpack(lay, functools.reduce(jnp.add, payloads))
    new, grad, moved = renormed(coefficient, body, total, initial)
    return [pack(lay, new, total), grad, moved]


def renorm_all_fn(lay, coefficient, *args):
    body, total = unpack_parts(lay, *args[:4])
    new, grad, moved = renormed(coefficient, body, total, args[4])
    return [new, grad, moved, jnp.broadcast_to(total, (SUBLANES, LANES))]


def apply_math(lay, slabs, weights):
    queries, cotangents = join_rows(lay, slabs)
    gate, up, down = (split(lay, w) for w in weights)
    a, b = dots_left((gate, up), queries, NN)
    (u,) = dots_left((down,), cotangents, NN)
    _, silu, _, slope = gates(a)
    da = split(lay, u * b * slope)
    db = split(lay, u * silu)
    h = split(lay, silu * b)
    grads = dots_left((da, db), queries, NT) + dots_left((h,), cotangents, NT)
    turned = split(lay, cat([weights[0], weights[1]], 0).T)
    both = tuple(cat([x, y], 0) for x, y in zip(da, db))
    d_query = dot_both(turned, both, NN)
    rows = slabs[0].shape[1]
    return grads, [d_query[:, i * rows : (i + 1) * rows] for i in range(len(slabs))]


def apply_fn(lay, *args):
    weights, slabs = unpack_all(lay, args[: lay.plane]), args[lay.plane :]
    grads, parts = apply_math(lay, slabs, weights)
    outs = pack_all(lay, grads, jnp.zeros((1, 1), F32))
    heads = lay.heads
    return outs + parts[:heads] + ([stack(parts[heads:])] if lay.cores > 1 else [])


def apply_near_fn(lay, count, new, *slabs):
    grads, parts = apply_math(lay, slabs, in_three(lay, new))
    return [cat(grads, 0), *parts[:count], stack(parts[count:])]


def apply_far_fn(lay, count, new, before, *slabs):
    grads, parts = apply_math(lay, slabs, in_three(lay, new))
    grads = [g + b for g, b in zip(grads, in_three(lay, before))]
    outs = pack_parts(lay, grads, jnp.zeros((1, 1), F32))
    return outs + [*parts[:count], stack(parts[count:])]


def stack(parts):
    return cat([p[None] for p in parts], 0)


def renormed_back(coefficient, d_new, total, initial, grad, moved):
    norm, inverse = norms(initial, moved)
    dots = jnp.sum(d_new * moved, 1, keepdims=True)
    d_moved = d_new * (norm * inverse) - moved * (dots * norm * inverse * inverse * inverse)
    direct = d_moved + initial * (dots * inverse / norm)
    d_update = -d_moved
    part = jnp.sum(jnp.sum(d_update * grad, 1, keepdims=True), 0, keepdims=True)
    return d_update * (coefficient / total), -part / total, direct


def renorm_back_fn(lay, coefficient, *args):
    payloads = args[: lay.plane]
    total_payload, initial, grad, moved = args[lay.plane :]
    d_new, _ = unpack(lay, functools.reduce(jnp.add, payloads))
    _, total = unpack(lay, total_payload)
    move, d_total, direct = renormed_back(coefficient, d_new, total, initial, grad, moved)
    return [pack(lay, move, d_total), direct]


def renorm_back_all_fn(lay, coefficient, *args):
    d_new, _ = unpack_parts(lay, *args[:4])
    initial, grad, moved, total = args[4:]
    move, d_total, _ = renormed_back(
        coefficient, d_new, total[0:1, 0:1], initial, grad, moved
    )
    return [move, jnp.broadcast_to(d_total, (SUBLANES, LANES))]


def direct_fn(lay, coefficient, *args):
    d_new, _ = unpack_parts(lay, *args[:4])
    initial, grad, moved, total, places = args[4:]
    direct = renormed_back(coefficient, d_new, total[0:1, 0:1], initial, grad, moved)[2]
    return [held_pieces(places, in_pieces(lay, in_three(lay, direct)), 0)]


def pull_math(lay, slabs, weights, moves, d_total):
    keys, values = join_rows(lay, slabs)
    rates = join_rates(lay, slabs)
    gate, up, down = (split(lay, w) for w in weights)
    gate_move, up_move, down_move = (split(lay, w) for w in moves)
    a, b, ta, tb = dots_left((gate, up, gate_move, up_move), keys, NN)
    u, w = dots_left((down, down_move), values, NN)
    sig, silu, rest, slope = gates(a)
    bend = sig * rest * (2.0 + a * (rest - sig))
    hidden = silu * b
    hidden_dot = slope * ta * b + silu * tb
    rate_part = -jnp.sum(w * hidden + u * hidden_dot, 0, keepdims=True) + d_total
    mu = -rates
    wm, um = mu * w, mu * u
    ga = split(lay, wm * b * slope + um * (bend * ta * b + slope * tb))
    gb = split(lay, wm * silu + um * slope * ta)
    gta = split(lay, um * slope * b)
    gtb = split(lay, um * silu)
    mh = split(lay, mu * hidden)
    md = split(lay, mu * hidden_dot)
    grads = dots_left((ga, gb), keys, NT) + dots_left((md,), values, NT)
    turned = split(lay, cat([weights[0], weights[1], moves[0], moves[1]], 0).T)
    d_key = dot_both(turned, tuple(cat(x, 0) for x in zip(ga, gb, gta, gtb)), NN)
    turned = split(lay, cat([moves[2], weights[2]], 0).T)
    d_value = dot_both(turned, tuple(cat(x, 0) for x in zip(mh, md)), NN)
    rows = slabs[0].shape[1]
    parts = []
    for i in range(len(slabs)):
        take = slice(i * rows, (i + 1) * rows)
        rate_rows = jnp.broadcast_to(rate_part[:, take], (SUBLANES, rows))
        parts.append(cat([d_key[:, take], d_value[:, take], rate_rows], 0))
    return grads, parts


def pull_fn(lay, *args):
    payloads, slabs, weights = args[: lay.plane], args[lay.plane : -1], args[-1]
    d_total = functools.reduce(jnp.add, [unpack(lay, p)[1] for p in payloads])
    grads, parts = pull_math(
        lay, slabs, in_three(lay, weights), unpack_all(lay, payloads), d_total
    )
    outs = pack_all(lay, grads, jnp.zeros((1, 1), F32))
    heads = lay.heads
    return outs + parts[:heads] + ([stack(parts[heads:])] if lay.cores > 1 else [])


def ready_fn(lay, weights, *slabs):
    keys, values = join_rows(lay, slabs)
    gate, up, down = (split(lay, w) for w in in_three(lay, weights))
    a, b = dots_left((gate, up), keys, NN)
    (u,) = dots_left((down,), values, NN)
    sig, silu, rest, slope = gates(a)
    mu = -join_rates(lay, slabs)
    hidden, um = silu * b, mu * u
    steep = slope * b
    bent = um * (sig * rest * (2.0 + a * (rest - sig))) * b
    wide = jnp.broadcast_to(mu, (SUBLANES, mu.shape[1]))
    outs = [keys, values, wide, steep, silu, hidden, u, bent, um * slope]
    return outs + [*split(lay, um * steep), *split(lay, um * silu), *split(lay, mu * hidden)]


def pull_ready(lay, ready, weights, moves, d_total):
    keys, values, mu, steep, silu, hidden, u, bent, ums = ready[:9]
    gta, gtb, mh = ready[9:11], ready[11:13], ready[13:15]
    mu = mu[0:1]
    gate_move, up_move, down_move = (split(lay, w) for w in moves)
    ta, tb = dots_left((gate_move, up_move), keys, NN)
    (w,) = dots_left((down_move,), values, NN)
    hidden_dot = steep * ta + silu * tb
    rate_part = -jnp.sum(w * hidden + u * hidden_dot, 0, keepdims=True) + d_total
    wm = mu * w
    ga = split(lay, wm * steep + bent * ta + ums * tb)
    gb = split(lay, wm * silu + ums * ta)
    md = split(lay, mu * hidden_dot)
    grads = dots_left((ga, gb), keys, NT) + dots_left((md,), values, NT)
    turned = split(lay, cat([weights[0], weights[1], moves[0], moves[1]], 0).T)
    d_key = dot_both(turned, tuple(cat(x, 0) for x in zip(ga, gb, gta, gtb)), NN)
    turned = split(lay, cat([moves[2], weights[2]], 0).T)
    d_value = dot_both(turned, tuple(cat(x, 0) for x in zip(mh, md)), NN)
    parts = []
    for i in range(keys.shape[1] // LANES):
        take = slice(i * LANES, (i + 1) * LANES)
        rate_rows = jnp.broadcast_to(rate_part[:, take], (SUBLANES, LANES))
        parts.append(cat([d_key[:, take], d_value[:, take], rate_rows], 0))
    return grads, parts


def pull_other_fn(lay, moves, d_total, weights, *ready):
    grads, parts = pull_ready(
        lay, ready, in_three(lay, weights), in_three(lay, moves), d_total[0:1, 0:1]
    )
    return [stack(parts), cat(grads, 0)]


def pull_own_fn(lay, moves, d_total, weights, before, *ready):
    grads, parts = pull_ready(
        lay, ready, in_three(lay, weights), in_three(lay, moves), d_total[0:1, 0:1]
    )
    return [cat(grads, 0) + before, *parts]


def pull_last_fn(lay, count, moves, d_total, weights, before, places, *ready):
    grads, parts = pull_ready(
        lay, ready, in_three(lay, weights), in_three(lay, moves), d_total[0:1, 0:1]
    )
    grads = [g + b for g, b in zip(grads, in_three(lay, before))]
    pieces = in_pieces(lay, grads)
    zero = jnp.zeros((1, 1), F32)
    outs = [pack(lay, held_pieces(places, pieces, r), zero) for r in range(lay.plane)]
    return outs + [*parts[:count], stack(parts[count:])]


def add_two_fn(first, first_in, second, second_in):
    return [first + first_in, second + second_in]


def finish_fn(lay, count, *args):
    slabs, head_ids = args[:-1], args[-1]
    dim = lay.head_dim
    outs = []
    for n in range(count):
        pieces = [s[n * dim : (n + 1) * dim] for s in slabs]
        ordered = [
            select_steps(lay, pieces, head_ids, h) for h in range(lay.heads)
        ]
        outs.append(cat(ordered, 0).T.astype(BF16))
    if slabs[0].shape[0] > count * dim:
        pieces = [s[count * dim : count * dim + 1] for s in slabs]
        rows = [select_steps(lay, pieces, head_ids, h) for h in range(lay.heads)]
        outs.append(cat(rows, 0))
    return outs


def add_fn(*args):
    return [part + args[-1][i] for i, part in enumerate(args[:-1])]


def total_fn(lay, scale, *args):
    payloads, direct, places = args[: lay.plane], args[-2], args[-1]
    body, _ = unpack(lay, functools.reduce(jnp.add, payloads))
    final = (body + direct) / scale
    pieces = [final[m * lay.slot : (m + 1) * lay.slot] for m in range(3)]
    return [choose(pieces, places[0:1, t : t + 1]) for t in range(3)]


def place_fn(*args):
    pieces, places = args[:3], args[3]
    return [cat([choose(pieces, places[0:1, 3 + q : 4 + q]) for q in range(3)], 0)]


def total_two_fn(lay, scale, *args):
    payloads, direct = args[: lay.plane], args[-1]
    body, extra = unpack(lay, functools.reduce(jnp.add, payloads))
    final = (body + direct) / scale
    return [pack(lay, final, extra), final[2 * lay.slot :]]


def finish_all_fn(lay, *args):
    first, second, places, slabs = args[0], args[1], args[2], args[3:]
    body, _ = unpack(lay, first)
    pieces = [body[t * lay.slot : (t + 1) * lay.slot] for t in range(3)] + [second]
    placed = cat([choose(pieces, places[0:1, t : t + 1]) for t in range(3, 6)], 0)
    return [placed, *finish_fn(lay, 2, *slabs)]


VMEM_LIMIT = 24 * 1024 * 1024


def run(lay, fn, args, always=False, deps=()):
    if not (lay.packed or always):
        return fn(*args)
    shapes = jax.eval_shape(fn, *args)
    deps = [x[: min(SUBLANES, x.shape[0])] for x in deps]
    count = len(args)

    def kernel(*refs):
        ins, outs = refs[:count], refs[count + len(deps) :]
        for ref, value in zip(outs, fn(*[r[...] for r in ins])):
            ref[...] = value

    vmem = pl.BlockSpec(memory_space=pltpu.VMEM)
    return pl.pallas_call(
        kernel,
        out_shape=[jax.ShapeDtypeStruct(s.shape, s.dtype) for s in shapes],
        in_specs=[vmem] * (count + len(deps)),
        out_specs=[vmem] * len(shapes),
        compiler_params=pltpu.CompilerParams(vmem_limit_bytes=VMEM_LIMIT),
    )(*args, *deps)


def tie(lay, arrays, deps):
    if not lay.packed:
        return arrays
    deps = [x[:SUBLANES] for x in deps]
    vmem = pl.BlockSpec(memory_space=pltpu.VMEM)
    return list(
        pl.pallas_call(
            lambda *refs: None,
            out_shape=[jax.ShapeDtypeStruct(a.shape, a.dtype) for a in arrays],
            in_specs=[vmem] * (len(arrays) + len(deps)),
            out_specs=[vmem] * len(arrays),
            input_output_aliases={i: i for i in range(len(arrays))},
            compiler_params=pltpu.CompilerParams(vmem_limit_bytes=VMEM_LIMIT),
        )(*arrays, *deps)
    )


def on_device(lay, queries, key_rows, value_rows, step_rates, fast_init, out_grad):
    head_dim, _ = fast_init.shape
    heads, slot, plane = lay.heads, lay.slot, lay.plane
    coefficient = step_size * math.sqrt(queries.shape[0] * lay.devices)
    view, patch = lax.axis_index("view"), lax.axis_index("patch")
    core = lax.rem(view, lay.cores)
    head = patch // lay.sub
    member = view // lay.cores * lay.sub + lax.rem(patch, lay.sub)
    me = view * lay.patches + patch
    head_ids = jnp.full((SUBLANES, LANES), head, jnp.int32)

    def send(x, perm):
        return lax.ppermute(x, AXES, perm)

    def over_heads(slabs, hold=()):
        close = [send(slabs[t], lay.head_perm(t)) for t in range(1, min(2, heads))]
        away = slabs[2:]
        if hold:
            away = tie(lay, away, hold)
        away = [send(x, lay.head_perm(t)) for t, x in enumerate(away, 2)]
        return [slabs[0]] + close + away

    def over_cores(slabs):
        return [send(x, lay.core_perm()) for x in slabs] if lay.cores > 1 else []

    def total_rows(parts):
        if lay.cores == 1:
            return parts
        return run(lay, add_fn, (*parts[:heads], send(parts[heads], lay.core_perm())))

    def add_home(parts, away):
        return list(run(lay, add_fn, (*parts, send(away, lay.core_perm()))))

    def back_home(slabs):
        away = [send(slabs[t], lay.head_perm(t)) for t in range(2, heads)]
        close = [send(slabs[t], lay.head_perm(t)) for t in range(1, min(2, heads))]
        return [slabs[0]] + close + away

    def scatter(payloads):
        moved = [send(payloads[r], lay.scatter_perm(r)) for r in range(1, plane)]
        return [payloads[0]] + moved

    def gather(payload):
        return [payload] + [send(payload, lay.gather_perm(r)) for r in range(1, plane)]

    fn = functools.partial
    scale = math.sqrt(queries.shape[0] * lay.devices)
    kv = run(
        lay,
        fn(spread_rows, lay, True),
        (jnp.concatenate([key_rows, value_rows], 0), step_rates.T, head_ids),
        always=True,
    )
    kv = over_heads(kv)
    qg = run(
        lay,
        fn(spread_rows, lay, False),
        (jnp.concatenate([queries, out_grad], 0), head_ids),
        always=True,
        deps=(kv[1],),
    )
    qg = over_heads(qg, tuple(kv[2:]))
    kv = kv + over_cores(kv)

    owner_perms, table = (direct_plan if lay.packed else owner_plan)(lay)
    places = lax.dynamic_slice_in_dim(jnp.array(table, jnp.int32), me, 1, 0)
    first = head * lay.hidden + core * lay.half
    turned = []
    for m in range(3):
        part = lax.dynamic_slice_in_dim(fast_init, m * heads * lay.hidden + first, lay.half, 1)
        turned.append(part.T)
    if not lay.packed:
        order = jnp.stack([lay.target(member, r) for r in range(plane)])
        turned = [
            t.reshape(plane, slot, head_dim)[order].reshape(lay.half, head_dim) for t in turned
        ]
    weights = jnp.concatenate(turned, 0)

    def exchange(first, second):
        bits = [1 << i for i in range(plane.bit_length() - 1)]
        turned_bits = bits[1:] + bits[:1]
        for i, (one, two) in enumerate(zip(bits, turned_bits)):
            if i:
                first, second = run(lay, add_two_fn, (first, first_in, second, second_in))
            first_in = send(first, lay.flip_perm(one))
            second_in = send(second, lay.flip_perm(two))
        return first, first_in, second, second_in

    if lay.packed:
        near = (heads + 1) // 2
        before = run(lay, fn(update_near_fn, lay), (weights, *kv[:near]), deps=(places,))
        rest = run(lay, fn(update_rest_fn, lay), (weights, *before, *kv[near:]))
        sums = exchange(*rest)
        close, away = qg[:2], tie(lay, qg[2:], (sums[0],))
        close, away = close + over_cores(close), away + over_cores(away)
        renewed, grad, moved, total = run(
            lay, fn(renorm_all_fn, lay, coefficient), (*sums, weights)
        )
        before, *query_close = run(lay, fn(apply_near_fn, lay, 2), (renewed, *close))
        applied = run(lay, fn(apply_far_fn, lay, heads - 2), (renewed, before, *away))
        query_home = add_home(query_close[:-1], query_close[-1]) + add_home(
            applied[2:-1], applied[-1]
        )
        sums = exchange(*applied[:2])
        groups = (kv[heads + 2 :], kv[2:heads], kv[:2] + kv[heads : heads + 2])
        ready = [run(lay, fn(ready_fn, lay), (weights, *rows)) for rows in groups]
        state = (*sums, weights, grad, moved, total)
        move, d_total = run(lay, fn(renorm_back_all_fn, lay, coefficient), state)
        query_home = back_home(query_home)
        other, before = run(lay, fn(pull_other_fn, lay), (move, d_total, weights, *ready[0]))
        before, *key_far = run(
            lay, fn(pull_own_fn, lay), (move, d_total, weights, before, *ready[1])
        )
        key_far = add_home(key_far, other)
        pulled = run(
            lay, fn(pull_last_fn, lay, 2), (move, d_total, weights, before, places, *ready[2])
        )
        (direct,) = run(
            lay, fn(direct_fn, lay, coefficient), (*state, places), deps=tuple(pulled[:1])
        )
        key_home = add_home(pulled[plane : plane + 2], pulled[-1]) + key_far
    else:
        own = jnp.concatenate([t[:slot] for t in turned], 0)
        sums = scatter(run(lay, fn(update_fn, lay), (weights, *kv)))
        payload, grad, moved = run(lay, fn(renorm_fn, lay, coefficient), (*sums, own))
        qg = qg + over_cores(qg)
        applied = run(lay, fn(apply_fn, lay), (*gather(payload), *qg))
        sums = scatter(applied[:plane])
        query_home = back_home(total_rows(applied[plane:]))
        d_payload, direct = run(
            lay, fn(renorm_back_fn, lay, coefficient), (*sums, payload, own, grad, moved)
        )
        pulled = run(lay, fn(pull_fn, lay), (*gather(d_payload), *kv, weights))
        key_home = total_rows(pulled[plane:])
    sums = scatter(pulled[:plane])
    key_slabs = back_home(key_home)
    (query_grad,) = run(
        lay, fn(finish_fn, lay, 1), (*query_home, head_ids), always=True, deps=tuple(pulled[:1])
    )
    if lay.packed:
        ready = run(lay, fn(total_two_fn, lay, scale), (*sums, direct), deps=tuple(key_home))
        arrived = [send(x, perm) for x, perm in zip(ready, owner_perms)]
        fast_grad, key_grad, value_grad, rate_grad = run(
            lay, fn(finish_all_fn, lay), (*arrived, places, *key_slabs, head_ids)
        )
    else:
        pieces = run(lay, fn(total_fn, lay, scale), (*sums, direct, places))
        arrived = [send(x, perm) for x, perm in zip(pieces, owner_perms)]
        (fast_grad,) = run(lay, place_fn, (*arrived, places))
        key_grad, value_grad, rate_grad = run(
            lay, fn(finish_fn, lay, 2), (*key_slabs, head_ids), always=True
        )
    return query_grad, key_grad, value_grad, rate_grad.T, fast_grad.T


def owner_plan(lay):
    rounds = lay.owner_rounds()
    table = [[0] * LANES for _ in range(lay.devices)]
    for t, chosen in enumerate(rounds):
        for source, owner, m, spot in chosen:
            table[source][t] = m
            table[owner][3 + spot] = t
    return [[(i, o) for i, o, _, _ in chosen] for chosen in rounds], table


def solution(mesh):
    rows = P(AXES, None)

    def whole(queries, key_rows, value_rows, step_rates, fast_init, out_grad):
        heads = step_rates.shape[1]
        head_dim, columns = fast_init.shape
        lay = Layout(
            mesh.shape["view"], mesh.shape["patch"], heads, columns // (3 * heads), head_dim
        )

        def body(*args):
            return on_device(lay, *args)

        return jax.shard_map(
            body,
            mesh=mesh,
            in_specs=(rows, rows, rows, rows, P(), rows),
            out_specs=(rows, rows, rows, rows, P(None, AXES)),
            check_vma=False,
        )(queries, key_rows, value_rows, step_rates, fast_init, out_grad)

    return whole
```
